128 devices in a mesh: dp: 32 (over z, y, x_hi), mp: 4 (over x_lo, core).
Axes of the slice: x: 4 (x_hi: 2, x_lo: 2; x = x_hi * 2 + x_lo), y: 4, z: 4, core: 2. Of those that a mesh axis runs over, the one named last changes fastest.
Arguments:
- tokens: bfloat16 [2, 4096, 2048], P(None, 'dp'), may hold values from -6 to 6
- segment_ids: int32 [2, 4096], replicated, may hold values from 0 to 1, never falling along the last dimension, each value on 1 to 3584 neighbouring positions
- skip_mask: int32 [2, 2], replicated, may hold values 0 or 1
- norm1_gain: bfloat16 [2048], P('dp'), may hold values from 0.25 to 1.75
- w_query: bfloat16 [2048, 2048], P('dp', 'mp'), may hold values from -0.125 to 0.125
- w_key: bfloat16 [2048, 512], P('dp', 'mp'), may hold values from -0.125 to 0.125
- w_value: bfloat16 [2048, 512], P('dp', 'mp'), may hold values from -0.125 to 0.125
- w_out: bfloat16 [2048, 2048], P('mp', 'dp'), may hold values from -1 to 1
- norm2_gain: bfloat16 [2048], P('dp'), may hold values from 0.25 to 1.75
- w_gate: bfloat16 [2048, 5632], P('dp', 'mp'), may hold values from -0.125 to 0.125
- w_up: bfloat16 [2048, 5632], P('dp', 'mp'), may hold values from -0.125 to 0.125
- w_down: bfloat16 [5632, 2048], P('mp', 'dp'), may hold values from -0.078125 to 0.078125
- cotangent: bfloat16 [2, 4096, 2048], P(None, 'dp'), may hold values from -6 to 6
Outputs:
- result: bfloat16 [2, 4096, 2048], P(None, 'dp')
- d_tokens: bfloat16 [2, 4096, 2048], P(None, 'dp')
- d_norm1_gain: float32 [2048], P('dp')
- d_w_query: float32 [2048, 2048], P('dp', 'mp')
- d_w_key: float32 [2048, 512], P('dp', 'mp')
- d_w_value: float32 [2048, 512], P('dp', 'mp')
- d_w_out: float32 [2048, 2048], P('mp', 'dp')
- d_norm2_gain: float32 [2048], P('dp')
- d_w_gate: float32 [2048, 5632], P('dp', 'mp')
- d_w_up: float32 [2048, 5632], P('dp', 'mp')
- d_w_down: float32 [5632, 2048], P('mp', 'dp')
The draws below stay inside these ranges and needn't reach their ends.
Inputs may be any that keep to these rules, and one draw needn't show every extreme that they name: `segment_ids`: document numbers never fall along a micro-batch; 2 documents of 1 to 3584 tokens each.
All inputs are finite; a program needn't handle non-finite values.
Results may differ from the reference program's by a relative error of at most 0.03.
Values may be sent and summed in bfloat16 or wider, within the bound.
No kernel may reach another device: no remote copies, remote signals or barrier semaphores. Data moves between devices by JAX's collectives and lax.ppermute only.
A program may use at most 192 MiB of HBM per device.

```python
import math
import jax
import jax.numpy as jnp
import numpy as np
from jax import lax

D = 2048
H = 16
KV = 4
HD = 128
FF = 5632
BLOCK = 256
NSEG = 2
MB = 2
TOKENS = 4096
LONGEST = 3584


def plant(array, rng, low, top_value):
    index_at = [jax.random.randint(jax.random.fold_in(rng, axis), (), 0, length) for axis, length in enumerate(array.shape)]
    main_axis = array.shape.index(max(array.shape))
    beside = index_at[:main_axis] + [(index_at[main_axis] + 1) % array.shape[main_axis]] + index_at[main_axis + 1:]
    return array.at[tuple(index_at)].set(low).at[tuple(beside)].set(top_value)


def with_spikes(result, own_key, source, target, parts, factor):
    def block_of(position):
        return (jnp.arange(result.shape[position]) // (result.shape[position] // parts)).reshape((-1,) + (1,) * (result.ndim - 1 - position))

    near = jax.random.permutation(own_key, parts)[block_of(target)]
    far = (block_of(target) + parts // 2) % parts
    return jnp.where((block_of(source) == near) | (block_of(source) == far), factor * result, result)


def block_scale(key, shape, shards, low, high):
    def one(position, parts):
        heights = jax.random.uniform(jax.random.fold_in(jax.random.fold_in(key, 6), position), (parts,), jnp.float32, low / len(shards), high / len(shards))
        return jnp.repeat(jnp.exp(heights), shape[position] // parts).reshape((-1,) + (1,) * (len(shape) - position - 1))

    factor_of = one(*shards[0])
    for cut in shards[1:]:
        factor_of = factor_of * one(*cut)
    return factor_of


def length_profile(number_of, total, most, slope):
    weights = [(1 << 20) // math.isqrt(grade ** slope) + 1 for grade in range(2, number_of + 1)]
    rest, given = total - most - (number_of - 1), [1] * (number_of - 1)
    while rest > 0:
        candidates = [i for i in range(number_of - 1) if given[i] < most]
        whole, budget = sum([weights[i] for i in candidates]), rest
        for i in candidates:
            addition = min(most - given[i], max(1, budget * weights[i] // whole), rest)
            given[i] = given[i] + addition
            rest = rest - addition
    return np.array([most] + given)


def ragged(stream_key, number_of, total, bound, lean):
    if number_of == 2:
        one = jax.random.randint(stream_key, (), max(1, total - bound), min(bound, total - 1) + 1)
        return jnp.stack([one, total - one])
    tallies = jnp.asarray(length_profile(number_of, total, bound, lean), jnp.int32)
    couples = (number_of - 1) // 2
    donor, taker = tallies[1:1 + 2 * couples:2], tallies[2:2 + 2 * couples:2]
    room = jnp.minimum(donor - 1, bound - taker)
    passed = jax.random.randint(jax.random.fold_in(stream_key, 1), (couples,), 0, 1 << 20) % (room + 1)
    tallies = tallies.at[1:1 + 2 * couples:2].set(donor - passed).at[2:2 + 2 * couples:2].set(taker + passed)
    return tallies[jax.random.permutation(jax.random.fold_in(stream_key, 2), number_of)]


def gaussian(own_key, shape, deviation, limit, pieces=(), held_as=jnp.bfloat16):
    result = deviation * jax.random.normal(own_key, shape, jnp.float32)
    if pieces:
        result = result * block_scale(own_key, shape, pieces, -0.22, 0.18)
    return jnp.clip(result, -limit, limit).astype(held_as)


def noise_with(rng, shape, scale, bound, pieces, heavy, kind=jnp.bfloat16):
    entries = scale * jax.random.normal(rng, shape, jnp.float32)
    if pieces:
        entries = entries * block_scale(rng, shape, pieces, -0.22, 0.18)
    return jnp.clip(with_spikes(entries, jax.random.fold_in(rng, 3), *heavy), -bound, bound).astype(kind)


def setup_inputs(seed: int = 0) -> dict:
    seeds = jax.random.split(jax.random.key(seed), 14)
    return {
        "tokens": noise_with(seeds[0], (MB, TOKENS, D), 1.0, 6.0, ((1, 32),), (1, 2, 32, 2.75)),
        "segment_ids": jax.vmap(lambda own: jnp.searchsorted(jnp.cumsum(ragged(own, NSEG, TOKENS, LONGEST, 1)), jnp.arange(TOKENS), side="right"))(jax.random.split(seeds[1], MB)).reshape((MB, TOKENS)).astype(jnp.int32),
        "skip_mask": plant((jax.random.randint(seeds[2], (MB, NSEG), 0, 6) < 1).astype(jnp.int32), jax.random.fold_in(seeds[2], 1), 0, 1),
        "norm1_gain": jnp.clip(1.0 + 0.15 * jax.random.normal(seeds[3], (D,), jnp.float32), 0.25, 1.75).astype(jnp.bfloat16),
        "w_query": gaussian(seeds[4], (D, H * HD), D ** -0.5, 0.125, ((0, 32), (1, 4))),
        "w_key": gaussian(seeds[5], (D, KV * HD), D ** -0.5, 0.125, ((0, 32), (1, 4))),
        "w_value": gaussian(seeds[6], (D, KV * HD), D ** -0.5, 0.125, ((0, 32), (1, 4))),
        "w_out": gaussian(seeds[7], (H * HD, D), (H * HD // 64) ** -0.5, 1.0, ((0, 4), (1, 32))),
        "norm2_gain": jnp.clip(1.0 + 0.15 * jax.random.normal(seeds[8], (D,), jnp.float32), 0.25, 1.75).astype(jnp.bfloat16),
        "w_gate": gaussian(seeds[9], (D, FF), D ** -0.5, 0.125, ((0, 32), (1, 4))),
        "w_up": gaussian(seeds[10], (D, FF), D ** -0.5, 0.125, ((0, 32), (1, 4))),
        "w_down": gaussian(seeds[11], (FF, D), FF ** -0.5, 0.078125, ((0, 4), (1, 32))),
        "cotangent": noise_with(seeds[12], (MB, TOKENS, D), 1.0, 6.0, ((1, 32),), (1, 2, 32, 2.75)),
    }


@jax.custom_vjp
def low(v):
    return lax.optimization_barrier(v.astype(jnp.bfloat16)).astype(jnp.float32)

@jax.custom_vjp
def low_back(v):
    return v

def low_keep(v):
    return (low(v), None)

def low_pass(kept, grad):
    return (grad,)

def back_keep(v):
    return (v, None)

def back_low(kept, grad):
    return (low(grad),)
low.defvjp(low_keep, low_pass)
low_back.defvjp(back_keep, back_low)
EPSILON = 1e-05
NEGATIVE = -1e+30

def matmul(left, right):
    return jnp.dot(left, right, precision=lax.Precision.HIGHEST, preferred_element_type=jnp.float32)

def rotate(values, place, sign):
    width = values.shape[-1]
    half = width // 2
    rates = jnp.exp(jnp.arange(half, dtype=jnp.float32) * (-2.0 * math.log(10000.0) / width))
    angles = place.astype(jnp.float32)[:, None] * rates[None, :]
    cosine = jnp.cos(angles)[:, None, :]
    sine = sign * jnp.sin(angles)[:, None, :]
    first = values[..., :half]
    second = values[..., half:]
    return jnp.concatenate([first * cosine - second * sine, second * cosine + first * sine], axis=-1)

def layout(segments, skips, documents):
    count = segments.shape[0]
    labels = jnp.arange(documents, dtype=jnp.int32)
    member = segments[:, None] == labels[None, :]
    starts = lax.optimization_barrier(jnp.sum((segments[:, None] < labels[None, :]).astype(jnp.int32), axis=0))
    place = jnp.arange(count, dtype=jnp.int32) - lax.optimization_barrier(jnp.sum(jnp.where(member, starts[None, :], 0), axis=1))
    keep = 1.0 - lax.optimization_barrier(jnp.sum(jnp.where(member, skips[None, :], 0), axis=1)).astype(jnp.float32)
    return (place, place // BLOCK, keep)

def unit(values):
    return values * lax.rsqrt(lax.optimization_barrier(jnp.mean(values * values, axis=1, keepdims=True)) + EPSILON)

def layer(inputs, segments, skips, gain_one, query_weight, key_weight, value_weight, out_weight, gain_two, gate_weight, up_weight, down_weight):
    count = inputs.shape[0]
    place, blocks, keep = layout(segments, skips, NSEG)
    keep = keep[:, None]
    first_normed = low(unit(inputs) * gain_one)
    raw_query = low_back(matmul(first_normed, query_weight)).reshape(count, H, HD)
    raw_key = low_back(matmul(first_normed, key_weight)).reshape(count, KV, HD)
    values = low(low_back(matmul(first_normed, value_weight))).reshape(count, KV, HD)
    queries = low(rotate(raw_query, place, 1.0))
    keys = low(rotate(raw_key, place, 1.0))
    allowed = (segments[:, None] == segments[None, :]) & (blocks[None, :] <= blocks[:, None])
    share = H // KV
    scale = 1.0 / math.sqrt(HD)

    def one_head(head):
        query = lax.dynamic_index_in_dim(queries, head, axis=1, keepdims=False)
        key = lax.dynamic_index_in_dim(keys, head // share, axis=1, keepdims=False)
        value = lax.dynamic_index_in_dim(values, head // share, axis=1, keepdims=False)
        scores = low_back(matmul(query, key.T) * scale)
        probs = jax.nn.softmax(jnp.where(allowed, scores, NEGATIVE), axis=1)
        return matmul(low(probs), value)
    heads = lax.map(jax.checkpoint(one_head), jnp.arange(H, dtype=jnp.int32))
    attended = heads.transpose(1, 0, 2).reshape(count, H * HD)
    mixed = low(low_back(attended))
    branch = low_back(matmul(mixed, out_weight))
    middle = inputs + keep * branch
    second_normed = low(unit(middle) * gain_two)
    gate = low_back(matmul(second_normed, gate_weight))
    up = low_back(matmul(second_normed, up_weight))
    hidden = low(jax.nn.silu(gate) * up)
    feedforward = low_back(matmul(hidden, down_weight))
    return middle + keep * feedforward

def reference(tokens, segment_ids, skip_mask, norm1_gain, w_query, w_key, w_value, w_out, norm2_gain, w_gate, w_up, w_down, cotangent):
    weights = tuple((weight.astype(jnp.float32) for weight in (norm1_gain, w_query, w_key, w_value, w_out, norm2_gain, w_gate, w_up, w_down)))

    def step(sums, item):
        inputs, segments, skips, upstream = item

        def apply(values, *params):
            return layer(values, segments, skips, *params)
        output, pullback = jax.vjp(apply, inputs.astype(jnp.float32), *weights)
        grads = pullback(upstream.astype(jnp.float32))
        sums = tuple((total + grad for total, grad in zip(sums, grads[1:])))
        return (sums, (output.astype(jnp.bfloat16), grads[0].astype(jnp.bfloat16)))
    start = tuple((jnp.zeros(weight.shape, jnp.float32) for weight in weights))
    totals, (outputs, input_grads) = lax.scan(step, start, (tokens, segment_ids, skip_mask, cotangent))
    return (outputs, input_grads, totals[0], totals[1], totals[2], totals[3], totals[4], totals[5], totals[6], totals[7], totals[8])
```

```python
import math

import jax
import jax.numpy as jnp
from jax import lax
from jax.sharding import Mesh
from jax.sharding import PartitionSpec as P

HD = 128
BLOCK = 256
EPSILON = 1e-05
NEGATIVE = -1e30

AXES = ("z", "y", "xh", "xl", "c")
DP = ("z", "y", "xh")
MP = ("xl", "c")
ZY = ("z", "y")
X4 = ("xh", "xl")
F32 = jnp.float32
BF16 = jnp.bfloat16


def exchange(value, axes):
    return lax.all_to_all(value, axes, split_axis=0, concat_axis=0, tiled=True)


def from_everyone(value, axes):
    return exchange(jnp.broadcast_to(value, (lax.axis_size(axes), *value.shape)), axes)


def flip(value, axis):
    return lax.ppermute(value, axis, [(0, 1), (1, 0)])


def swap(value):
    return lax.ppermute(value, ("xh", "c"), [(1, 2), (2, 1)])


def pick(first, when, own, other):
    return jnp.where(when == 0, own, other) if first else jnp.where(when == 0, other, own)


def ordered(when, own, other, axis):
    return jnp.concatenate([pick(True, when, own, other), pick(False, when, own, other)], axis=axis)


def rope_tables(place, sign):
    half = HD // 2
    rates = jnp.exp(jnp.arange(half, dtype=F32) * (-2.0 * math.log(10000.0) / HD))
    angles = place.astype(F32)[:, None] * rates[None, :]
    return jnp.cos(angles)[:, None, :], sign * jnp.sin(angles)[:, None, :]


def rotate(values, cosine, sine):
    half = HD // 2
    first, second = values[..., :half], values[..., half:]
    return jnp.concatenate(
        [first * cosine - second * sine, second * cosine + first * sine], axis=-1
    )


def layout(segments, skips, documents):
    count = segments.shape[0]
    labels = jnp.arange(documents, dtype=jnp.int32)
    member = segments[:, None] == labels[None, :]
    starts = jnp.sum((segments[:, None] < labels[None, :]).astype(jnp.int32), axis=0)
    place = jnp.arange(count, dtype=jnp.int32) - jnp.sum(
        jnp.where(member, starts[None, :], 0), axis=1
    )
    keep = 1.0 - jnp.sum(jnp.where(member, skips[None, :], 0), axis=1).astype(F32)
    return place, place // BLOCK, keep


def unit_scale(values):
    factor = lax.rsqrt(jnp.mean(values * values, axis=1, keepdims=True) + EPSILON)
    return values * factor, factor


def dot(a, b, dims):
    return lax.dot_general(a, b, (dims, ((), ())), preferred_element_type=F32)


def spread(piece, xl, core):
    both = ordered(xl, piece, flip(piece, "xl"), 0)
    return ordered(core, both[None], flip(both, "c")[None], 0)


def on_device(
    tokens,
    segment_ids,
    skip_mask,
    norm1_gain,
    w_query,
    w_key,
    w_value,
    w_out,
    norm2_gain,
    w_gate,
    w_up,
    w_down,
    cotangent,
):
    local, width = tokens.shape[1:]
    documents = skip_mask.shape[1]
    xh, xl, core = lax.axis_index("xh"), lax.axis_index("xl"), lax.axis_index("c")
    chip = lax.axis_index(X4)
    plane = lax.axis_index(ZY)
    planes = lax.axis_size(ZY)
    queries = 2 * local
    mine = queries // 4
    offset = plane * queries
    heads = w_query.shape[1] // HD
    wide = heads * HD
    scale = 1.0 / math.sqrt(HD)
    rows = w_query.shape[0]
    hidden_local = w_gate.shape[1]
    tiles = hidden_local // 128
    part = (tiles + 1) // 2 * 128
    lead = hidden_local - part
    spare = part - lead

    gain_one = norm1_gain.astype(F32)[:, None]
    gain_two = norm2_gain.astype(F32)[:, None]

    with jax.named_scope("attn_weights"):
        own_heads = jnp.concatenate(
            [
                (gain_one * w_query.astype(F32)).astype(BF16),
                (gain_one * w_key.astype(F32)).astype(BF16),
                (gain_one * w_value.astype(F32)).astype(BF16),
                w_out.T,
            ],
            axis=1,
        )
        half_heads = jnp.where(core == xh, own_heads, swap(own_heads))
        total_in = wide + 2 * HD
        half_in = from_everyone(half_heads[:, :total_in], ZY)
        half_out = from_everyone(half_heads[:, total_in:], ZY)

        def both_halves(half):
            other = flip(half, "c")
            pair = ordered(core, half[:, None], other[:, None], 1)
            return pair.reshape(width, half.shape[-1])

        weight_in = both_halves(half_in)
        weight_out = both_halves(half_out)

    with jax.named_scope("ffn_weights"):
        own_hidden = jnp.stack(
            [
                (gain_two * w_gate.astype(F32)).astype(BF16),
                (gain_two * w_up.astype(F32)).astype(BF16),
                w_down.T,
            ],
            axis=1,
        ).reshape(rows, 3, hidden_local)

        def columns(which):
            share = lax.dynamic_slice_in_dim(own_hidden, which * lead, part, axis=2)
            blank = (which == 1) & (lax.broadcasted_iota(jnp.int32, share.shape, 2) < spare)
            return jnp.where(blank, jnp.zeros_like(share), share).reshape(rows, 3 * part)

        pair_rows = ordered(xh, columns(xh), flip(columns(1 - xh), "xh"), 0)
        hidden_weight = lax.all_gather(pair_rows, ZY, axis=0, tiled=True)

    with jax.named_scope("layout"):
        segment_own = lax.dynamic_index_in_dim(segment_ids, core, 0, keepdims=False)
        segment_other = lax.dynamic_index_in_dim(segment_ids, 1 - core, 0, keepdims=False)
        skip_own = lax.dynamic_index_in_dim(skip_mask, core, 0, keepdims=False)
        skip_other = lax.dynamic_index_in_dim(skip_mask, 1 - core, 0, keepdims=False)
        place, blocks, keep = layout(segment_own, skip_own, documents)
        keep_other = layout(segment_other, skip_other, documents)[2]
        here = lambda a, at, n: lax.dynamic_slice_in_dim(a, at, n)
        here_place, here_block = here(place, offset, queries), here(blocks, offset, queries)
        here_seg = here(segment_own, offset, queries)
        keep_all = jnp.concatenate([here(keep, offset, queries), here(keep_other, offset, queries)])
        keep_mine = here(keep, offset + chip * mine, mine)[:, None]
        cosine, sine = rope_tables(here_place, 1.0)

    with jax.named_scope("first_norm"):
        tokens_own = lax.dynamic_index_in_dim(tokens, core, 0, keepdims=False)
        tokens_all = ordered(xh, tokens_own, flip(tokens_own, "xh"), 0)
        unit_all = unit_scale(tokens_all.astype(F32))[0].astype(BF16)
        x_mine = lax.dynamic_slice_in_dim(tokens_own, xl * mine, mine).astype(F32)
        first_unit, first_factor = unit_scale(x_mine)

    with jax.named_scope("cotangent"):
        grad_own = lax.dynamic_index_in_dim(cotangent, core, 0, keepdims=False)
        grad_all = ordered(xh, grad_own, flip(grad_own, "xh"), 0)
        grad_both = jnp.concatenate([grad_all, flip(grad_all, "c")], axis=0)
        ffn_grad = (keep_all[:, None] * grad_both.astype(F32)).astype(BF16)
        upstream = lax.dynamic_slice_in_dim(grad_own, xl * mine, mine).astype(F32)

    with jax.named_scope("project"):
        raw = dot(unit_all, weight_in, ((1,), (0,)))
        query = rotate(raw[:, :wide].reshape(queries, heads, HD), cosine, sine).astype(BF16)
        key = rotate(raw[:, wide : wide + HD].reshape(queries, 1, HD), cosine, sine)
        key_value = jnp.concatenate([key[:, 0], raw[:, wide + HD :]], axis=1).astype(BF16)
    with jax.named_scope("kv_gather"):
        everyone = from_everyone(key_value, ZY)
        every = planes * queries
        everyone = everyone.reshape(every, 2 * HD)
        keys, values = everyone[:, :HD], everyone[:, HD:]

    with jax.named_scope("attend"):
        allowed = (here_seg[:, None] == segment_own[None, :]) & (
            blocks[None, :] <= here_block[:, None]
        )
        query_rows = query.transpose(1, 0, 2)
        scores = jnp.einsum("hqd,nd->hqn", query_rows, keys, preferred_element_type=F32) * scale
        masked = jnp.where(allowed[None], scores, NEGATIVE)
        top = jnp.max(masked, axis=2)
        weights = jnp.where(allowed[None], jnp.exp(masked - top[..., None]), 0.0)
        total = jnp.sum(weights, axis=2)
        running = jnp.einsum("hqn,nd->hqd", weights.astype(BF16), values, preferred_element_type=F32)
        log_total = top + jnp.log(total)
        mixed_rows = (running / total[..., None]).astype(BF16)
        mixed = mixed_rows.transpose(1, 0, 2).reshape(queries, wide)

    with jax.named_scope("branch"):
        partial = dot(mixed, weight_out, ((1,), (1,))).astype(BF16)
        branch = exchange(partial.reshape(4, mine, width), X4).astype(F32).sum(axis=0)
        middle = x_mine + keep_mine * branch
        second_unit, second_factor = unit_scale(middle)
        unit_own = from_everyone(second_unit.astype(BF16), X4).reshape(queries, width)
        unit_both = jnp.concatenate([unit_own, flip(unit_own, "c")], axis=0)

    with jax.named_scope("ffn"):
        gate_weight = hidden_weight[:, :part]
        up_weight = hidden_weight[:, part : 2 * part]
        down_weight = hidden_weight[:, 2 * part :]
        gate = dot(unit_both, gate_weight, ((1,), (0,)))
        up = dot(unit_both, up_weight, ((1,), (0,)))
        sigmoid = jax.nn.sigmoid(gate)
        activated = gate * sigmoid
        hidden = (activated * up).astype(BF16)

        def own_sum(partial):
            sent = flip(partial[queries:].astype(BF16), "c")
            both = (partial[:queries] + sent.astype(F32)).astype(BF16)
            return exchange(both.reshape(4, mine, width), X4).astype(F32).sum(axis=0)

    with jax.named_scope("ffn_back"):
        hidden_grad = dot(ffn_grad, down_weight, ((1,), (0,)))
        gate_grad = (hidden_grad * up * sigmoid * (1.0 + gate * (1.0 - sigmoid))).astype(BF16)
        up_grad = (hidden_grad * activated).astype(BF16)
        scaled_two = own_sum(
            dot(gate_grad, gate_weight, ((1,), (1,))) + dot(up_grad, up_weight, ((1,), (1,)))
        )
        hidden_weight_grad = jnp.concatenate(
            [
                dot(unit_both, gate_grad, ((0,), (0,))).astype(BF16),
                dot(unit_both, up_grad, ((0,), (0,))).astype(BF16),
                dot(ffn_grad, hidden, ((0,), (0,))).astype(BF16),
            ],
            axis=1,
        )
        hidden_owned = lax.psum_scatter(hidden_weight_grad, ZY, scatter_dimension=0, tiled=True)
        gain_two_sum = jnp.sum(scaled_two * second_unit, axis=0)
        middle_grad = upstream + second_factor * (
            scaled_two - second_unit * jnp.mean(scaled_two * second_unit, axis=1, keepdims=True)
        )
        branch_grad = from_everyone((keep_mine * middle_grad).astype(BF16), X4)
        branch_grad = branch_grad.reshape(queries, width)

    with jax.named_scope("result"):
        feedforward = own_sum(dot(hidden, down_weight, ((1,), (1,))))
        result = spread((middle + keep_mine * feedforward).astype(BF16), xl, core)

    with jax.named_scope("attend_back"):
        mixed_grad = dot(branch_grad, weight_out, ((1,), (0,))).astype(BF16)
        out_weight_grad = dot(branch_grad, mixed, ((0,), (0,)))
        grad_rows = mixed_grad.reshape(queries, heads, HD).transpose(1, 0, 2)
        delta = jnp.sum(grad_rows.astype(F32) * mixed_rows.astype(F32), axis=2)
        probs = jnp.where(allowed[None], jnp.exp(scores - log_total[..., None]), 0.0)
        prob_grad = jnp.einsum("hqd,nd->hqn", grad_rows, values, preferred_element_type=F32)
        score_grad = (probs * (prob_grad - delta[..., None])).astype(BF16)
        query_grad = jnp.einsum("hqn,nd->qhd", score_grad, keys, preferred_element_type=F32) * scale
        key_grad = (
            jnp.einsum("hqn,hqd->nd", score_grad, query_rows, preferred_element_type=F32) * scale
        )
        value_grad = jnp.einsum(
            "hqn,hqd->nd", probs.astype(BF16), grad_rows, preferred_element_type=F32
        )
        stacked = jnp.concatenate([key_grad, value_grad], axis=1).astype(BF16)
        owned = exchange(stacked.reshape(planes, queries, 2 * HD), ZY).astype(F32).sum(axis=0)
        query_pre = rotate(query_grad, cosine, -sine).astype(BF16).reshape(queries, wide)
        key_pre = rotate(owned[:, None, :HD], cosine, -sine)[:, 0].astype(BF16)
        pre = jnp.concatenate([query_pre, key_pre, owned[:, HD:].astype(BF16)], axis=1)

    with jax.named_scope("input_grad"):
        partial = dot(pre, weight_in, ((1,), (1,))).astype(BF16)
        scaled_one = exchange(partial.reshape(4, mine, width), X4).astype(F32).sum(axis=0)
        gain_one_sum = jnp.sum(scaled_one * first_unit, axis=0)
        input_grad = middle_grad + first_factor * (
            scaled_one - first_unit * jnp.mean(scaled_one * first_unit, axis=1, keepdims=True)
        )
        input_grad = spread(input_grad.astype(BF16), xl, core)

    with jax.named_scope("head_grads"):
        in_weight_grad = dot(unit_all, pre, ((0,), (0,)))

        def owned_heads(grad):
            pair = grad.reshape(planes, 2, rows, grad.shape[-1])
            here_half = jnp.where(core == 0, pair[:, 0], pair[:, 1])
            there_half = jnp.where(core == 0, pair[:, 1], pair[:, 0])
            half = (here_half + flip(there_half.astype(BF16), "c").astype(F32)).astype(BF16)
            summed = exchange(half, ZY).astype(F32).sum(axis=0)
            return jnp.where(core == xh, summed, swap(summed.astype(BF16)).astype(F32))

        in_owned = owned_heads(in_weight_grad)
        out_owned = owned_heads(out_weight_grad)

    with jax.named_scope("ffn_grads"):
        owned_pair = hidden_owned.reshape(2, rows, 3 * part)
        kept = jnp.where(xh == 0, owned_pair[0], owned_pair[1])
        sent = flip(jnp.where(xh == 0, owned_pair[1], owned_pair[0]), "xh")
        low = pick(True, xh, kept, sent).reshape(rows, 3, part).astype(F32)
        high = pick(False, xh, kept, sent).reshape(rows, 3, part).astype(F32)
        hidden_full = [
            jnp.concatenate([low[:, i], high[:, i, spare:]], axis=1) for i in range(3)
        ]

    with jax.named_scope("gain_grads"):
        sums = jnp.stack([gain_one_sum, gain_two_sum]).reshape(2, planes * 2, 1, rows)
        sums = jnp.broadcast_to(sums.transpose(1, 2, 0, 3), (planes * 2, 4, 2, rows))
        sums = exchange(sums.reshape(planes * 8, 2, rows), AXES).sum(axis=0)

    return (
        result,
        input_grad,
        sums[0] / gain_one[:, 0],
        gain_one * in_owned[:, :wide],
        gain_one * in_owned[:, wide : wide + HD],
        gain_one * in_owned[:, wide + HD :],
        out_owned.T,
        sums[1] / gain_two[:, 0],
        gain_two * hidden_full[0],
        gain_two * hidden_full[1],
        hidden_full[2].T,
    )


def solution(mesh):
    split = Mesh(mesh.devices.reshape(4, 4, 2, 2, 2), AXES)
    token = P(None, DP, None)
    by_row = P(DP, MP)
    by_column = P(MP, DP)
    in_specs = (
        token, P(), P(), P(DP), by_row, by_row, by_row, by_column,
        P(DP), by_row, by_row, by_column, token,
    )
    out_specs = (
        token, token, P(DP), by_row, by_row, by_row, by_column,
        P(DP), by_row, by_row, by_column,
    )
    return jax.shard_map(
        on_device, mesh=split, in_specs=in_specs, out_specs=out_specs, check_vma=False
    )
```

```python
import math

import jax
import jax.numpy as jnp
from jax import lax
from jax.experimental import pallas as pl
from jax.experimental.pallas import tpu as pltpu
from jax.sharding import Mesh
from jax.sharding import PartitionSpec as P

HD = 128
BLOCK = 256
EPSILON = 1e-05
MASKED = -1e30
FLOOR = -1e29
LOG2E = 1.4426950408889634
TILE = 512
VMEM_LIMIT = 56 * 1024 * 1024

AXES = ("z", "y", "xh", "xl", "c")
DP = ("z", "y", "xh")
MP = ("xl", "c")
ZY = ("z", "y")
X4 = ("xh", "xl")
F32 = jnp.float32
BF16 = jnp.bfloat16


def after(value, *others):
    return lax.optimization_barrier((value, *others))[0]


def exchange(value, axes):
    return lax.all_to_all(value, axes, split_axis=0, concat_axis=0, tiled=True)


def from_everyone(value, axes):
    return exchange(jnp.broadcast_to(value, (lax.axis_size(axes), *value.shape)), axes)


def flip(value, axis):
    return lax.ppermute(value, axis, [(0, 1), (1, 0)])


def swap(value):
    return lax.ppermute(value, ("xh", "c"), [(1, 2), (2, 1)])


def turn(value, step):
    return lax.ppermute(value, X4, [(i, (i + step) % 4) for i in range(4)])


def ring_gather(block):
    far = turn(block, 2)
    return [block, turn(block, 1), far, turn(block, 3)]


def ring_sum(pieces):
    far = turn(pieces[2], -2)
    near = [turn(pieces[s], -s) for s in (1, 3)]
    return sum((a.astype(F32) for a in (*near, far)), pieces[0].astype(F32))


def behind(blocks, chip):
    return [lax.dynamic_index_in_dim(blocks, (chip - s) % 4, 0, keepdims=False) for s in range(4)]


def pick(first, when, own, other):
    return jnp.where(when == 0, own, other) if first else jnp.where(when == 0, other, own)


def ordered(when, own, other, axis):
    return jnp.concatenate([pick(True, when, own, other), pick(False, when, own, other)], axis=axis)


def rope_tables(place):
    half = HD // 2
    rates = jnp.exp(jnp.arange(half, dtype=F32) * (-2.0 * math.log(10000.0) / HD))
    angles = place.astype(F32)[:, None] * rates[None, :]
    return jnp.cos(angles)[:, None, :], jnp.sin(angles)[:, None, :]


def rotate(values, cosine, sine):
    half = HD // 2
    first, second = values[..., :half], values[..., half:]
    return jnp.concatenate(
        [first * cosine - second * sine, second * cosine + first * sine], axis=-1
    )


def layout(segments, skips, documents):
    count = segments.shape[0]
    labels = jnp.arange(documents, dtype=jnp.int32)
    member = segments[:, None] == labels[None, :]
    starts = jnp.sum((segments[:, None] < labels[None, :]).astype(jnp.int32), axis=0)
    ends = jnp.sum((segments[:, None] <= labels[None, :]).astype(jnp.int32), axis=0)
    start = jnp.sum(jnp.where(member, starts[None, :], 0), axis=1)
    end = jnp.sum(jnp.where(member, ends[None, :], 0), axis=1)
    place = jnp.arange(count, dtype=jnp.int32) - start
    keep = 1.0 - jnp.sum(jnp.where(member, skips[None, :], 0), axis=1).astype(F32)
    last = jnp.minimum(start + (place // BLOCK + 1) * BLOCK, end)
    return place, start, last, keep


def unit_scale(values):
    factor = lax.rsqrt(jnp.mean(values * values, axis=1, keepdims=True) + EPSILON)
    return values * factor, factor


def dot(a, b, dims):
    return lax.dot_general(a, b, (dims, ((), ())), preferred_element_type=F32)


def whole(shape):
    return pl.BlockSpec(shape, lambda *_: (0,) * len(shape))


def call(kernel, name, flops, moved, exps=0, **options):
    params = pltpu.CompilerParams(vmem_limit_bytes=VMEM_LIMIT)
    cost = pl.CostEstimate(flops=flops, bytes_accessed=moved, transcendentals=exps)
    return pl.pallas_call(
        kernel, name=name, compiler_params=params, cost_estimate=cost, **options
    )


def by_heads(block, heads):
    return jnp.concatenate([block[:, h * HD : (h + 1) * HD] for h in range(heads)], axis=0)


def store_heads(out_ref, turned, heads, queries):
    for h in range(heads):
        piece = turned[:, h * queries : (h + 1) * queries]
        out_ref[:, h * HD : (h + 1) * HD] = piece.T.astype(out_ref.dtype)


def reach(start, low_ref, high_ref, count):
    spot = start + lax.broadcasted_iota(jnp.int32, (TILE, count), 0)
    return (spot >= low_ref[...]) & (spot < high_ref[...])


def attend_kernel(heads, queries, scale, span, q_ref, kv_ref, low_ref, high_ref,
                  out_ref, turned_ref, log_ref, rows, top, total, running):
    count = heads * queries
    rows[...] = by_heads(q_ref[...], heads)
    top[...] = jnp.full_like(top, FLOOR)
    total[...] = jnp.zeros_like(total)
    running[...] = jnp.zeros_like(running)

    def step(i, _):
        start = pl.multiple_of(i * TILE, TILE)
        keys = kv_ref[pl.ds(start, TILE), :HD]
        values = kv_ref[pl.ds(start, TILE), HD:]
        scores = dot(keys, rows[...], ((1,), (1,))) * (scale * LOG2E)
        scores = jnp.where(reach(start, low_ref, high_ref, count), scores, MASKED)
        higher = jnp.maximum(top[...], jnp.max(scores, axis=0, keepdims=True))
        weights = jnp.exp2(scores - higher)
        fade = jnp.exp2(top[...] - higher)
        total[...] = total[...] * fade + jnp.sum(weights, axis=0, keepdims=True)
        running[...] = running[...] * fade + dot(values, weights.astype(BF16), ((0,), (0,)))
        top[...] = higher
        return 0

    lax.fori_loop(span[0], span[1], step, 0)
    mixed = running[...] / total[...]
    turned_ref[...] = mixed.astype(BF16)
    store_heads(out_ref, mixed, heads, queries)
    log_ref[...] = top[...] + jnp.log2(total[...])


def attend(span, query, key_value, low, high, heads, scale):
    queries = query.shape[0]
    count = heads * queries
    line = whole((1, count))
    return call(
        lambda *refs: attend_kernel(heads, queries, scale, *refs),
        "attend",
        4 * count * key_value.shape[0] * HD,
        2 * key_value.size + 6 * query.size,
        count * key_value.shape[0],
        out_shape=[
            jax.ShapeDtypeStruct(query.shape, BF16),
            jax.ShapeDtypeStruct((HD, count), BF16),
            jax.ShapeDtypeStruct((1, count), F32),
        ],
        grid_spec=pltpu.PrefetchScalarGridSpec(
            num_scalar_prefetch=1,
            grid=(1,),
            in_specs=[whole(query.shape), whole(key_value.shape), line, line],
            out_specs=[whole(query.shape), whole((HD, count)), line],
            scratch_shapes=[
                pltpu.VMEM((count, HD), BF16),
                pltpu.VMEM((1, count), F32),
                pltpu.VMEM((1, count), F32),
                pltpu.VMEM((HD, count), F32),
            ],
        ),
    )(span, query, key_value, low, high)


def attend_back_kernel(heads, queries, scale, span, q_ref, kv_ref, weight_ref, mixed_ref, log_ref,
                       low_ref, high_ref, p0_ref, p1_ref, p2_ref, p3_ref,
                       dq_ref, dkv_ref, branch_ref, rows, grads, delta, turned):
    count = heads * queries
    mine = queries // 4
    for s, piece in enumerate((p0_ref, p1_ref, p2_ref, p3_ref)):
        at = pl.multiple_of(lax.rem(span[2] + 4 - s, 4) * mine, mine)
        branch_ref[pl.ds(at, mine), :] = piece[...]
    mixed_grad = dot(branch_ref[...], weight_ref[...], ((1,), (0,))).astype(BF16).astype(F32)
    for h in range(heads):
        here = slice(h * queries, (h + 1) * queries)
        grads[:, here] = mixed_grad[:, h * HD : (h + 1) * HD].T.astype(BF16)
    delta[...] = jnp.sum(
        grads[...].astype(F32) * mixed_ref[...].astype(F32), axis=0, keepdims=True
    )
    rows[...] = by_heads(q_ref[...], heads)
    turned[...] = jnp.zeros_like(turned)
    dkv_ref[...] = jnp.zeros_like(dkv_ref)

    def step(i, _):
        start = pl.multiple_of(i * TILE, TILE)
        keys = kv_ref[pl.ds(start, TILE), :HD]
        values = kv_ref[pl.ds(start, TILE), HD:]
        scores = dot(keys, rows[...], ((1,), (1,))) * (scale * LOG2E) - log_ref[...]
        scores = jnp.where(reach(start, low_ref, high_ref, count), scores, MASKED)
        probs = jnp.exp2(scores)
        prob_grad = dot(values, grads[...], ((1,), (0,)))
        score_grad = (probs * (prob_grad - delta[...])).astype(BF16)
        dkv_ref[pl.ds(start, TILE), :HD] = (
            dot(score_grad, rows[...], ((1,), (0,))) * scale
        ).astype(BF16)
        dkv_ref[pl.ds(start, TILE), HD:] = dot(
            probs.astype(BF16), grads[...], ((1,), (1,))
        ).astype(BF16)
        turned[...] += dot(keys, score_grad, ((0,), (0,)))
        return 0

    lax.fori_loop(span[0], span[1], step, 0)
    store_heads(dq_ref, turned[...] * scale, heads, queries)


def attend_back(span, query, key_value, weight, mixed_turned, log_total, low, high, pieces,
                heads, scale):
    queries = query.shape[0]
    width = weight.shape[0]
    count = heads * queries
    line = whole((1, count))
    return call(
        lambda *refs: attend_back_kernel(heads, queries, scale, *refs),
        "attend_back",
        10 * count * key_value.shape[0] * HD,
        4 * key_value.size + 6 * query.size + 2 * weight.size,
        count * key_value.shape[0],
        out_shape=[
            jax.ShapeDtypeStruct(query.shape, F32),
            jax.ShapeDtypeStruct(key_value.shape, BF16),
            jax.ShapeDtypeStruct((queries, width), BF16),
        ],
        grid_spec=pltpu.PrefetchScalarGridSpec(
            num_scalar_prefetch=1,
            grid=(1,),
            in_specs=[
                whole(query.shape), whole(key_value.shape), whole(weight.shape),
                whole((HD, count)), line, line, line, *[whole(p.shape) for p in pieces],
            ],
            out_specs=[whole(query.shape), whole(key_value.shape), whole((queries, width))],
            scratch_shapes=[
                pltpu.VMEM((count, HD), BF16),
                pltpu.VMEM((HD, count), BF16),
                pltpu.VMEM((1, count), F32),
                pltpu.VMEM((HD, count), F32),
            ],
        ),
    )(span, query, key_value, weight, mixed_turned, log_total, low, high, *pieces)


def hidden_kernel(half, own_ref, other_ref, grad_own_ref, grad_other_ref, gate_ref, up_ref,
                  down_ref, hid_ref, dgate_ref, dup_ref, unit, grad):
    @pl.when(pl.program_id(0) == 0)
    def _():
        unit[:half] = own_ref[...]
        unit[half:] = other_ref[...]
        grad[:half] = grad_own_ref[...]
        grad[half:] = grad_other_ref[...]

    gate = dot(unit[...], gate_ref[...], ((1,), (0,)))
    up = dot(unit[...], up_ref[...], ((1,), (0,)))
    sigmoid = jax.nn.sigmoid(gate)
    activated = gate * sigmoid
    hid_ref[...] = (activated * up).astype(BF16)
    hidden_grad = dot(grad[...], down_ref[...], ((1,), (0,)))
    dgate_ref[...] = (hidden_grad * up * sigmoid * (1.0 + gate * (1.0 - sigmoid))).astype(BF16)
    dup_ref[...] = (hidden_grad * activated).astype(BF16)


def hidden_units(units, grads, weight, part):
    half, width = units[0].shape
    count = 2 * half
    step = 256
    steps = part // step
    block = lambda which: pl.BlockSpec((width, step), lambda j: (0, which * steps + j))
    out = pl.BlockSpec((count, step), lambda j: (0, j))
    return call(
        lambda *refs: hidden_kernel(half, *refs),
        "hidden_units",
        6 * count * width * part,
        2 * weight.size + 4 * count * width,
        count * part,
        grid=(steps,),
        in_specs=[whole((half, width))] * 4 + [block(0), block(1), block(2)],
        out_specs=[out] * 3,
        out_shape=[jax.ShapeDtypeStruct((count, part), BF16)] * 3,
        scratch_shapes=[pltpu.VMEM((count, width), BF16)] * 2,
    )(*units, *grads, weight, weight, weight)


def unit_grad_kernel(half, part, dgate_ref, dup_ref, weight_ref, own_ref, other_ref):
    weight = weight_ref[...]
    full = dot(dgate_ref[...], weight[:, :part], ((1,), (1,)))
    full += dot(dup_ref[...], weight[:, part : 2 * part], ((1,), (1,)))
    own_ref[...] = full[:half]
    other_ref[...] = full[half:].astype(BF16)


def unit_grad(dgate, dup, weight, part):
    count = dgate.shape[0]
    width = weight.shape[0]
    half, step = count // 2, 512
    out = pl.BlockSpec((half, step), lambda j: (0, j))
    return call(
        lambda *refs: unit_grad_kernel(half, part, *refs),
        "unit_grad",
        4 * count * width * part,
        4 * width * part + 6 * half * width,
        grid=(width // step,),
        in_specs=[
            whole(dgate.shape),
            whole(dup.shape),
            pl.BlockSpec((step, 2 * part), lambda j: (j, 0)),
        ],
        out_specs=[out] * 2,
        out_shape=[
            jax.ShapeDtypeStruct((half, width), F32),
            jax.ShapeDtypeStruct((half, width), BF16),
        ],
    )(dgate, dup, weight)


def weight_grad_kernel(half, part, own_ref, other_ref, grad_own_ref, grad_other_ref, dgate_ref,
                       dup_ref, hid_ref, out_ref):
    unit = jnp.concatenate([own_ref[...], other_ref[...]], axis=0)
    grad = jnp.concatenate([grad_own_ref[...], grad_other_ref[...]], axis=0)
    out_ref[:, :part] = dot(unit, dgate_ref[...], ((0,), (0,))).astype(BF16)
    out_ref[:, part : 2 * part] = dot(unit, dup_ref[...], ((0,), (0,))).astype(BF16)
    out_ref[:, 2 * part :] = dot(grad, hid_ref[...], ((0,), (0,))).astype(BF16)


def weight_grad(units, grads, dgate, dup, hid):
    half, width = units[0].shape
    count, part = hid.shape
    step = 256
    column = pl.BlockSpec((half, step), lambda j: (0, j))
    return call(
        lambda *refs: weight_grad_kernel(half, part, *refs),
        "weight_grad",
        6 * count * width * part,
        6 * width * part + 8 * half * width,
        grid=(width // step,),
        in_specs=[column] * 4 + [whole(dgate.shape), whole(dup.shape), whole(hid.shape)],
        out_specs=pl.BlockSpec((step, 3 * part), lambda j: (j, 0)),
        out_shape=jax.ShapeDtypeStruct((width, 3 * part), BF16),
    )(*units, *grads, dgate, dup, hid)


def spread(piece, xl, core):
    both = ordered(xl, piece, flip(piece, "xl"), 0)
    return ordered(core, both[None], flip(both, "c")[None], 0)


def over_mp(value):
    value = value + flip(value, "c")
    return value + flip(value, "xl")


def on_device(
    tokens,
    segment_ids,
    skip_mask,
    norm1_gain,
    w_query,
    w_key,
    w_value,
    w_out,
    norm2_gain,
    w_gate,
    w_up,
    w_down,
    cotangent,
):
    local, width = tokens.shape[1:]
    documents = skip_mask.shape[1]
    xh, xl, core = lax.axis_index("xh"), lax.axis_index("xl"), lax.axis_index("c")
    chip = lax.axis_index(X4)
    plane = lax.axis_index(ZY)
    planes = lax.axis_size(ZY)
    queries = 2 * local
    mine = queries // 4
    every = planes * queries
    offset = plane * queries
    heads = w_query.shape[1] // HD
    wide = heads * HD
    scale = 1.0 / math.sqrt(HD)
    rows = w_query.shape[0]
    hidden_local = w_gate.shape[1]
    part = (hidden_local // 128 + 1) // 2 * 128
    lead = hidden_local - part
    spare = part - lead

    gain_one = norm1_gain.astype(F32)[:, None]
    gain_two = norm2_gain.astype(F32)[:, None]

    with jax.named_scope("attn_weights"):
        scaled = lambda w: (gain_one * w.astype(F32)).astype(BF16)
        own_heads = jnp.concatenate(
            [scaled(w_key), scaled(w_value), scaled(w_query), w_out.T], axis=1
        )
        half_heads = jnp.where(core == xh, own_heads, swap(own_heads))
        at_query, at_out = 2 * HD, 2 * HD + wide
        wide_weight = lax.all_gather(half_heads[:, at_query:], ("z", "y", "c"), axis=0, tiled=True)
        half_kv = from_everyone(half_heads[:, :at_query], ZY)
        pair_kv = ordered(core, half_kv[:, None], flip(half_kv, "c")[:, None], 1)
        weight_kv = pair_kv.reshape(width, at_query)

    with jax.named_scope("first_norm"):
        tokens_own = lax.dynamic_index_in_dim(tokens, core, 0, keepdims=False)
        tokens_all = ordered(xh, tokens_own, flip(tokens_own, "xh"), 0)
        unit_all = unit_scale(tokens_all.astype(F32))[0].astype(BF16)
        x_mine = lax.dynamic_slice_in_dim(tokens_own, xl * mine, mine).astype(F32)
        first_unit, first_factor = unit_scale(x_mine)

    with jax.named_scope("layout"):
        segment_own = lax.dynamic_index_in_dim(segment_ids, core, 0, keepdims=False)
        skip_own = lax.dynamic_index_in_dim(skip_mask, core, 0, keepdims=False)
        place, start, last, keep = layout(segment_own, skip_own, documents)
        here = lambda a: lax.dynamic_slice_in_dim(a, offset, queries)
        low, high = here(start), here(last)
        span = jnp.stack([low[0] // TILE, (high[-1] + TILE - 1) // TILE, chip])
        low, high = (jnp.tile(a, heads)[None] for a in (low, high))
        keep_here = here(keep).reshape(4, mine, 1)
        keep_mine = lax.dynamic_index_in_dim(keep_here, chip, 0, keepdims=False)
        cosine, sine = rope_tables(here(place))

    with jax.named_scope("project"):
        raw = dot(unit_all, weight_kv, ((1,), (0,)))
        key = rotate(raw[:, :HD].reshape(queries, 1, HD), cosine, sine)[:, 0]
        key_value = jnp.concatenate([key, raw[:, HD:]], axis=1).astype(BF16)
        everyone = from_everyone(key_value, ZY).reshape(every, 2 * HD)
        weight_query, weight_out = wide_weight[:, :wide], wide_weight[:, wide:]
        raw = dot(unit_all, weight_query, ((1,), (0,)))
        query = rotate(raw.reshape(queries, heads, HD), cosine, sine).astype(BF16)
        query = query.reshape(queries, wide)

    with jax.named_scope("ffn_weights"):
        own_hidden = [
            (gain_two * w_gate.astype(F32)).astype(BF16),
            (gain_two * w_up.astype(F32)).astype(BF16),
            w_down.T,
        ]

        def columns(which):
            blank = (which == 1) & (lax.broadcasted_iota(jnp.int32, (rows, part), 1) < spare)
            shares = []
            for w in own_hidden:
                share = jnp.where(which == 0, w[:, :part], w[:, lead:])
                shares.append(jnp.where(blank, jnp.zeros_like(share), share))
            return jnp.concatenate(shares, axis=1)

        pair_rows = ordered(xh, columns(xh), flip(after(columns(1 - xh), weight_kv), "xh"), 0)
        hidden_weight = lax.all_gather(after(pair_rows, key_value), ZY, axis=0, tiled=True)

    with jax.named_scope("cotangent"):
        grad_local = lax.dynamic_index_in_dim(cotangent, core, 0, keepdims=False)
        upstream = lax.dynamic_slice_in_dim(grad_local, xl * mine, mine).astype(F32)
        grad_all = ordered(xh, grad_local, flip(after(grad_local, key_value), "xh"), 0)
        grad_kept = (keep_here * grad_all.reshape(4, mine, width).astype(F32)).astype(BF16)
        grad_own = jnp.concatenate(behind(grad_kept, chip), axis=0)
        ffn_grads = (grad_own, flip(grad_own, "c"))

    with jax.named_scope("attend"):
        mixed, mixed_turned, log_total = attend(
            span, after(query, ffn_grads[1]), everyone, low, high, heads, scale
        )

    with jax.named_scope("branch"):
        partial = dot(mixed, weight_out, ((1,), (1,))).astype(BF16)
        branch = ring_sum(behind(partial.reshape(4, mine, width), chip))
        middle = x_mine + keep_mine * branch
        second_unit, second_factor = unit_scale(middle)
        unit_own = jnp.concatenate(ring_gather(second_unit.astype(BF16)), axis=0)
        units = (unit_own, flip(unit_own, "c"))

    def own_sum(own_part, other_part):
        both = (own_part + flip(other_part, "c").astype(F32)).astype(BF16)
        return both, ring_sum(list(both.reshape(4, mine, width)))

    with jax.named_scope("ffn"):
        hidden, gate_grad, up_grad = hidden_units(units, ffn_grads, hidden_weight, part)
        own_part, other_part = unit_grad(gate_grad, up_grad, hidden_weight, part)
        both, scaled_two = own_sum(own_part, other_part)
        hidden_weight_grad = weight_grad(
            units, ffn_grads, gate_grad, up_grad, after(hidden, both)
        )
        hidden_owned = lax.psum_scatter(hidden_weight_grad, ZY, scatter_dimension=0, tiled=True)
        middle_grad = upstream + second_factor * (
            scaled_two - second_unit * jnp.mean(scaled_two * second_unit, axis=1, keepdims=True)
        )
        pieces = ring_gather((keep_mine * middle_grad).astype(BF16))

    with jax.named_scope("attend_back"):
        query_grad, kv_grad, branch_grad = attend_back(
            span, query, everyone, weight_out, mixed_turned, log_total, low, high, pieces,
            heads, scale,
        )
        owned = exchange(kv_grad.reshape(planes, queries, 2 * HD), ZY)
        owned = owned.astype(F32).sum(axis=0)
        query_pre = rotate(query_grad.reshape(queries, heads, HD), cosine, -sine)
        query_pre = query_pre.astype(BF16).reshape(queries, wide)
        key_pre = rotate(owned[:, None, :HD], cosine, -sine)[:, 0].astype(BF16)
        kv_pre = jnp.concatenate([key_pre, owned[:, HD:].astype(BF16)], axis=1)

    def owned_half(grad):
        pair = grad.reshape(planes, 2, rows, grad.shape[-1])
        here_half = jnp.where(core == 0, pair[:, 0], pair[:, 1])
        there_half = jnp.where(core == 0, pair[:, 1], pair[:, 0])
        return (here_half + flip(there_half.astype(BF16), "c").astype(F32)).astype(BF16)

    def over_planes(half):
        return exchange(half, ZY).astype(F32).sum(axis=0)

    with jax.named_scope("head_grads"):
        query_half = owned_half(dot(unit_all, query_pre, ((0,), (0,))))
        out_half = owned_half(dot(branch_grad, mixed, ((0,), (0,))))
        wide_half = jnp.concatenate([query_half, out_half], axis=2)
        wide_owned = over_planes(after(wide_half, owned))
        kv_half = owned_half(dot(unit_all, kv_pre, ((0,), (0,))))
        kv_owned = over_planes(after(kv_half, wide_owned))
        summed = jnp.concatenate([kv_owned, wide_owned], axis=1)
        heads_owned = jnp.where(core == xh, summed, swap(summed.astype(BF16)).astype(F32))
        query_owned = heads_owned[:, at_query:at_out]
        key_owned, value_owned = heads_owned[:, :HD], heads_owned[:, HD:at_query]
        row_sum = lambda *pairs: sum(
            jnp.sum(g * w.astype(F32), axis=1, keepdims=True) for g, w in pairs
        )
        gain_one_grad = over_mp(
            row_sum((query_owned, w_query), (key_owned, w_key), (value_owned, w_value))
        )

    with jax.named_scope("result"):
        down = hidden_weight[:, 2 * part :]
        partial = dot(after(hidden, kv_grad), down, ((1,), (1,)))
        feedforward = own_sum(partial[:queries], partial[queries:].astype(BF16))[1]
        result = spread((middle + keep_mine * feedforward).astype(BF16), xl, core)

    with jax.named_scope("input_grad"):
        partial = dot(query_pre, weight_query, ((1,), (1,))) + dot(kv_pre, weight_kv, ((1,), (1,)))
        scaled_one = ring_sum(behind(partial.astype(BF16).reshape(4, mine, width), chip))
        input_grad = middle_grad + first_factor * (
            scaled_one - first_unit * jnp.mean(scaled_one * first_unit, axis=1, keepdims=True)
        )
        input_grad = spread(input_grad.astype(BF16), xl, core)

    with jax.named_scope("ffn_grads"):
        owned_pair = hidden_owned.reshape(2, rows, 3 * part)
        kept = jnp.where(xh == 0, owned_pair[0], owned_pair[1])
        sent = flip(jnp.where(xh == 0, owned_pair[1], owned_pair[0]), "xh")
        low_part = pick(True, xh, kept, sent).astype(F32)
        high_part = pick(False, xh, kept, sent).astype(F32)
        gate_owned, up_owned, down_owned = (
            jnp.concatenate(
                [low_part[:, i * part : (i + 1) * part], high_part[:, i * part + spare : (i + 1) * part]],
                axis=1,
            )
            for i in range(3)
        )
        gain_two_grad = over_mp(row_sum((gate_owned, w_gate), (up_owned, w_up)))

    return (
        result,
        input_grad,
        gain_one_grad[:, 0],
        gain_one * query_owned,
        gain_one * key_owned,
        gain_one * value_owned,
        heads_owned[:, at_out:].T,
        gain_two_grad[:, 0],
        gain_two * gate_owned,
        gain_two * up_owned,
        down_owned.T,
    )


def solution(mesh):
    split = Mesh(mesh.devices.reshape(4, 4, 2, 2, 2), AXES)
    token = P(None, DP, None)
    by_row = P(DP, MP)
    by_column = P(MP, DP)
    in_specs = (
        token, P(), P(), P(DP), by_row, by_row, by_row, by_column,
        P(DP), by_row, by_row, by_column, token,
    )
    out_specs = (
        token, token, P(DP), by_row, by_row, by_row, by_column,
        P(DP), by_row, by_row, by_column,
    )
    return jax.shard_map(
        on_device, mesh=split, in_specs=in_specs, out_specs=out_specs, check_vma=False
    )
```

```python
import math

import jax
import jax.numpy as jnp
from jax import lax
from jax.experimental import pallas as pl
from jax.experimental.pallas import tpu as pltpu
from jax.sharding import Mesh
from jax.sharding import PartitionSpec as P

HD = 128
BLOCK = 256
EPSILON = 1e-05
MASKED = -1e30
FLOOR = -1e29
LOG2E = 1.4426950408889634
TILE = 1024
BEHIND = 200
AHEAD = 100
VMEM_LIMIT = 56 * 1024 * 1024

AXES = ("z", "y", "xh", "xl", "c")
DP = ("z", "y", "xh")
MP = ("xl", "c")
ZY = ("z", "y")
X4 = ("xh", "xl")
F32 = jnp.float32
BF16 = jnp.bfloat16


def after(value, *others):
    return lax.optimization_barrier((value, *others))[0]


def exchange(value, axes):
    return lax.all_to_all(value, axes, split_axis=0, concat_axis=0, tiled=True)


def from_everyone(value, axes):
    return exchange(jnp.broadcast_to(value, (lax.axis_size(axes), *value.shape)), axes)


def flip(value, axis):
    return lax.ppermute(value, axis, [(0, 1), (1, 0)])


def swap(value):
    return lax.ppermute(value, ("xh", "c"), [(1, 2), (2, 1)])


def turn(value, step):
    return lax.ppermute(value, X4, [(i, (i + step) % 4) for i in range(4)])


def ring_gather(block):
    far = turn(block, 2)
    return [block, turn(block, 1), far, turn(block, 3)]


def ring_parts(pieces):
    far = turn(pieces[2], -2)
    return [pieces[0], *(turn(pieces[s], -s) for s in (1, 3)), far]


def ring_sum(pieces):
    return sum(a.astype(F32) for a in ring_parts(pieces))


def behind(blocks, chip):
    return [lax.dynamic_index_in_dim(blocks, (chip - s) % 4, 0, keepdims=False) for s in range(4)]


def pick(first, when, own, other):
    return jnp.where(when == 0, own, other) if first else jnp.where(when == 0, other, own)


def ordered(when, own, other, axis):
    return jnp.concatenate([pick(True, when, own, other), pick(False, when, own, other)], axis=axis)


def rope_tables(place, along):
    half = HD // 2
    rates = jnp.exp(jnp.arange(half, dtype=F32) * (-2.0 * math.log(10000.0) / HD))
    angles = jnp.expand_dims(place.astype(F32), 1 - along) * jnp.expand_dims(rates, along)
    return jnp.cos(angles), jnp.sin(angles)


def rotate(values, cosine, sine):
    half = HD // 2
    first, second = values[..., :half], values[..., half:]
    return jnp.concatenate(
        [first * cosine - second * sine, second * cosine + first * sine], axis=-1
    )


def layout(segments, skips, documents):
    count = segments.shape[0]
    labels = jnp.arange(documents, dtype=jnp.int32)
    member = segments[:, None] == labels[None, :]
    starts = jnp.sum((segments[:, None] < labels[None, :]).astype(jnp.int32), axis=0)
    ends = jnp.sum((segments[:, None] <= labels[None, :]).astype(jnp.int32), axis=0)
    start = jnp.sum(jnp.where(member, starts[None, :], 0), axis=1)
    end = jnp.sum(jnp.where(member, ends[None, :], 0), axis=1)
    place = jnp.arange(count, dtype=jnp.int32) - start
    keep = 1.0 - jnp.sum(jnp.where(member, skips[None, :], 0), axis=1).astype(F32)
    last = jnp.minimum(start + (place // BLOCK + 1) * BLOCK, end)
    return place, start, last, keep


def unit_scale(values):
    factor = lax.rsqrt(jnp.mean(values * values, axis=1, keepdims=True) + EPSILON)
    return values * factor, factor


def dot(a, b, dims):
    return lax.dot_general(a, b, (dims, ((), ())), preferred_element_type=F32)


def whole(shape):
    return pl.BlockSpec(shape, lambda *_: (0,) * len(shape))


def call(kernel, name, flops, moved, exps=0, **options):
    params = pltpu.CompilerParams(vmem_limit_bytes=VMEM_LIMIT)
    cost = pl.CostEstimate(flops=flops, bytes_accessed=moved, transcendentals=exps)
    return pl.pallas_call(
        kernel, name=name, compiler_params=params, cost_estimate=cost, **options
    )


def by_heads(block, heads):
    return jnp.concatenate([block[:, h * HD : (h + 1) * HD] for h in range(heads)], axis=0)


def store_heads(out_ref, turned, heads, queries):
    for h in range(heads):
        piece = turned[:, h * queries : (h + 1) * queries]
        out_ref[:, h * HD : (h + 1) * HD] = piece.T.astype(out_ref.dtype)


def reach(start, low_ref, high_ref, count):
    spot = start + lax.broadcasted_iota(jnp.int32, (TILE, count), 0)
    return (spot >= low_ref[...]) & (spot < high_ref[...])


def attend_kernel(heads, queries, scale, span, q_ref, kv_ref, low_ref, high_ref,
                  out_ref, turned_ref, log_ref, rows, top, total, running):
    count = heads * queries
    rows[...] = by_heads(q_ref[...], heads)
    top[...] = jnp.full_like(top, FLOOR)
    total[...] = jnp.zeros_like(total)
    running[...] = jnp.zeros_like(running)

    def step(i, _):
        start = pl.multiple_of(i * TILE, TILE)
        keys = kv_ref[pl.ds(start, TILE), :HD]
        values = kv_ref[pl.ds(start, TILE), HD:]
        scores = dot(keys, rows[...], ((1,), (1,))) * (scale * LOG2E)
        scores = jnp.where(reach(start, low_ref, high_ref, count), scores, MASKED)
        higher = jnp.maximum(top[...], jnp.max(scores, axis=0, keepdims=True))
        weights = jnp.exp2(scores - higher)
        fade = jnp.exp2(top[...] - higher)
        total[...] = total[...] * fade + jnp.sum(weights, axis=0, keepdims=True)
        running[...] = running[...] * fade + dot(values, weights.astype(BF16), ((0,), (0,)))
        top[...] = higher
        return 0

    lax.fori_loop(span[0], span[1], step, 0)
    mixed = running[...] / total[...]
    turned_ref[...] = mixed.astype(BF16)
    store_heads(out_ref, mixed, heads, queries)
    log_ref[...] = top[...] + jnp.log2(total[...])


def attend(span, query, key_value, low, high, heads, scale):
    queries = query.shape[0]
    count = heads * queries
    line = whole((1, count))
    return call(
        lambda *refs: attend_kernel(heads, queries, scale, *refs),
        "attend",
        BEHIND * count * key_value.shape[0] * HD,
        2 * key_value.size + 6 * query.size,
        count * key_value.shape[0],
        out_shape=[
            jax.ShapeDtypeStruct(query.shape, BF16),
            jax.ShapeDtypeStruct((HD, count), BF16),
            jax.ShapeDtypeStruct((1, count), F32),
        ],
        grid_spec=pltpu.PrefetchScalarGridSpec(
            num_scalar_prefetch=1,
            grid=(1,),
            in_specs=[whole(query.shape), whole(key_value.shape), line, line],
            out_specs=[whole(query.shape), whole((HD, count)), line],
            scratch_shapes=[
                pltpu.VMEM((count, HD), BF16),
                pltpu.VMEM((1, count), F32),
                pltpu.VMEM((1, count), F32),
                pltpu.VMEM((HD, count), F32),
            ],
        ),
    )(span, query, key_value, low, high)


def attend_back_kernel(heads, queries, scale, span, q_ref, kv_ref, weight_ref, mixed_ref, log_ref,
                       low_ref, high_ref, cos_ref, sin_ref, p0_ref, p1_ref, p2_ref, p3_ref,
                       dq_ref, dkv_ref, branch_ref, rows, grads, delta, turned):
    count = heads * queries
    mine = queries // 4
    for s, piece in enumerate((p0_ref, p1_ref, p2_ref, p3_ref)):
        at = pl.multiple_of(lax.rem(span[2] + 4 - s, 4) * mine, mine)
        branch_ref[pl.ds(at, mine), :] = piece[...]
    mixed_grad = dot(branch_ref[...], weight_ref[...], ((1,), (0,))).astype(BF16).astype(F32)
    for h in range(heads):
        here = slice(h * queries, (h + 1) * queries)
        grads[:, here] = mixed_grad[:, h * HD : (h + 1) * HD].T.astype(BF16)
    delta[...] = jnp.sum(
        grads[...].astype(F32) * mixed_ref[...].astype(F32), axis=0, keepdims=True
    )
    rows[...] = by_heads(q_ref[...], heads)
    turned[...] = jnp.zeros_like(turned)
    dkv_ref[...] = jnp.zeros_like(dkv_ref)

    def step(i, _):
        start = pl.multiple_of(i * TILE, TILE)
        keys = kv_ref[pl.ds(start, TILE), :HD]
        values = kv_ref[pl.ds(start, TILE), HD:]
        scores = dot(keys, rows[...], ((1,), (1,))) * (scale * LOG2E) - log_ref[...]
        scores = jnp.where(reach(start, low_ref, high_ref, count), scores, MASKED)
        probs = jnp.exp2(scores)
        prob_grad = dot(values, grads[...], ((1,), (0,)))
        score_grad = (probs * (prob_grad - delta[...])).astype(BF16)
        key_grad = (dot(score_grad, rows[...], ((1,), (0,))) * scale).astype(BF16)
        value_grad = dot(probs.astype(BF16), grads[...], ((1,), (1,))).astype(BF16)
        for k in range(TILE // queries):
            here = slice(k * queries, (k + 1) * queries)
            dkv_ref[i * (TILE // queries) + k, :, :HD] = key_grad[here]
            dkv_ref[i * (TILE // queries) + k, :, HD:] = value_grad[here]
        turned[...] += dot(keys, score_grad, ((0,), (0,)))
        return 0

    lax.fori_loop(span[0], span[1], step, 0)
    cosine = jnp.concatenate([cos_ref[...] * scale] * heads, axis=1)
    sine = jnp.concatenate([sin_ref[...] * scale] * heads, axis=1)
    first, second = turned[: HD // 2], turned[HD // 2 :]
    back = jnp.concatenate([first * cosine + second * sine, second * cosine - first * sine], axis=0)
    store_heads(dq_ref, back, heads, queries)


def attend_back(span, query, key_value, weight, mixed_turned, log_total, low, high, tables, pieces,
                heads, scale):
    queries = query.shape[0]
    width, wide = weight.shape[0], heads * HD
    count = heads * queries
    line = whole((1, count))
    kv_shape = (key_value.shape[0] // queries, queries, 2 * HD)
    return call(
        lambda *refs: attend_back_kernel(heads, queries, scale, *refs),
        "attend_back",
        AHEAD * count * key_value.shape[0] * HD,
        4 * key_value.size + 6 * query.size + 2 * weight.size,
        count * key_value.shape[0],
        out_shape=[
            jax.ShapeDtypeStruct(query.shape, BF16),
            jax.ShapeDtypeStruct(kv_shape, BF16),
            jax.ShapeDtypeStruct((queries, width), BF16),
        ],
        grid_spec=pltpu.PrefetchScalarGridSpec(
            num_scalar_prefetch=1,
            grid=(1,),
            in_specs=[
                whole(query.shape), whole(key_value.shape),
                whole(weight.shape),
                whole((HD, count)), line, line, line,
                *[whole(p.shape) for p in (*tables, *pieces)],
            ],
            out_specs=[whole(query.shape), whole(kv_shape), whole((queries, width))],
            scratch_shapes=[
                pltpu.VMEM((count, HD), BF16),
                pltpu.VMEM((HD, count), BF16),
                pltpu.VMEM((1, count), F32),
                pltpu.VMEM((HD, count), F32),
            ],
        ),
    )(span, query, key_value, weight, mixed_turned, log_total, low, high, *tables, *pieces)


def hidden_kernel(half, part, step, own_ref, other_ref, grad_own_ref, grad_other_ref, gate_ref,
                  up_ref, down_ref, rows_ref, hid_ref, dgate_ref, dup_ref, back_own_ref,
                  back_other_ref, unit, grad):
    at = pl.program_id(0)
    steps = part // step

    @pl.when(at == 0)
    def _():
        unit[:half] = own_ref[...]
        unit[half:] = other_ref[...]
        grad[:half] = grad_own_ref[...]
        grad[half:] = grad_other_ref[...]

    @pl.when(at < steps)
    def _():
        here = pl.ds(pl.multiple_of(jnp.minimum(at, steps - 1) * step, step), step)
        gate = dot(unit[...], gate_ref[...], ((1,), (0,)))
        up = dot(unit[...], up_ref[...], ((1,), (0,)))
        sigmoid = jax.nn.sigmoid(gate)
        activated = gate * sigmoid
        hid_ref[:, here] = (activated * up).astype(BF16)
        hidden_grad = dot(grad[...], down_ref[...], ((1,), (0,)))
        dgate_ref[:, here] = (
            hidden_grad * up * sigmoid * (1.0 + gate * (1.0 - sigmoid))
        ).astype(BF16)
        dup_ref[:, here] = (hidden_grad * activated).astype(BF16)

    @pl.when(at >= steps)
    def _():
        full = dot(dgate_ref[...], rows_ref[:, :part], ((1,), (1,)))
        full += dot(dup_ref[...], rows_ref[:, part:], ((1,), (1,)))
        back_own_ref[...] = full[:half]
        back_other_ref[...] = full[half:].astype(BF16)


def hidden_units(units, grads, weight, part):
    half, width = units[0].shape
    count = 2 * half
    step, rows = 256, 512
    steps = part // step
    block = lambda which: pl.BlockSpec(
        (width, step), lambda j: (0, which * steps + jnp.minimum(j, steps - 1))
    )
    back = pl.BlockSpec((half, rows), lambda j: (0, jnp.maximum(j - steps, 0)))
    return call(
        lambda *refs: hidden_kernel(half, part, step, *refs),
        "hidden_units",
        10 * count * width * part,
        2 * weight.size + 4 * width * part + 4 * count * width,
        count * part,
        grid=(steps + width // rows,),
        in_specs=[whole((half, width))] * 4
        + [block(0), block(1), block(2)]
        + [pl.BlockSpec((rows, 2 * part), lambda j: (jnp.maximum(j - steps, 0), 0))],
        out_specs=[whole((count, part))] * 3 + [back, back],
        out_shape=[jax.ShapeDtypeStruct((count, part), BF16)] * 3
        + [
            jax.ShapeDtypeStruct((half, width), F32),
            jax.ShapeDtypeStruct((half, width), BF16),
        ],
        scratch_shapes=[pltpu.VMEM((count, width), BF16)] * 2,
    )(*units, *grads, weight, weight, weight, weight)


def weight_grad_kernel(half, part, own_ref, other_ref, grad_own_ref, grad_other_ref, dgate_ref,
                       dup_ref, hid_ref, out_ref):
    unit = jnp.concatenate([own_ref[...], other_ref[...]], axis=0)
    grad = jnp.concatenate([grad_own_ref[...], grad_other_ref[...]], axis=0)
    out_ref[:, :part] = dot(unit, dgate_ref[...], ((0,), (0,))).astype(BF16)
    out_ref[:, part : 2 * part] = dot(unit, dup_ref[...], ((0,), (0,))).astype(BF16)
    out_ref[:, 2 * part :] = dot(grad, hid_ref[...], ((0,), (0,))).astype(BF16)


def weight_grad(units, grads, dgate, dup, hid):
    half, width = units[0].shape
    count, part = hid.shape
    step = 256
    column = pl.BlockSpec((half, step), lambda j: (0, j))
    return call(
        lambda *refs: weight_grad_kernel(half, part, *refs),
        "weight_grad",
        6 * count * width * part,
        6 * width * part + 8 * half * width,
        grid=(width // step,),
        in_specs=[column] * 4 + [whole(dgate.shape), whole(dup.shape), whole(hid.shape)],
        out_specs=pl.BlockSpec((step, 3 * part), lambda j: (j, 0)),
        out_shape=jax.ShapeDtypeStruct((width, 3 * part), BF16),
    )(*units, *grads, dgate, dup, hid)


def both_half_rows(block, core, here_ref, there_ref, columns):
    half = here_ref.shape[1]
    for p in range(here_ref.shape[0]):
        low, high = (block[(2 * p + k) * half : (2 * p + k + 1) * half] for k in (0, 1))
        here_ref[p, :, columns] = jnp.where(core == 0, low, high)
        there_ref[p, :, columns] = jnp.where(core == 0, high, low).astype(BF16)


def wide_grad_kernel(wide, spot, unit_ref, pre_ref, grad_ref, mixed_ref, here_ref, there_ref):
    for k, (a, b) in enumerate(((unit_ref, pre_ref), (grad_ref, mixed_ref))):
        block = dot(a[...], b[...], ((0,), (0,)))
        both_half_rows(block, spot[0], here_ref, there_ref, slice(k * wide, (k + 1) * wide))


def wide_grad(spot, unit, query_pre, branch_grad, mixed, planes):
    queries, width = unit.shape
    wide = mixed.shape[1]
    rows, step = width // (2 * planes), 512
    column = pl.BlockSpec((queries, step), lambda j, *_: (0, j))
    out = pl.BlockSpec((step // (2 * rows), rows, 2 * wide), lambda j, *_: (j, 0, 0))
    return call(
        lambda *refs: wide_grad_kernel(wide, *refs),
        "wide_grad",
        1000 * queries * width * wide,
        2 * (4 * queries * width + 4 * queries * wide),
        grid_spec=pltpu.PrefetchScalarGridSpec(
            num_scalar_prefetch=1,
            grid=(width // step,),
            in_specs=[column, whole(query_pre.shape), column, whole(mixed.shape)],
            out_specs=[out, out],
        ),
        out_shape=[
            jax.ShapeDtypeStruct((planes, rows, 2 * wide), F32),
            jax.ShapeDtypeStruct((planes, rows, 2 * wide), BF16),
        ],
    )(spot, unit, query_pre, branch_grad, mixed)


def input_grad_kernel(spot, got_ref, pre_ref, query_ref, kv_ref, unit_ref, cos_ref, sin_ref,
                      p0_ref, p1_ref, p2_ref, p3_ref, here_ref, there_ref, kv_pre, part):
    mine = p0_ref.shape[0]

    @pl.when(pl.program_id(0) == 0)
    def _():
        total = jnp.sum(got_ref[...].astype(F32), axis=0)
        key = total[:, :HD]
        key = key * cos_ref[...] + pltpu.roll(key, HD // 2, 1) * sin_ref[...]
        kv_pre[:, :HD] = key.astype(BF16)
        kv_pre[:, HD:] = total[:, HD:].astype(BF16)

    part[...] = dot(pre_ref[...], query_ref[...], ((1,), (1,))) + dot(
        kv_pre[...], kv_ref[...], ((1,), (1,))
    )
    for s, piece in enumerate((p0_ref, p1_ref, p2_ref, p3_ref)):
        at = pl.multiple_of(lax.rem(spot[1] + 4 - s, 4) * mine, mine)
        piece[...] = part[pl.ds(at, mine), :].astype(BF16)
    block = dot(unit_ref[...], kv_pre[...], ((0,), (0,)))
    both_half_rows(block, spot[0], here_ref, there_ref, slice(0, 2 * HD))


def input_grad_parts(spot, got, query_pre, weight_query, weight_kv, unit, cosine, sine):
    planes, queries, pair = got.shape
    width, wide = weight_query.shape[0], query_pre.shape[1]
    rows, step, mine = width // (2 * planes), 512, queries // 4
    out = pl.BlockSpec((step // (2 * rows), rows, pair), lambda j, *_: (j, 0, 0))
    piece = pl.BlockSpec((mine, step), lambda j, *_: (0, j))
    return call(
        input_grad_kernel,
        "input_grad",
        100 * queries * width * (wide + 2 * pair),
        2 * (got.size + weight_query.size + weight_kv.size + 2 * unit.size),
        grid_spec=pltpu.PrefetchScalarGridSpec(
            num_scalar_prefetch=1,
            grid=(width // step,),
            in_specs=[
                whole(got.shape),
                whole(query_pre.shape),
                pl.BlockSpec((step, wide), lambda j, *_: (j, 0)),
                pl.BlockSpec((step, pair), lambda j, *_: (j, 0)),
                pl.BlockSpec((queries, step), lambda j, *_: (0, j)),
                whole(cosine.shape),
                whole(sine.shape),
            ],
            out_specs=[piece] * 4 + [out, out],
            scratch_shapes=[pltpu.VMEM((queries, pair), BF16), pltpu.VMEM((queries, step), F32)],
        ),
        out_shape=[jax.ShapeDtypeStruct((mine, width), BF16)] * 4
        + [
            jax.ShapeDtypeStruct((planes, rows, pair), F32),
            jax.ShapeDtypeStruct((planes, rows, pair), BF16),
        ],
    )(spot, got, query_pre, weight_query, weight_kv, unit, cosine, sine)


def spread(piece, xl, core):
    near = flip(piece, "xl")
    both = ordered(xl, piece, near, 0)
    far = flip(both, "c")
    return ordered(core, both[None], far[None], 0), near, far


def over_mp(value):
    turned = [lax.ppermute(value, MP, [(i, (i + s) % 4) for i in range(4)]) for s in (1, 2, 3)]
    return sum(turned, value)


def on_device(
    tokens,
    segment_ids,
    skip_mask,
    norm1_gain,
    w_query,
    w_key,
    w_value,
    w_out,
    norm2_gain,
    w_gate,
    w_up,
    w_down,
    cotangent,
):
    local, width = tokens.shape[1:]
    documents = skip_mask.shape[1]
    xh, xl, core = lax.axis_index("xh"), lax.axis_index("xl"), lax.axis_index("c")
    chip = lax.axis_index(X4)
    plane = lax.axis_index(ZY)
    planes = lax.axis_size(ZY)
    queries = 2 * local
    mine = queries // 4
    every = planes * queries
    offset = plane * queries
    heads = w_query.shape[1] // HD
    wide = heads * HD
    scale = 1.0 / math.sqrt(HD)
    rows = w_query.shape[0]
    hidden_local = w_gate.shape[1]
    part = (hidden_local // 128 + 1) // 2 * 128
    lead = hidden_local - part
    spare = part - lead

    gain_one = norm1_gain.astype(F32)[:, None]
    gain_two = norm2_gain.astype(F32)[:, None]

    with jax.named_scope("attn_weights"):
        scaled = lambda w: (gain_one * w.astype(F32)).astype(BF16)
        own_heads = jnp.concatenate(
            [scaled(w_key), scaled(w_value), scaled(w_query), w_out.T], axis=1
        )
        half_heads = jnp.where(core == xh, own_heads, swap(own_heads))
        at_query, at_out = 2 * HD, 2 * HD + wide
        weight_out = lax.all_gather(half_heads[:, at_out:], ("z", "y", "c"), axis=0, tiled=True)
        half_in = from_everyone(half_heads[:, :at_out], ZY)

        def both_halves(half):
            pair = ordered(core, half[:, None], flip(half, "c")[:, None], 1)
            return pair.reshape(width, half.shape[-1])

        weight_kv = both_halves(half_in[:, :, :at_query])

    with jax.named_scope("first_norm"):
        tokens_own = lax.dynamic_index_in_dim(tokens, core, 0, keepdims=False)
        tokens_got = flip(tokens_own, "xh")
        tokens_all = ordered(xh, tokens_own, tokens_got, 0)
        unit_all = unit_scale(tokens_all.astype(F32))[0].astype(BF16)
        x_mine = lax.dynamic_slice_in_dim(tokens_own, xl * mine, mine).astype(F32)
        first_unit, first_factor = unit_scale(x_mine)

    with jax.named_scope("layout"):
        segment_own = lax.dynamic_index_in_dim(segment_ids, core, 0, keepdims=False)
        skip_own = lax.dynamic_index_in_dim(skip_mask, core, 0, keepdims=False)
        place, start, last, keep = layout(segment_own, skip_own, documents)
        here = lambda a: lax.dynamic_slice_in_dim(a, offset, queries)
        low, high = here(start), here(last)
        span = jnp.stack([low[0] // TILE, (high[-1] + TILE - 1) // TILE, chip])
        low, high = (jnp.tile(a, heads)[None] for a in (low, high))
        keep_here = here(keep).reshape(4, mine, 1)
        keep_mine = lax.dynamic_index_in_dim(keep_here, chip, 0, keepdims=False)
        cos_rows, sin_rows = rope_tables(here(place), 0)
        cosine, sine = cos_rows[:, None, :], sin_rows[:, None, :]

    with jax.named_scope("project"):
        raw = dot(unit_all, weight_kv, ((1,), (0,)))
        key = rotate(raw[:, :HD].reshape(queries, 1, HD), cosine, sine)[:, 0]
        key_value = jnp.concatenate([key, raw[:, HD:]], axis=1).astype(BF16)
        everyone = from_everyone(key_value, ZY).reshape(every, 2 * HD)
        weight_query = both_halves(after(half_in[:, :, at_query:], key_value))
        raw = dot(unit_all, weight_query, ((1,), (0,)))
        query = rotate(raw.reshape(queries, heads, HD), cosine, sine).astype(BF16)
        query = query.reshape(queries, wide)

    with jax.named_scope("ffn_weights"):
        gate_in, up_in, down_in, _ = lax.optimization_barrier((w_gate, w_up, w_down, tokens_got))
        own_hidden = [
            (gain_two * gate_in.astype(F32)).astype(BF16),
            (gain_two * up_in.astype(F32)).astype(BF16),
            down_in.T,
        ]

        def columns(which):
            blank = (which == 1) & (lax.broadcasted_iota(jnp.int32, (rows, part), 1) < spare)
            shares = []
            for w in own_hidden:
                share = jnp.where(which == 0, w[:, :part], w[:, lead:])
                shares.append(jnp.where(blank, jnp.zeros_like(share), share))
            return jnp.concatenate(shares, axis=1)

        pair_rows = ordered(xh, columns(xh), flip(columns(1 - xh), "xh"), 0)
        hidden_weight = lax.all_gather(pair_rows, ZY, axis=0, tiled=True)

    with jax.named_scope("cotangent"):
        grad_local = lax.dynamic_index_in_dim(cotangent, core, 0, keepdims=False)
        upstream = lax.dynamic_slice_in_dim(grad_local, xl * mine, mine).astype(F32)
        grad_all = ordered(xh, grad_local, flip(after(grad_local, key_value), "xh"), 0)
        grad_kept = (keep_here * grad_all.reshape(4, mine, width).astype(F32)).astype(BF16)
        grad_own = jnp.concatenate(behind(grad_kept, chip), axis=0)
        ffn_grads = (grad_own, flip(grad_own, "c"))

    with jax.named_scope("attend"):
        mixed, mixed_turned, log_total = attend(
            span, after(query, ffn_grads[1]), everyone, low, high, heads, scale
        )

    with jax.named_scope("branch"):
        partial = dot(mixed, weight_out, ((1,), (1,))).astype(BF16)
        branch = ring_sum(behind(partial.reshape(4, mine, width), chip))
        middle = x_mine + keep_mine * branch
        second_unit, second_factor = unit_scale(middle)
        unit_own = jnp.concatenate(ring_gather(second_unit.astype(BF16)), axis=0)
        units = (unit_own, flip(unit_own, "c"))

    def both_cores(own_part, other_part):
        return (own_part + flip(other_part, "c").astype(F32)).astype(BF16)

    with jax.named_scope("ffn"):
        hidden, gate_grad, up_grad, own_part, other_part = hidden_units(
            units, ffn_grads, hidden_weight, part
        )
        both = both_cores(own_part, other_part)
        ring_got = ring_parts(list(both.reshape(4, mine, width)))
        scaled_two = sum(a.astype(F32) for a in ring_got)
        down = hidden_weight[:, 2 * part :]
        partial = dot(after(hidden, ring_got[3]), down, ((1,), (1,)))
        result_both = both_cores(partial[:queries], partial[queries:].astype(BF16))
        hidden_weight_grad = weight_grad(
            units, ffn_grads, gate_grad, up_grad, after(hidden, both)
        )
        hidden_owned = lax.psum_scatter(hidden_weight_grad, ZY, scatter_dimension=0, tiled=True)
        middle_grad = upstream + second_factor * (
            scaled_two - second_unit * jnp.mean(scaled_two * second_unit, axis=1, keepdims=True)
        )
        pieces = ring_gather((keep_mine * middle_grad).astype(BF16))

    with jax.named_scope("attend_back"):
        query_pre, kv_grad, branch_grad = attend_back(
            span, query, everyone, weight_out, mixed_turned, log_total, low, high,
            rope_tables(here(place), 1), pieces, heads, scale,
        )
        got = exchange(kv_grad, ZY)
    with jax.named_scope("attend_back"):
        spot = jnp.stack([core, chip])
        turn_back = [jnp.concatenate(t, axis=1) for t in ((cos_rows, cos_rows), (sin_rows, -sin_rows))]
        *input_parts, kv_here, kv_there = input_grad_parts(
            spot, got, query_pre, weight_query, weight_kv, unit_all, *turn_back
        )

    with jax.named_scope("ffn_grads"):
        owned_pair = hidden_owned.reshape(2, rows, 3 * part)
        hidden_kept = jnp.where(xh == 0, owned_pair[0], owned_pair[1])
        hidden_sent = jnp.where(xh == 0, owned_pair[1], owned_pair[0])

    def both_batches(here_half, there_half):
        return (here_half + flip(there_half, "c").astype(F32)).astype(BF16)

    with jax.named_scope("head_grads"):
        wide_half = both_batches(
            *wide_grad(spot, unit_all, query_pre, branch_grad, mixed, planes)
        )
        ring_parts_one = ring_parts(input_parts)
        kv_half = both_batches(kv_here, kv_there)
        wide_got = exchange(after(wide_half, got), ZY)
        kv_got = exchange(after(kv_half, wide_got), ZY)
        result_parts = ring_parts(list(after(result_both, wide_got).reshape(4, mine, width)))
        hidden_sent = flip(hidden_sent, "xh")
        owned = jnp.concatenate([a.astype(F32).sum(axis=0) for a in (after(kv_got, hidden_sent), wide_got)], axis=1)
        kv_owned, wide_owned = owned[:, :at_query], owned[:, at_query:]
        to_owner = lambda a: jnp.where(core == xh, a, swap(a.astype(BF16)).astype(F32))
        owned = to_owner(owned)
        kv_owned, wide_owned = owned[:, :at_query], owned[:, at_query:]
        query_owned, out_owned = wide_owned[:, :wide], wide_owned[:, wide:]
        key_owned, value_owned = kv_owned[:, :HD], kv_owned[:, HD:]
        row_sum = lambda *pairs: sum(
            jnp.sum(g * w.astype(F32), axis=1, keepdims=True) for g, w in pairs
        )
        gain_one_sum = row_sum((query_owned, w_query), (key_owned, w_key), (value_owned, w_value))

    with jax.named_scope("result"):
        feedforward = sum(a.astype(F32) for a in result_parts)
        result = spread(after((middle + keep_mine * feedforward).astype(BF16), kv_got), xl, core)[0]

    with jax.named_scope("input_grad"):
        scaled_one = sum(a.astype(F32) for a in ring_parts_one)
        input_grad = middle_grad + first_factor * (
            scaled_one - first_unit * jnp.mean(scaled_one * first_unit, axis=1, keepdims=True)
        )
        input_grad = spread(input_grad.astype(BF16), xl, core)[0]

    with jax.named_scope("ffn_grads"):
        low_part = pick(True, xh, hidden_kept, hidden_sent).astype(F32)
        high_part = pick(False, xh, hidden_kept, hidden_sent).astype(F32)
        gate_owned, up_owned, down_owned = (
            jnp.concatenate(
                [low_part[:, i * part : (i + 1) * part], high_part[:, i * part + spare : (i + 1) * part]],
                axis=1,
            )
            for i in range(3)
        )
        gain_two_sum = row_sum((gate_owned, w_gate), (up_owned, w_up))
        gain_sums = over_mp(jnp.concatenate([gain_one_sum, gain_two_sum], axis=1))

    return (
        result,
        input_grad,
        gain_sums[:, 0],
        gain_one * query_owned,
        gain_one * key_owned,
        gain_one * value_owned,
        out_owned.T,
        gain_sums[:, 1],
        gain_two * gate_owned,
        gain_two * up_owned,
        down_owned.T,
    )


def solution(mesh):
    split = Mesh(mesh.devices.reshape(4, 4, 2, 2, 2), AXES)
    token = P(None, DP, None)
    by_row = P(DP, MP)
    by_column = P(MP, DP)
    in_specs = (
        token, P(), P(), P(DP), by_row, by_row, by_row, by_column,
        P(DP), by_row, by_row, by_column, token,
    )
    out_specs = (
        token, token, P(DP), by_row, by_row, by_row, by_column,
        P(DP), by_row, by_row, by_column,
    )
    return jax.shard_map(
        on_device, mesh=split, in_specs=in_specs, out_specs=out_specs, check_vma=False
    )
```

```python
import math

import jax
import jax.numpy as jnp
from jax import lax
from jax.experimental import pallas as pl
from jax.experimental.pallas import tpu as pltpu
from jax.sharding import Mesh
from jax.sharding import PartitionSpec as P

HD = 128
BLOCK = 256
EPSILON = 1e-05
MASKED = -1e30
FLOOR = -1e29
LOG2E = 1.4426950408889634
TILE = 1024
VMEM_LIMIT = 56 * 1024 * 1024

AXES = ("z", "y", "xh", "xl", "c")
DP = ("z", "y", "xh")
MP = ("xl", "c")
ZY = ("z", "y")
X4 = ("xh", "xl")
F32 = jnp.float32
BF16 = jnp.bfloat16


def after(value, *others):
    return lax.optimization_barrier((value, *others))[0]


def exchange(value, axes):
    return lax.all_to_all(value, axes, split_axis=0, concat_axis=0, tiled=True)


def from_everyone(value, axes):
    return exchange(jnp.broadcast_to(value, (lax.axis_size(axes), *value.shape)), axes)


def flip(value, axis):
    return lax.ppermute(value, axis, [(0, 1), (1, 0)])


def swap(value):
    return lax.ppermute(value, ("xh", "c"), [(1, 2), (2, 1)])


def turn(value, step):
    return lax.ppermute(value, X4, [(i, (i + step) % 4) for i in range(4)])


def ring_gather(block):
    far = turn(block, 2)
    return [block, turn(block, 1), far, turn(block, 3)]


def ring_sum(pieces):
    far = turn(pieces[2], -2)
    near = [turn(pieces[s], -s) for s in (1, 3)]
    return sum((a.astype(F32) for a in (*near, far)), pieces[0].astype(F32))


def behind(blocks, chip):
    return [lax.dynamic_index_in_dim(blocks, (chip - s) % 4, 0, keepdims=False) for s in range(4)]


def pick(first, when, own, other):
    return jnp.where(when == 0, own, other) if first else jnp.where(when == 0, other, own)


def ordered(when, own, other, axis):
    return jnp.concatenate([pick(True, when, own, other), pick(False, when, own, other)], axis=axis)


def rope_tables(place):
    half = HD // 2
    rates = jnp.exp(jnp.arange(half, dtype=F32) * (-2.0 * math.log(10000.0) / HD))
    angles = place.astype(F32)[:, None] * rates[None, :]
    return jnp.cos(angles)[:, None, :], jnp.sin(angles)[:, None, :]


def rotate(values, cosine, sine):
    half = HD // 2
    first, second = values[..., :half], values[..., half:]
    return jnp.concatenate(
        [first * cosine - second * sine, second * cosine + first * sine], axis=-1
    )


def layout(segments, skips, documents):
    count = segments.shape[0]
    labels = jnp.arange(documents, dtype=jnp.int32)
    member = segments[:, None] == labels[None, :]
    starts = jnp.sum((segments[:, None] < labels[None, :]).astype(jnp.int32), axis=0)
    ends = jnp.sum((segments[:, None] <= labels[None, :]).astype(jnp.int32), axis=0)
    start = jnp.sum(jnp.where(member, starts[None, :], 0), axis=1)
    end = jnp.sum(jnp.where(member, ends[None, :], 0), axis=1)
    place = jnp.arange(count, dtype=jnp.int32) - start
    keep = 1.0 - jnp.sum(jnp.where(member, skips[None, :], 0), axis=1).astype(F32)
    last = jnp.minimum(start + (place // BLOCK + 1) * BLOCK, end)
    return place, start, last, keep


def unit_scale(values):
    factor = lax.rsqrt(jnp.mean(values * values, axis=1, keepdims=True) + EPSILON)
    return values * factor, factor


def dot(a, b, dims):
    return lax.dot_general(a, b, (dims, ((), ())), preferred_element_type=F32)


def whole(shape):
    return pl.BlockSpec(shape, lambda *_: (0,) * len(shape))


def call(kernel, name, flops, moved, exps=0, **options):
    params = pltpu.CompilerParams(vmem_limit_bytes=VMEM_LIMIT)
    cost = pl.CostEstimate(flops=flops, bytes_accessed=moved, transcendentals=exps)
    return pl.pallas_call(
        kernel, name=name, compiler_params=params, cost_estimate=cost, **options
    )


def by_heads(block, heads):
    return jnp.concatenate([block[:, h * HD : (h + 1) * HD] for h in range(heads)], axis=0)


def store_heads(out_ref, turned, heads, queries):
    for h in range(heads):
        piece = turned[:, h * queries : (h + 1) * queries]
        out_ref[:, h * HD : (h + 1) * HD] = piece.T.astype(out_ref.dtype)


def reach(start, low_ref, high_ref, count):
    spot = start + lax.broadcasted_iota(jnp.int32, (TILE, count), 0)
    return (spot >= low_ref[...]) & (spot < high_ref[...])


def attend_kernel(heads, queries, scale, span, q_ref, kv_ref, low_ref, high_ref,
                  out_ref, turned_ref, log_ref, rows, top, total, running):
    count = heads * queries
    rows[...] = by_heads(q_ref[...], heads)
    top[...] = jnp.full_like(top, FLOOR)
    total[...] = jnp.zeros_like(total)
    running[...] = jnp.zeros_like(running)

    def step(i, _):
        start = pl.multiple_of(i * TILE, TILE)
        keys = kv_ref[pl.ds(start, TILE), :HD]
        values = kv_ref[pl.ds(start, TILE), HD:]
        scores = dot(keys, rows[...], ((1,), (1,))) * (scale * LOG2E)
        scores = jnp.where(reach(start, low_ref, high_ref, count), scores, MASKED)
        higher = jnp.maximum(top[...], jnp.max(scores, axis=0, keepdims=True))
        weights = jnp.exp2(scores - higher)
        fade = jnp.exp2(top[...] - higher)
        total[...] = total[...] * fade + jnp.sum(weights, axis=0, keepdims=True)
        running[...] = running[...] * fade + dot(values, weights.astype(BF16), ((0,), (0,)))
        top[...] = higher
        return 0

    lax.fori_loop(span[0], span[1], step, 0)
    mixed = running[...] / total[...]
    turned_ref[...] = mixed.astype(BF16)
    store_heads(out_ref, mixed, heads, queries)
    log_ref[...] = top[...] + jnp.log2(total[...])


def attend(span, query, key_value, low, high, heads, scale):
    queries = query.shape[0]
    count = heads * queries
    line = whole((1, count))
    return call(
        lambda *refs: attend_kernel(heads, queries, scale, *refs),
        "attend",
        4 * count * key_value.shape[0] * HD,
        2 * key_value.size + 6 * query.size,
        count * key_value.shape[0],
        out_shape=[
            jax.ShapeDtypeStruct(query.shape, BF16),
            jax.ShapeDtypeStruct((HD, count), BF16),
            jax.ShapeDtypeStruct((1, count), F32),
        ],
        grid_spec=pltpu.PrefetchScalarGridSpec(
            num_scalar_prefetch=1,
            grid=(1,),
            in_specs=[whole(query.shape), whole(key_value.shape), line, line],
            out_specs=[whole(query.shape), whole((HD, count)), line],
            scratch_shapes=[
                pltpu.VMEM((count, HD), BF16),
                pltpu.VMEM((1, count), F32),
                pltpu.VMEM((1, count), F32),
                pltpu.VMEM((HD, count), F32),
            ],
        ),
    )(span, query, key_value, low, high)


def attend_back_kernel(heads, queries, scale, span, q_ref, kv_ref, weight_ref, mixed_ref, log_ref,
                       low_ref, high_ref, p0_ref, p1_ref, p2_ref, p3_ref,
                       dq_ref, dkv_ref, branch_ref, rows, grads, delta, turned):
    count = heads * queries
    mine = queries // 4
    for s, piece in enumerate((p0_ref, p1_ref, p2_ref, p3_ref)):
        at = pl.multiple_of(lax.rem(span[2] + 4 - s, 4) * mine, mine)
        branch_ref[pl.ds(at, mine), :] = piece[...]
    mixed_grad = dot(branch_ref[...], weight_ref[...], ((1,), (0,))).astype(BF16).astype(F32)
    for h in range(heads):
        here = slice(h * queries, (h + 1) * queries)
        grads[:, here] = mixed_grad[:, h * HD : (h + 1) * HD].T.astype(BF16)
    delta[...] = jnp.sum(
        grads[...].astype(F32) * mixed_ref[...].astype(F32), axis=0, keepdims=True
    )
    rows[...] = by_heads(q_ref[...], heads)
    turned[...] = jnp.zeros_like(turned)
    dkv_ref[...] = jnp.zeros_like(dkv_ref)

    def step(i, _):
        start = pl.multiple_of(i * TILE, TILE)
        keys = kv_ref[pl.ds(start, TILE), :HD]
        values = kv_ref[pl.ds(start, TILE), HD:]
        scores = dot(keys, rows[...], ((1,), (1,))) * (scale * LOG2E) - log_ref[...]
        scores = jnp.where(reach(start, low_ref, high_ref, count), scores, MASKED)
        probs = jnp.exp2(scores)
        prob_grad = dot(values, grads[...], ((1,), (0,)))
        score_grad = (probs * (prob_grad - delta[...])).astype(BF16)
        dkv_ref[pl.ds(start, TILE), :HD] = (
            dot(score_grad, rows[...], ((1,), (0,))) * scale
        ).astype(BF16)
        dkv_ref[pl.ds(start, TILE), HD:] = dot(
            probs.astype(BF16), grads[...], ((1,), (1,))
        ).astype(BF16)
        turned[...] += dot(keys, score_grad, ((0,), (0,)))
        return 0

    lax.fori_loop(span[0], span[1], step, 0)
    store_heads(dq_ref, turned[...] * scale, heads, queries)


def attend_back(span, query, key_value, weight, mixed_turned, log_total, low, high, pieces,
                heads, scale):
    queries = query.shape[0]
    width = weight.shape[0]
    count = heads * queries
    line = whole((1, count))
    return call(
        lambda *refs: attend_back_kernel(heads, queries, scale, *refs),
        "attend_back",
        100 * count * key_value.shape[0] * HD,
        4 * key_value.size + 6 * query.size + 2 * weight.size,
        count * key_value.shape[0],
        out_shape=[
            jax.ShapeDtypeStruct(query.shape, F32),
            jax.ShapeDtypeStruct(key_value.shape, BF16),
            jax.ShapeDtypeStruct((queries, width), BF16),
        ],
        grid_spec=pltpu.PrefetchScalarGridSpec(
            num_scalar_prefetch=1,
            grid=(1,),
            in_specs=[
                whole(query.shape), whole(key_value.shape), whole(weight.shape),
                whole((HD, count)), line, line, line, *[whole(p.shape) for p in pieces],
            ],
            out_specs=[whole(query.shape), whole(key_value.shape), whole((queries, width))],
            scratch_shapes=[
                pltpu.VMEM((count, HD), BF16),
                pltpu.VMEM((HD, count), BF16),
                pltpu.VMEM((1, count), F32),
                pltpu.VMEM((HD, count), F32),
            ],
        ),
    )(span, query, key_value, weight, mixed_turned, log_total, low, high, *pieces)


def hidden_kernel(half, part, step, own_ref, other_ref, grad_own_ref, grad_other_ref, gate_ref,
                  up_ref, down_ref, rows_ref, hid_ref, dgate_ref, dup_ref, back_own_ref,
                  back_other_ref, unit, grad):
    at = pl.program_id(0)
    steps = part // step

    @pl.when(at == 0)
    def _():
        unit[:half] = own_ref[...]
        unit[half:] = other_ref[...]
        grad[:half] = grad_own_ref[...]
        grad[half:] = grad_other_ref[...]

    @pl.when(at < steps)
    def _():
        here = pl.ds(pl.multiple_of(jnp.minimum(at, steps - 1) * step, step), step)
        gate = dot(unit[...], gate_ref[...], ((1,), (0,)))
        up = dot(unit[...], up_ref[...], ((1,), (0,)))
        sigmoid = jax.nn.sigmoid(gate)
        activated = gate * sigmoid
        hid_ref[:, here] = (activated * up).astype(BF16)
        hidden_grad = dot(grad[...], down_ref[...], ((1,), (0,)))
        dgate_ref[:, here] = (
            hidden_grad * up * sigmoid * (1.0 + gate * (1.0 - sigmoid))
        ).astype(BF16)
        dup_ref[:, here] = (hidden_grad * activated).astype(BF16)

    @pl.when(at >= steps)
    def _():
        full = dot(dgate_ref[...], rows_ref[:, :part], ((1,), (1,)))
        full += dot(dup_ref[...], rows_ref[:, part:], ((1,), (1,)))
        back_own_ref[...] = full[:half]
        back_other_ref[...] = full[half:].astype(BF16)


def hidden_units(units, grads, weight, part):
    half, width = units[0].shape
    count = 2 * half
    step, rows = 256, 512
    steps = part // step
    block = lambda which: pl.BlockSpec(
        (width, step), lambda j: (0, which * steps + jnp.minimum(j, steps - 1))
    )
    back = pl.BlockSpec((half, rows), lambda j: (0, jnp.maximum(j - steps, 0)))
    return call(
        lambda *refs: hidden_kernel(half, part, step, *refs),
        "hidden_units",
        10 * count * width * part,
        2 * weight.size + 4 * width * part + 4 * count * width,
        count * part,
        grid=(steps + width // rows,),
        in_specs=[whole((half, width))] * 4
        + [block(0), block(1), block(2)]
        + [pl.BlockSpec((rows, 2 * part), lambda j: (jnp.maximum(j - steps, 0), 0))],
        out_specs=[whole((count, part))] * 3 + [back, back],
        out_shape=[jax.ShapeDtypeStruct((count, part), BF16)] * 3
        + [
            jax.ShapeDtypeStruct((half, width), F32),
            jax.ShapeDtypeStruct((half, width), BF16),
        ],
        scratch_shapes=[pltpu.VMEM((count, width), BF16)] * 2,
    )(*units, *grads, weight, weight, weight, weight)


def weight_grad_kernel(half, part, own_ref, other_ref, grad_own_ref, grad_other_ref, dgate_ref,
                       dup_ref, hid_ref, out_ref):
    unit = jnp.concatenate([own_ref[...], other_ref[...]], axis=0)
    grad = jnp.concatenate([grad_own_ref[...], grad_other_ref[...]], axis=0)
    out_ref[:, :part] = dot(unit, dgate_ref[...], ((0,), (0,))).astype(BF16)
    out_ref[:, part : 2 * part] = dot(unit, dup_ref[...], ((0,), (0,))).astype(BF16)
    out_ref[:, 2 * part :] = dot(grad, hid_ref[...], ((0,), (0,))).astype(BF16)


def weight_grad(units, grads, dgate, dup, hid):
    half, width = units[0].shape
    count, part = hid.shape
    step = 256
    column = pl.BlockSpec((half, step), lambda j: (0, j))
    return call(
        lambda *refs: weight_grad_kernel(half, part, *refs),
        "weight_grad",
        6 * count * width * part,
        6 * width * part + 8 * half * width,
        grid=(width // step,),
        in_specs=[column] * 4 + [whole(dgate.shape), whole(dup.shape), whole(hid.shape)],
        out_specs=pl.BlockSpec((step, 3 * part), lambda j: (j, 0)),
        out_shape=jax.ShapeDtypeStruct((width, 3 * part), BF16),
    )(*units, *grads, dgate, dup, hid)


def spread(piece, xl, core):
    both = ordered(xl, piece, flip(piece, "xl"), 0)
    return ordered(core, both[None], flip(both, "c")[None], 0)


def over_mp(value):
    turned = [lax.ppermute(value, MP, [(i, (i + s) % 4) for i in range(4)]) for s in (1, 2, 3)]
    return sum(turned, value)


def on_device(
    tokens,
    segment_ids,
    skip_mask,
    norm1_gain,
    w_query,
    w_key,
    w_value,
    w_out,
    norm2_gain,
    w_gate,
    w_up,
    w_down,
    cotangent,
):
    local, width = tokens.shape[1:]
    documents = skip_mask.shape[1]
    xh, xl, core = lax.axis_index("xh"), lax.axis_index("xl"), lax.axis_index("c")
    chip = lax.axis_index(X4)
    plane = lax.axis_index(ZY)
    planes = lax.axis_size(ZY)
    queries = 2 * local
    mine = queries // 4
    every = planes * queries
    offset = plane * queries
    heads = w_query.shape[1] // HD
    wide = heads * HD
    scale = 1.0 / math.sqrt(HD)
    rows = w_query.shape[0]
    hidden_local = w_gate.shape[1]
    part = (hidden_local // 128 + 1) // 2 * 128
    lead = hidden_local - part
    spare = part - lead

    gain_one = norm1_gain.astype(F32)[:, None]
    gain_two = norm2_gain.astype(F32)[:, None]

    with jax.named_scope("attn_weights"):
        scaled = lambda w: (gain_one * w.astype(F32)).astype(BF16)
        own_heads = jnp.concatenate(
            [scaled(w_key), scaled(w_value), scaled(w_query), w_out.T], axis=1
        )
        half_heads = jnp.where(core == xh, own_heads, swap(own_heads))
        at_query, at_out = 2 * HD, 2 * HD + wide
        wide_weight = lax.all_gather(half_heads[:, at_query:], ("z", "y", "c"), axis=0, tiled=True)
        half_kv = from_everyone(half_heads[:, :at_query], ZY)
        pair_kv = ordered(core, half_kv[:, None], flip(half_kv, "c")[:, None], 1)
        weight_kv = pair_kv.reshape(width, at_query)

    with jax.named_scope("first_norm"):
        tokens_own = lax.dynamic_index_in_dim(tokens, core, 0, keepdims=False)
        tokens_all = ordered(xh, tokens_own, flip(tokens_own, "xh"), 0)
        unit_all = unit_scale(tokens_all.astype(F32))[0].astype(BF16)
        x_mine = lax.dynamic_slice_in_dim(tokens_own, xl * mine, mine).astype(F32)
        first_unit, first_factor = unit_scale(x_mine)

    with jax.named_scope("layout"):
        segment_own = lax.dynamic_index_in_dim(segment_ids, core, 0, keepdims=False)
        skip_own = lax.dynamic_index_in_dim(skip_mask, core, 0, keepdims=False)
        place, start, last, keep = layout(segment_own, skip_own, documents)
        here = lambda a: lax.dynamic_slice_in_dim(a, offset, queries)
        low, high = here(start), here(last)
        span = jnp.stack([low[0] // TILE, (high[-1] + TILE - 1) // TILE, chip])
        low, high = (jnp.tile(a, heads)[None] for a in (low, high))
        keep_here = here(keep).reshape(4, mine, 1)
        keep_mine = lax.dynamic_index_in_dim(keep_here, chip, 0, keepdims=False)
        cosine, sine = rope_tables(here(place))

    with jax.named_scope("project"):
        raw = dot(unit_all, weight_kv, ((1,), (0,)))
        key = rotate(raw[:, :HD].reshape(queries, 1, HD), cosine, sine)[:, 0]
        key_value = jnp.concatenate([key, raw[:, HD:]], axis=1).astype(BF16)
        everyone = from_everyone(key_value, ZY).reshape(every, 2 * HD)
        weight_query, weight_out = wide_weight[:, :wide], wide_weight[:, wide:]
        raw = dot(unit_all, weight_query, ((1,), (0,)))
        query = rotate(raw.reshape(queries, heads, HD), cosine, sine).astype(BF16)
        query = query.reshape(queries, wide)

    with jax.named_scope("ffn_weights"):
        own_hidden = [
            (gain_two * w_gate.astype(F32)).astype(BF16),
            (gain_two * w_up.astype(F32)).astype(BF16),
            w_down.T,
        ]

        def columns(which):
            blank = (which == 1) & (lax.broadcasted_iota(jnp.int32, (rows, part), 1) < spare)
            shares = []
            for w in own_hidden:
                share = jnp.where(which == 0, w[:, :part], w[:, lead:])
                shares.append(jnp.where(blank, jnp.zeros_like(share), share))
            return jnp.concatenate(shares, axis=1)

        pair_rows = ordered(xh, columns(xh), flip(after(columns(1 - xh), weight_kv), "xh"), 0)
        hidden_weight = lax.all_gather(after(pair_rows, key_value), ZY, axis=0, tiled=True)

    with jax.named_scope("cotangent"):
        grad_local = lax.dynamic_index_in_dim(cotangent, core, 0, keepdims=False)
        upstream = lax.dynamic_slice_in_dim(grad_local, xl * mine, mine).astype(F32)
        grad_all = ordered(xh, grad_local, flip(after(grad_local, key_value), "xh"), 0)
        grad_kept = (keep_here * grad_all.reshape(4, mine, width).astype(F32)).astype(BF16)
        grad_own = jnp.concatenate(behind(grad_kept, chip), axis=0)
        ffn_grads = (grad_own, flip(grad_own, "c"))

    with jax.named_scope("attend"):
        mixed, mixed_turned, log_total = attend(
            span, after(query, ffn_grads[1]), everyone, low, high, heads, scale
        )

    with jax.named_scope("branch"):
        partial = dot(mixed, weight_out, ((1,), (1,))).astype(BF16)
        branch = ring_sum(behind(partial.reshape(4, mine, width), chip))
        middle = x_mine + keep_mine * branch
        second_unit, second_factor = unit_scale(middle)
        unit_own = jnp.concatenate(ring_gather(second_unit.astype(BF16)), axis=0)
        units = (unit_own, flip(unit_own, "c"))

    def own_sum(own_part, other_part):
        both = (own_part + flip(other_part, "c").astype(F32)).astype(BF16)
        return both, ring_sum(list(both.reshape(4, mine, width)))

    with jax.named_scope("ffn"):
        hidden, gate_grad, up_grad, own_part, other_part = hidden_units(
            units, ffn_grads, hidden_weight, part
        )
        both, scaled_two = own_sum(own_part, other_part)
        hidden_weight_grad = weight_grad(
            units, ffn_grads, gate_grad, up_grad, after(hidden, both)
        )
        hidden_owned = lax.psum_scatter(hidden_weight_grad, ZY, scatter_dimension=0, tiled=True)
        middle_grad = upstream + second_factor * (
            scaled_two - second_unit * jnp.mean(scaled_two * second_unit, axis=1, keepdims=True)
        )
        pieces = ring_gather((keep_mine * middle_grad).astype(BF16))

    with jax.named_scope("attend_back"):
        query_grad, kv_grad, branch_grad = attend_back(
            span, query, everyone, weight_out, mixed_turned, log_total, low, high, pieces,
            heads, scale,
        )
        owned = exchange(kv_grad.reshape(planes, queries, 2 * HD), ZY)
        owned = owned.astype(F32).sum(axis=0)
        query_pre = rotate(query_grad.reshape(queries, heads, HD), cosine, -sine)
        query_pre = query_pre.astype(BF16).reshape(queries, wide)
        key_pre = rotate(owned[:, None, :HD], cosine, -sine)[:, 0].astype(BF16)
        kv_pre = jnp.concatenate([key_pre, owned[:, HD:].astype(BF16)], axis=1)

    with jax.named_scope("ffn_grads"):
        owned_pair = hidden_owned.reshape(2, rows, 3 * part)
        kept = jnp.where(xh == 0, owned_pair[0], owned_pair[1])
        sent = flip(jnp.where(xh == 0, owned_pair[1], owned_pair[0]), "xh")

    def owned_half(grad):
        pair = grad.reshape(planes, 2, rows, grad.shape[-1])
        here_half = jnp.where(core == 0, pair[:, 0], pair[:, 1])
        there_half = jnp.where(core == 0, pair[:, 1], pair[:, 0])
        return (here_half + flip(there_half.astype(BF16), "c").astype(F32)).astype(BF16)

    def over_planes(half):
        return exchange(half, ZY).astype(F32).sum(axis=0)

    with jax.named_scope("head_grads"):
        query_half = owned_half(dot(unit_all, query_pre, ((0,), (0,))))
        out_half = owned_half(dot(branch_grad, mixed, ((0,), (0,))))
        wide_half = jnp.concatenate([query_half, out_half], axis=2)
        wide_owned = over_planes(after(wide_half, owned))
        kv_half = owned_half(dot(unit_all, kv_pre, ((0,), (0,))))
        kv_got = exchange(after(kv_half, wide_owned), ZY)
        kv_owned = after(kv_got, sent).astype(F32).sum(axis=0)
        summed = jnp.concatenate([kv_owned, wide_owned], axis=1)
        heads_owned = jnp.where(core == xh, summed, swap(summed.astype(BF16)).astype(F32))
        query_owned = heads_owned[:, at_query:at_out]
        key_owned, value_owned = heads_owned[:, :HD], heads_owned[:, HD:at_query]
        row_sum = lambda *pairs: sum(
            jnp.sum(g * w.astype(F32), axis=1, keepdims=True) for g, w in pairs
        )
        gain_one_sum = row_sum((query_owned, w_query), (key_owned, w_key), (value_owned, w_value))

    with jax.named_scope("result"):
        down = hidden_weight[:, 2 * part :]
        partial = dot(after(hidden, kv_grad), down, ((1,), (1,)))
        feedforward = own_sum(partial[:queries], partial[queries:].astype(BF16))[1]
        result = spread((middle + keep_mine * feedforward).astype(BF16), xl, core)

    with jax.named_scope("input_grad"):
        partial = dot(query_pre, weight_query, ((1,), (1,))) + dot(kv_pre, weight_kv, ((1,), (1,)))
        scaled_one = ring_sum(behind(partial.astype(BF16).reshape(4, mine, width), chip))
        input_grad = middle_grad + first_factor * (
            scaled_one - first_unit * jnp.mean(scaled_one * first_unit, axis=1, keepdims=True)
        )
        input_grad = spread(after(input_grad.astype(BF16), sent), xl, core)

    with jax.named_scope("ffn_grads"):
        low_part = pick(True, xh, kept, sent).astype(F32)
        high_part = pick(False, xh, kept, sent).astype(F32)
        gate_owned, up_owned, down_owned = (
            jnp.concatenate(
                [low_part[:, i * part : (i + 1) * part], high_part[:, i * part + spare : (i + 1) * part]],
                axis=1,
            )
            for i in range(3)
        )
        gain_two_sum = row_sum((gate_owned, w_gate), (up_owned, w_up))

    with jax.named_scope("gain_grads"):
        gain_grads = over_mp(jnp.concatenate([gain_one_sum, gain_two_sum], axis=1))

    return (
        result,
        input_grad,
        gain_grads[:, 0],
        gain_one * query_owned,
        gain_one * key_owned,
        gain_one * value_owned,
        heads_owned[:, at_out:].T,
        gain_grads[:, 1],
        gain_two * gate_owned,
        gain_two * up_owned,
        down_owned.T,
    )


def solution(mesh):
    split = Mesh(mesh.devices.reshape(4, 4, 2, 2, 2), AXES)
    token = P(None, DP, None)
    by_row = P(DP, MP)
    by_column = P(MP, DP)
    in_specs = (
        token, P(), P(), P(DP), by_row, by_row, by_row, by_column,
        P(DP), by_row, by_row, by_column, token,
    )
    out_specs = (
        token, token, P(DP), by_row, by_row, by_row, by_column,
        P(DP), by_row, by_row, by_column,
    )
    return jax.shard_map(
        on_device, mesh=split, in_specs=in_specs, out_specs=out_specs, check_vma=False
    )
```

```python
import math

import jax
import jax.numpy as jnp
from jax import lax
from jax.experimental import pallas as pl
from jax.experimental.pallas import tpu as pltpu
from jax.sharding import Mesh
from jax.sharding import PartitionSpec as P

HD = 128
BLOCK = 256
EPSILON = 1e-05
MASKED = -1e30
FLOOR = -1e29
LOG2E = 1.4426950408889634
TILE = 512
VMEM_LIMIT = 56 * 1024 * 1024

AXES = ("z", "y", "xh", "xl", "c")
DP = ("z", "y", "xh")
MP = ("xl", "c")
ZY = ("z", "y")
X4 = ("xh", "xl")
F32 = jnp.float32
BF16 = jnp.bfloat16


def after(value, *others):
    return lax.optimization_barrier((value, *others))[0]


def exchange(value, axes):
    return lax.all_to_all(value, axes, split_axis=0, concat_axis=0, tiled=True)


def from_everyone(value, axes):
    return exchange(jnp.broadcast_to(value, (lax.axis_size(axes), *value.shape)), axes)


def flip(value, axis):
    return lax.ppermute(value, axis, [(0, 1), (1, 0)])


def swap(value):
    return lax.ppermute(value, ("xh", "c"), [(1, 2), (2, 1)])


def turn(value, step):
    return lax.ppermute(value, X4, [(i, (i + step) % 4) for i in range(4)])


def ring_gather(block):
    far = turn(block, 2)
    return [block, turn(block, 1), far, turn(block, 3)]


def ring_parts(pieces):
    far = turn(pieces[2], -2)
    return [pieces[0], *(turn(pieces[s], -s) for s in (1, 3)), far]


def ring_sum(pieces):
    return sum(a.astype(F32) for a in ring_parts(pieces))


def behind(blocks, chip):
    return [lax.dynamic_index_in_dim(blocks, (chip - s) % 4, 0, keepdims=False) for s in range(4)]


def pick(first, when, own, other):
    return jnp.where(when == 0, own, other) if first else jnp.where(when == 0, other, own)


def ordered(when, own, other, axis):
    return jnp.concatenate([pick(True, when, own, other), pick(False, when, own, other)], axis=axis)


def rope_tables(place):
    half = HD // 2
    rates = jnp.exp(jnp.arange(half, dtype=F32) * (-2.0 * math.log(10000.0) / HD))
    angles = place.astype(F32)[:, None] * rates[None, :]
    return jnp.cos(angles)[:, None, :], jnp.sin(angles)[:, None, :]


def rotate(values, cosine, sine):
    half = HD // 2
    first, second = values[..., :half], values[..., half:]
    return jnp.concatenate(
        [first * cosine - second * sine, second * cosine + first * sine], axis=-1
    )


def layout(segments, skips, documents):
    count = segments.shape[0]
    labels = jnp.arange(documents, dtype=jnp.int32)
    member = segments[:, None] == labels[None, :]
    starts = jnp.sum((segments[:, None] < labels[None, :]).astype(jnp.int32), axis=0)
    ends = jnp.sum((segments[:, None] <= labels[None, :]).astype(jnp.int32), axis=0)
    start = jnp.sum(jnp.where(member, starts[None, :], 0), axis=1)
    end = jnp.sum(jnp.where(member, ends[None, :], 0), axis=1)
    place = jnp.arange(count, dtype=jnp.int32) - start
    keep = 1.0 - jnp.sum(jnp.where(member, skips[None, :], 0), axis=1).astype(F32)
    last = jnp.minimum(start + (place // BLOCK + 1) * BLOCK, end)
    return place, start, last, keep


def unit_scale(values):
    factor = lax.rsqrt(jnp.mean(values * values, axis=1, keepdims=True) + EPSILON)
    return values * factor, factor


def dot(a, b, dims):
    return lax.dot_general(a, b, (dims, ((), ())), preferred_element_type=F32)


def whole(shape):
    return pl.BlockSpec(shape, lambda *_: (0,) * len(shape))


def call(kernel, name, flops, moved, exps=0, **options):
    params = pltpu.CompilerParams(vmem_limit_bytes=VMEM_LIMIT)
    cost = pl.CostEstimate(flops=flops, bytes_accessed=moved, transcendentals=exps)
    return pl.pallas_call(
        kernel, name=name, compiler_params=params, cost_estimate=cost, **options
    )


def by_heads(block, heads):
    return jnp.concatenate([block[:, h * HD : (h + 1) * HD] for h in range(heads)], axis=0)


def store_heads(out_ref, turned, heads, queries):
    for h in range(heads):
        piece = turned[:, h * queries : (h + 1) * queries]
        out_ref[:, h * HD : (h + 1) * HD] = piece.T.astype(out_ref.dtype)


def reach(start, low_ref, high_ref, count):
    spot = start + lax.broadcasted_iota(jnp.int32, (TILE, count), 0)
    return (spot >= low_ref[...]) & (spot < high_ref[...])


def attend_kernel(heads, queries, scale, span, q_ref, kv_ref, low_ref, high_ref,
                  out_ref, turned_ref, log_ref, rows, top, total, running):
    count = heads * queries
    rows[...] = by_heads(q_ref[...], heads)
    top[...] = jnp.full_like(top, FLOOR)
    total[...] = jnp.zeros_like(total)
    running[...] = jnp.zeros_like(running)

    def step(i, _):
        start = pl.multiple_of(i * TILE, TILE)
        keys = kv_ref[pl.ds(start, TILE), :HD]
        values = kv_ref[pl.ds(start, TILE), HD:]
        scores = dot(keys, rows[...], ((1,), (1,))) * (scale * LOG2E)
        scores = jnp.where(reach(start, low_ref, high_ref, count), scores, MASKED)
        higher = jnp.maximum(top[...], jnp.max(scores, axis=0, keepdims=True))
        weights = jnp.exp2(scores - higher)
        fade = jnp.exp2(top[...] - higher)
        total[...] = total[...] * fade + jnp.sum(weights, axis=0, keepdims=True)
        running[...] = running[...] * fade + dot(values, weights.astype(BF16), ((0,), (0,)))
        top[...] = higher
        return 0

    lax.fori_loop(span[0], span[1], step, 0)
    mixed = running[...] / total[...]
    turned_ref[...] = mixed.astype(BF16)
    store_heads(out_ref, mixed, heads, queries)
    log_ref[...] = top[...] + jnp.log2(total[...])


def attend(span, query, key_value, low, high, heads, scale):
    queries = query.shape[0]
    count = heads * queries
    line = whole((1, count))
    return call(
        lambda *refs: attend_kernel(heads, queries, scale, *refs),
        "attend",
        4 * count * key_value.shape[0] * HD,
        2 * key_value.size + 6 * query.size,
        count * key_value.shape[0],
        out_shape=[
            jax.ShapeDtypeStruct(query.shape, BF16),
            jax.ShapeDtypeStruct((HD, count), BF16),
            jax.ShapeDtypeStruct((1, count), F32),
        ],
        grid_spec=pltpu.PrefetchScalarGridSpec(
            num_scalar_prefetch=1,
            grid=(1,),
            in_specs=[whole(query.shape), whole(key_value.shape), line, line],
            out_specs=[whole(query.shape), whole((HD, count)), line],
            scratch_shapes=[
                pltpu.VMEM((count, HD), BF16),
                pltpu.VMEM((1, count), F32),
                pltpu.VMEM((1, count), F32),
                pltpu.VMEM((HD, count), F32),
            ],
        ),
    )(span, query, key_value, low, high)


def attend_back_kernel(heads, queries, scale, span, q_ref, kv_ref, weight_ref, mixed_ref, log_ref,
                       low_ref, high_ref, p0_ref, p1_ref, p2_ref, p3_ref,
                       dq_ref, dkv_ref, branch_ref, rows, grads, delta, turned):
    count = heads * queries
    mine = queries // 4
    for s, piece in enumerate((p0_ref, p1_ref, p2_ref, p3_ref)):
        at = pl.multiple_of(lax.rem(span[2] + 4 - s, 4) * mine, mine)
        branch_ref[pl.ds(at, mine), :] = piece[...]
    mixed_grad = dot(branch_ref[...], weight_ref[...], ((1,), (0,))).astype(BF16).astype(F32)
    for h in range(heads):
        here = slice(h * queries, (h + 1) * queries)
        grads[:, here] = mixed_grad[:, h * HD : (h + 1) * HD].T.astype(BF16)
    delta[...] = jnp.sum(
        grads[...].astype(F32) * mixed_ref[...].astype(F32), axis=0, keepdims=True
    )
    rows[...] = by_heads(q_ref[...], heads)
    turned[...] = jnp.zeros_like(turned)
    dkv_ref[...] = jnp.zeros_like(dkv_ref)

    def step(i, _):
        start = pl.multiple_of(i * TILE, TILE)
        keys = kv_ref[pl.ds(start, TILE), :HD]
        values = kv_ref[pl.ds(start, TILE), HD:]
        scores = dot(keys, rows[...], ((1,), (1,))) * (scale * LOG2E) - log_ref[...]
        scores = jnp.where(reach(start, low_ref, high_ref, count), scores, MASKED)
        probs = jnp.exp2(scores)
        prob_grad = dot(values, grads[...], ((1,), (0,)))
        score_grad = (probs * (prob_grad - delta[...])).astype(BF16)
        key_grad = (dot(score_grad, rows[...], ((1,), (0,))) * scale).astype(BF16)
        value_grad = dot(probs.astype(BF16), grads[...], ((1,), (1,))).astype(BF16)
        for k in range(TILE // queries):
            here = slice(k * queries, (k + 1) * queries)
            dkv_ref[i * (TILE // queries) + k, :, :HD] = key_grad[here]
            dkv_ref[i * (TILE // queries) + k, :, HD:] = value_grad[here]
        turned[...] += dot(keys, score_grad, ((0,), (0,)))
        return 0

    lax.fori_loop(span[0], span[1], step, 0)
    store_heads(dq_ref, turned[...] * scale, heads, queries)


def attend_back(span, query, key_value, weight, mixed_turned, log_total, low, high, pieces,
                heads, scale):
    queries = query.shape[0]
    width = weight.shape[0]
    count = heads * queries
    line = whole((1, count))
    kv_shape = (key_value.shape[0] // queries, queries, 2 * HD)
    return call(
        lambda *refs: attend_back_kernel(heads, queries, scale, *refs),
        "attend_back",
        100 * count * key_value.shape[0] * HD,
        4 * key_value.size + 6 * query.size + 2 * weight.size,
        count * key_value.shape[0],
        out_shape=[
            jax.ShapeDtypeStruct(query.shape, F32),
            jax.ShapeDtypeStruct(kv_shape, BF16),
            jax.ShapeDtypeStruct((queries, width), BF16),
        ],
        grid_spec=pltpu.PrefetchScalarGridSpec(
            num_scalar_prefetch=1,
            grid=(1,),
            in_specs=[
                whole(query.shape), whole(key_value.shape), whole(weight.shape),
                whole((HD, count)), line, line, line, *[whole(p.shape) for p in pieces],
            ],
            out_specs=[whole(query.shape), whole(kv_shape), whole((queries, width))],
            scratch_shapes=[
                pltpu.VMEM((count, HD), BF16),
                pltpu.VMEM((HD, count), BF16),
                pltpu.VMEM((1, count), F32),
                pltpu.VMEM((HD, count), F32),
            ],
        ),
    )(span, query, key_value, weight, mixed_turned, log_total, low, high, *pieces)


def hidden_kernel(half, part, step, own_ref, other_ref, grad_own_ref, grad_other_ref, gate_ref,
                  up_ref, down_ref, rows_ref, hid_ref, dgate_ref, dup_ref, back_own_ref,
                  back_other_ref, unit, grad):
    at = pl.program_id(0)
    steps = part // step

    @pl.when(at == 0)
    def _():
        unit[:half] = own_ref[...]
        unit[half:] = other_ref[...]
        grad[:half] = grad_own_ref[...]
        grad[half:] = grad_other_ref[...]

    @pl.when(at < steps)
    def _():
        here = pl.ds(pl.multiple_of(jnp.minimum(at, steps - 1) * step, step), step)
        gate = dot(unit[...], gate_ref[...], ((1,), (0,)))
        up = dot(unit[...], up_ref[...], ((1,), (0,)))
        sigmoid = jax.nn.sigmoid(gate)
        activated = gate * sigmoid
        hid_ref[:, here] = (activated * up).astype(BF16)
        hidden_grad = dot(grad[...], down_ref[...], ((1,), (0,)))
        dgate_ref[:, here] = (
            hidden_grad * up * sigmoid * (1.0 + gate * (1.0 - sigmoid))
        ).astype(BF16)
        dup_ref[:, here] = (hidden_grad * activated).astype(BF16)

    @pl.when(at >= steps)
    def _():
        full = dot(dgate_ref[...], rows_ref[:, :part], ((1,), (1,)))
        full += dot(dup_ref[...], rows_ref[:, part:], ((1,), (1,)))
        back_own_ref[...] = full[:half]
        back_other_ref[...] = full[half:].astype(BF16)


def hidden_units(units, grads, weight, part):
    half, width = units[0].shape
    count = 2 * half
    step, rows = 256, 512
    steps = part // step
    block = lambda which: pl.BlockSpec(
        (width, step), lambda j: (0, which * steps + jnp.minimum(j, steps - 1))
    )
    back = pl.BlockSpec((half, rows), lambda j: (0, jnp.maximum(j - steps, 0)))
    return call(
        lambda *refs: hidden_kernel(half, part, step, *refs),
        "hidden_units",
        10 * count * width * part,
        2 * weight.size + 4 * width * part + 4 * count * width,
        count * part,
        grid=(steps + width // rows,),
        in_specs=[whole((half, width))] * 4
        + [block(0), block(1), block(2)]
        + [pl.BlockSpec((rows, 2 * part), lambda j: (jnp.maximum(j - steps, 0), 0))],
        out_specs=[whole((count, part))] * 3 + [back, back],
        out_shape=[jax.ShapeDtypeStruct((count, part), BF16)] * 3
        + [
            jax.ShapeDtypeStruct((half, width), F32),
            jax.ShapeDtypeStruct((half, width), BF16),
        ],
        scratch_shapes=[pltpu.VMEM((count, width), BF16)] * 2,
    )(*units, *grads, weight, weight, weight, weight)


def weight_grad_kernel(half, part, own_ref, other_ref, grad_own_ref, grad_other_ref, dgate_ref,
                       dup_ref, hid_ref, out_ref):
    unit = jnp.concatenate([own_ref[...], other_ref[...]], axis=0)
    grad = jnp.concatenate([grad_own_ref[...], grad_other_ref[...]], axis=0)
    out_ref[:, :part] = dot(unit, dgate_ref[...], ((0,), (0,))).astype(BF16)
    out_ref[:, part : 2 * part] = dot(unit, dup_ref[...], ((0,), (0,))).astype(BF16)
    out_ref[:, 2 * part :] = dot(grad, hid_ref[...], ((0,), (0,))).astype(BF16)


def weight_grad(units, grads, dgate, dup, hid):
    half, width = units[0].shape
    count, part = hid.shape
    step = 256
    column = pl.BlockSpec((half, step), lambda j: (0, j))
    return call(
        lambda *refs: weight_grad_kernel(half, part, *refs),
        "weight_grad",
        6 * count * width * part,
        6 * width * part + 8 * half * width,
        grid=(width // step,),
        in_specs=[column] * 4 + [whole(dgate.shape), whole(dup.shape), whole(hid.shape)],
        out_specs=pl.BlockSpec((step, 3 * part), lambda j: (j, 0)),
        out_shape=jax.ShapeDtypeStruct((width, 3 * part), BF16),
    )(*units, *grads, dgate, dup, hid)


def both_half_rows(block, core, here_ref, there_ref, columns):
    half = here_ref.shape[1]
    for p in range(here_ref.shape[0]):
        low, high = (block[(2 * p + k) * half : (2 * p + k + 1) * half] for k in (0, 1))
        here_ref[p, :, columns] = jnp.where(core == 0, low, high)
        there_ref[p, :, columns] = jnp.where(core == 0, high, low).astype(BF16)


def input_grad_kernel(spot, got_ref, pre_ref, query_ref, kv_ref, unit_ref, cos_ref, sin_ref,
                      p0_ref, p1_ref, p2_ref, p3_ref, here_ref, there_ref, kv_pre, part):
    mine = p0_ref.shape[0]

    @pl.when(pl.program_id(0) == 0)
    def _():
        total = jnp.sum(got_ref[...].astype(F32), axis=0)
        key = total[:, :HD]
        key = key * cos_ref[...] + pltpu.roll(key, HD // 2, 1) * sin_ref[...]
        kv_pre[:, :HD] = key.astype(BF16)
        kv_pre[:, HD:] = total[:, HD:].astype(BF16)

    part[...] = dot(pre_ref[...], query_ref[...], ((1,), (1,))) + dot(
        kv_pre[...], kv_ref[...], ((1,), (1,))
    )
    for s, piece in enumerate((p0_ref, p1_ref, p2_ref, p3_ref)):
        at = pl.multiple_of(lax.rem(spot[1] + 4 - s, 4) * mine, mine)
        piece[...] = part[pl.ds(at, mine), :].astype(BF16)
    block = dot(unit_ref[...], kv_pre[...], ((0,), (0,)))
    both_half_rows(block, spot[0], here_ref, there_ref, slice(0, 2 * HD))


def input_grad_parts(spot, got, query_pre, weight_query, weight_kv, unit, cosine, sine):
    planes, queries, pair = got.shape
    width, wide = weight_query.shape[0], query_pre.shape[1]
    rows, step, mine = width // (2 * planes), 512, queries // 4
    out = pl.BlockSpec((step // (2 * rows), rows, pair), lambda j, *_: (j, 0, 0))
    piece = pl.BlockSpec((mine, step), lambda j, *_: (0, j))
    return call(
        input_grad_kernel,
        "input_grad",
        140 * queries * width * (wide + 2 * pair),
        2 * (got.size + weight_query.size + weight_kv.size + 2 * unit.size),
        grid_spec=pltpu.PrefetchScalarGridSpec(
            num_scalar_prefetch=1,
            grid=(width // step,),
            in_specs=[
                whole(got.shape),
                whole(query_pre.shape),
                pl.BlockSpec((step, wide), lambda j, *_: (j, 0)),
                pl.BlockSpec((step, pair), lambda j, *_: (j, 0)),
                pl.BlockSpec((queries, step), lambda j, *_: (0, j)),
                whole(cosine.shape),
                whole(sine.shape),
            ],
            out_specs=[piece] * 4 + [out, out],
            scratch_shapes=[pltpu.VMEM((queries, pair), BF16), pltpu.VMEM((queries, step), F32)],
        ),
        out_shape=[jax.ShapeDtypeStruct((mine, width), BF16)] * 4
        + [
            jax.ShapeDtypeStruct((planes, rows, pair), F32),
            jax.ShapeDtypeStruct((planes, rows, pair), BF16),
        ],
    )(spot, got, query_pre, weight_query, weight_kv, unit, cosine, sine)


def spread(piece, xl, core):
    both = ordered(xl, piece, flip(piece, "xl"), 0)
    return ordered(core, both[None], flip(both, "c")[None], 0)


def over_mp(value):
    turned = [lax.ppermute(value, MP, [(i, (i + s) % 4) for i in range(4)]) for s in (1, 2, 3)]
    return sum(turned, value)


def on_device(
    tokens,
    segment_ids,
    skip_mask,
    norm1_gain,
    w_query,
    w_key,
    w_value,
    w_out,
    norm2_gain,
    w_gate,
    w_up,
    w_down,
    cotangent,
):
    local, width = tokens.shape[1:]
    documents = skip_mask.shape[1]
    xh, xl, core = lax.axis_index("xh"), lax.axis_index("xl"), lax.axis_index("c")
    chip = lax.axis_index(X4)
    plane = lax.axis_index(ZY)
    planes = lax.axis_size(ZY)
    queries = 2 * local
    mine = queries // 4
    every = planes * queries
    offset = plane * queries
    heads = w_query.shape[1] // HD
    wide = heads * HD
    scale = 1.0 / math.sqrt(HD)
    rows = w_query.shape[0]
    hidden_local = w_gate.shape[1]
    part = (hidden_local // 128 + 1) // 2 * 128
    lead = hidden_local - part
    spare = part - lead

    gain_one = norm1_gain.astype(F32)[:, None]
    gain_two = norm2_gain.astype(F32)[:, None]

    with jax.named_scope("attn_weights"):
        scaled = lambda w: (gain_one * w.astype(F32)).astype(BF16)
        own_heads = jnp.concatenate(
            [scaled(w_key), scaled(w_value), scaled(w_query), w_out.T], axis=1
        )
        half_heads = jnp.where(core == xh, own_heads, swap(own_heads))
        at_query, at_out = 2 * HD, 2 * HD + wide
        wide_weight = lax.all_gather(half_heads[:, at_query:], ("z", "y", "c"), axis=0, tiled=True)
        half_kv = from_everyone(half_heads[:, :at_query], ZY)
        pair_kv = ordered(core, half_kv[:, None], flip(half_kv, "c")[:, None], 1)
        weight_kv = pair_kv.reshape(width, at_query)

    with jax.named_scope("first_norm"):
        tokens_own = lax.dynamic_index_in_dim(tokens, core, 0, keepdims=False)
        tokens_all = ordered(xh, tokens_own, flip(tokens_own, "xh"), 0)
        unit_all = unit_scale(tokens_all.astype(F32))[0].astype(BF16)
        x_mine = lax.dynamic_slice_in_dim(tokens_own, xl * mine, mine).astype(F32)
        first_unit, first_factor = unit_scale(x_mine)

    with jax.named_scope("layout"):
        segment_own = lax.dynamic_index_in_dim(segment_ids, core, 0, keepdims=False)
        skip_own = lax.dynamic_index_in_dim(skip_mask, core, 0, keepdims=False)
        place, start, last, keep = layout(segment_own, skip_own, documents)
        here = lambda a: lax.dynamic_slice_in_dim(a, offset, queries)
        low, high = here(start), here(last)
        span = jnp.stack([low[0] // TILE, (high[-1] + TILE - 1) // TILE, chip])
        low, high = (jnp.tile(a, heads)[None] for a in (low, high))
        keep_here = here(keep).reshape(4, mine, 1)
        keep_mine = lax.dynamic_index_in_dim(keep_here, chip, 0, keepdims=False)
        cosine, sine = rope_tables(here(place))

    with jax.named_scope("project"):
        raw = dot(unit_all, weight_kv, ((1,), (0,)))
        key = rotate(raw[:, :HD].reshape(queries, 1, HD), cosine, sine)[:, 0]
        key_value = jnp.concatenate([key, raw[:, HD:]], axis=1).astype(BF16)
        everyone = from_everyone(key_value, ZY).reshape(every, 2 * HD)
        weight_query, weight_out = wide_weight[:, :wide], wide_weight[:, wide:]
        raw = dot(unit_all, weight_query, ((1,), (0,)))
        query = rotate(raw.reshape(queries, heads, HD), cosine, sine).astype(BF16)
        query = query.reshape(queries, wide)

    with jax.named_scope("ffn_weights"):
        own_hidden = [
            (gain_two * w_gate.astype(F32)).astype(BF16),
            (gain_two * w_up.astype(F32)).astype(BF16),
            w_down.T,
        ]

        def columns(which):
            blank = (which == 1) & (lax.broadcasted_iota(jnp.int32, (rows, part), 1) < spare)
            shares = []
            for w in own_hidden:
                share = jnp.where(which == 0, w[:, :part], w[:, lead:])
                shares.append(jnp.where(blank, jnp.zeros_like(share), share))
            return jnp.concatenate(shares, axis=1)

        pair_rows = ordered(xh, columns(xh), flip(after(columns(1 - xh), weight_kv), "xh"), 0)
        hidden_weight = lax.all_gather(after(pair_rows, key_value), ZY, axis=0, tiled=True)

    with jax.named_scope("cotangent"):
        grad_local = lax.dynamic_index_in_dim(cotangent, core, 0, keepdims=False)
        upstream = lax.dynamic_slice_in_dim(grad_local, xl * mine, mine).astype(F32)
        grad_all = ordered(xh, grad_local, flip(after(grad_local, key_value), "xh"), 0)
        grad_kept = (keep_here * grad_all.reshape(4, mine, width).astype(F32)).astype(BF16)
        grad_own = jnp.concatenate(behind(grad_kept, chip), axis=0)
        ffn_grads = (grad_own, flip(grad_own, "c"))

    with jax.named_scope("attend"):
        mixed, mixed_turned, log_total = attend(
            span, after(query, ffn_grads[1]), everyone, low, high, heads, scale
        )

    with jax.named_scope("branch"):
        partial = dot(mixed, weight_out, ((1,), (1,))).astype(BF16)
        branch = ring_sum(behind(partial.reshape(4, mine, width), chip))
        middle = x_mine + keep_mine * branch
        second_unit, second_factor = unit_scale(middle)
        unit_own = jnp.concatenate(ring_gather(second_unit.astype(BF16)), axis=0)
        units = (unit_own, flip(unit_own, "c"))

    def own_sum(own_part, other_part):
        both = (own_part + flip(other_part, "c").astype(F32)).astype(BF16)
        return both, ring_sum(list(both.reshape(4, mine, width)))

    with jax.named_scope("ffn"):
        hidden, gate_grad, up_grad, own_part, other_part = hidden_units(
            units, ffn_grads, hidden_weight, part
        )
        both, scaled_two = own_sum(own_part, other_part)
        hidden_weight_grad = weight_grad(
            units, ffn_grads, gate_grad, up_grad, after(hidden, both)
        )
        hidden_owned = lax.psum_scatter(hidden_weight_grad, ZY, scatter_dimension=0, tiled=True)
        middle_grad = upstream + second_factor * (
            scaled_two - second_unit * jnp.mean(scaled_two * second_unit, axis=1, keepdims=True)
        )
        pieces = ring_gather((keep_mine * middle_grad).astype(BF16))

    with jax.named_scope("attend_back"):
        query_grad, kv_grad, branch_grad = attend_back(
            span, query, everyone, weight_out, mixed_turned, log_total, low, high, pieces,
            heads, scale,
        )
        owned = exchange(kv_grad, ZY)
        query_pre = rotate(query_grad.reshape(queries, heads, HD), cosine, -sine)
        query_pre = query_pre.astype(BF16).reshape(queries, wide)
        cos_rows, sin_rows = cosine[:, 0], sine[:, 0]
        turn_back = [jnp.concatenate(t, axis=1) for t in ((cos_rows, cos_rows), (sin_rows, -sin_rows))]
        *input_parts, kv_here, kv_there = input_grad_parts(
            jnp.stack([core, chip]), owned, query_pre, wide_weight, weight_kv, unit_all, *turn_back
        )

    with jax.named_scope("ffn_grads"):
        owned_pair = hidden_owned.reshape(2, rows, 3 * part)
        kept = jnp.where(xh == 0, owned_pair[0], owned_pair[1])
        sent = flip(jnp.where(xh == 0, owned_pair[1], owned_pair[0]), "xh")

    def owned_half(grad):
        pair = grad.reshape(planes, 2, rows, grad.shape[-1])
        here_half = jnp.where(core == 0, pair[:, 0], pair[:, 1])
        there_half = jnp.where(core == 0, pair[:, 1], pair[:, 0])
        return (here_half + flip(there_half.astype(BF16), "c").astype(F32)).astype(BF16)

    def over_planes(half):
        return exchange(half, ZY).astype(F32).sum(axis=0)

    with jax.named_scope("head_grads"):
        query_half = owned_half(dot(unit_all, query_pre, ((0,), (0,))))
        out_half = owned_half(dot(branch_grad, mixed, ((0,), (0,))))
        wide_half = jnp.concatenate([query_half, out_half], axis=2)
        wide_got = exchange(after(wide_half, owned), ZY)
        wide_owned = wide_got.astype(F32).sum(axis=0)
        kv_half = (kv_here + flip(kv_there, "c").astype(F32)).astype(BF16)
        kv_got = exchange(after(kv_half, wide_got, sent), ZY)
        kv_owned = kv_got.astype(F32).sum(axis=0)
        summed = jnp.concatenate([kv_owned, wide_owned], axis=1)
        heads_owned = jnp.where(core == xh, summed, swap(summed.astype(BF16)).astype(F32))
        query_owned = heads_owned[:, at_query:at_out]
        key_owned, value_owned = heads_owned[:, :HD], heads_owned[:, HD:at_query]
        row_sum = lambda *pairs: sum(
            jnp.sum(g * w.astype(F32), axis=1, keepdims=True) for g, w in pairs
        )
        gain_one_sum = row_sum((query_owned, w_query), (key_owned, w_key), (value_owned, w_value))

    with jax.named_scope("result"):
        down = hidden_weight[:, 2 * part :]
        partial = dot(after(hidden, kv_grad), down, ((1,), (1,)))
        feedforward = own_sum(partial[:queries], partial[queries:].astype(BF16))[1]
        result = spread((middle + keep_mine * feedforward).astype(BF16), xl, core)

    with jax.named_scope("input_grad"):
        late_parts = lax.optimization_barrier((*input_parts, wide_got))[:-1]
        late_parts = ring_parts(list(late_parts))
        late_parts = lax.optimization_barrier((*late_parts, kv_got))[:-1]
        scaled_one = sum(a.astype(F32) for a in late_parts)
        input_grad = middle_grad + first_factor * (
            scaled_one - first_unit * jnp.mean(scaled_one * first_unit, axis=1, keepdims=True)
        )
        input_grad = spread(input_grad.astype(BF16), xl, core)

    with jax.named_scope("ffn_grads"):
        low_part = pick(True, xh, kept, sent).astype(F32)
        high_part = pick(False, xh, kept, sent).astype(F32)
        gate_owned, up_owned, down_owned = (
            jnp.concatenate(
                [low_part[:, i * part : (i + 1) * part], high_part[:, i * part + spare : (i + 1) * part]],
                axis=1,
            )
            for i in range(3)
        )
        gain_two_sum = row_sum((gate_owned, w_gate), (up_owned, w_up))

    with jax.named_scope("gain_grads"):
        gain_grads = over_mp(jnp.concatenate([gain_one_sum, gain_two_sum], axis=1))

    return (
        result,
        input_grad,
        gain_grads[:, 0],
        gain_one * query_owned,
        gain_one * key_owned,
        gain_one * value_owned,
        heads_owned[:, at_out:].T,
        gain_grads[:, 1],
        gain_two * gate_owned,
        gain_two * up_owned,
        down_owned.T,
    )


def solution(mesh):
    split = Mesh(mesh.devices.reshape(4, 4, 2, 2, 2), AXES)
    token = P(None, DP, None)
    by_row = P(DP, MP)
    by_column = P(MP, DP)
    in_specs = (
        token, P(), P(), P(DP), by_row, by_row, by_row, by_column,
        P(DP), by_row, by_row, by_column, token,
    )
    out_specs = (
        token, token, P(DP), by_row, by_row, by_row, by_column,
        P(DP), by_row, by_row, by_column,
    )
    return jax.shard_map(
        on_device, mesh=split, in_specs=in_specs, out_specs=out_specs, check_vma=False
    )
```

```python
import math

import jax
import jax.numpy as jnp
from jax import lax
from jax.experimental import pallas as pl
from jax.experimental.pallas import tpu as pltpu
from jax.sharding import Mesh
from jax.sharding import PartitionSpec as P

HD = 128
BLOCK = 256
EPSILON = 1e-05
MASKED = -1e30
FLOOR = -1e29
LOG2E = 1.4426950408889634
TILE = 512
VMEM_LIMIT = 56 * 1024 * 1024

AXES = ("z", "y", "xh", "xl", "c")
DP = ("z", "y", "xh")
MP = ("xl", "c")
ZY = ("z", "y")
X4 = ("xh", "xl")
F32 = jnp.float32
BF16 = jnp.bfloat16


def after(value, *others):
    return lax.optimization_barrier((value, *others))[0]


def exchange(value, axes):
    return lax.all_to_all(value, axes, split_axis=0, concat_axis=0, tiled=True)


def from_everyone(value, axes):
    return exchange(jnp.broadcast_to(value, (lax.axis_size(axes), *value.shape)), axes)


def flip(value, axis):
    return lax.ppermute(value, axis, [(0, 1), (1, 0)])


def swap(value):
    return lax.ppermute(value, ("xh", "c"), [(1, 2), (2, 1)])


def turn(value, step):
    return lax.ppermute(value, X4, [(i, (i + step) % 4) for i in range(4)])


def ring_gather(block):
    far = turn(block, 2)
    return [block, turn(block, 1), far, turn(block, 3)]


def ring_parts(pieces):
    far = turn(pieces[2], -2)
    return [pieces[0], *(turn(pieces[s], -s) for s in (1, 3)), far]


def ring_sum(pieces):
    return sum(a.astype(F32) for a in ring_parts(pieces))


def behind(blocks, chip):
    return [lax.dynamic_index_in_dim(blocks, (chip - s) % 4, 0, keepdims=False) for s in range(4)]


def pick(first, when, own, other):
    return jnp.where(when == 0, own, other) if first else jnp.where(when == 0, other, own)


def ordered(when, own, other, axis):
    return jnp.concatenate([pick(True, when, own, other), pick(False, when, own, other)], axis=axis)


def rope_tables(place):
    half = HD // 2
    rates = jnp.exp(jnp.arange(half, dtype=F32) * (-2.0 * math.log(10000.0) / HD))
    angles = place.astype(F32)[:, None] * rates[None, :]
    return jnp.cos(angles)[:, None, :], jnp.sin(angles)[:, None, :]


def rotate(values, cosine, sine):
    half = HD // 2
    first, second = values[..., :half], values[..., half:]
    return jnp.concatenate(
        [first * cosine - second * sine, second * cosine + first * sine], axis=-1
    )


def layout(segments, skips, documents):
    count = segments.shape[0]
    labels = jnp.arange(documents, dtype=jnp.int32)
    member = segments[:, None] == labels[None, :]
    starts = jnp.sum((segments[:, None] < labels[None, :]).astype(jnp.int32), axis=0)
    ends = jnp.sum((segments[:, None] <= labels[None, :]).astype(jnp.int32), axis=0)
    start = jnp.sum(jnp.where(member, starts[None, :], 0), axis=1)
    end = jnp.sum(jnp.where(member, ends[None, :], 0), axis=1)
    place = jnp.arange(count, dtype=jnp.int32) - start
    keep = 1.0 - jnp.sum(jnp.where(member, skips[None, :], 0), axis=1).astype(F32)
    last = jnp.minimum(start + (place // BLOCK + 1) * BLOCK, end)
    return place, start, last, keep


def unit_scale(values):
    factor = lax.rsqrt(jnp.mean(values * values, axis=1, keepdims=True) + EPSILON)
    return values * factor, factor


def dot(a, b, dims):
    return lax.dot_general(a, b, (dims, ((), ())), preferred_element_type=F32)


def whole(shape):
    return pl.BlockSpec(shape, lambda *_: (0,) * len(shape))


def call(kernel, name, flops, moved, exps=0, **options):
    params = pltpu.CompilerParams(vmem_limit_bytes=VMEM_LIMIT)
    cost = pl.CostEstimate(flops=flops, bytes_accessed=moved, transcendentals=exps)
    return pl.pallas_call(
        kernel, name=name, compiler_params=params, cost_estimate=cost, **options
    )


def by_heads(block, heads):
    return jnp.concatenate([block[:, h * HD : (h + 1) * HD] for h in range(heads)], axis=0)


def store_heads(out_ref, turned, heads, queries):
    for h in range(heads):
        piece = turned[:, h * queries : (h + 1) * queries]
        out_ref[:, h * HD : (h + 1) * HD] = piece.T.astype(out_ref.dtype)


def reach(start, low_ref, high_ref, count):
    spot = start + lax.broadcasted_iota(jnp.int32, (TILE, count), 0)
    return (spot >= low_ref[...]) & (spot < high_ref[...])


def attend_kernel(heads, queries, scale, span, q_ref, kv_ref, low_ref, high_ref,
                  out_ref, turned_ref, log_ref, rows, top, total, running):
    count = heads * queries
    rows[...] = by_heads(q_ref[...], heads)
    top[...] = jnp.full_like(top, FLOOR)
    total[...] = jnp.zeros_like(total)
    running[...] = jnp.zeros_like(running)

    def step(i, _):
        start = pl.multiple_of(i * TILE, TILE)
        keys = kv_ref[pl.ds(start, TILE), :HD]
        values = kv_ref[pl.ds(start, TILE), HD:]
        scores = dot(keys, rows[...], ((1,), (1,))) * (scale * LOG2E)
        scores = jnp.where(reach(start, low_ref, high_ref, count), scores, MASKED)
        higher = jnp.maximum(top[...], jnp.max(scores, axis=0, keepdims=True))
        weights = jnp.exp2(scores - higher)
        fade = jnp.exp2(top[...] - higher)
        total[...] = total[...] * fade + jnp.sum(weights, axis=0, keepdims=True)
        running[...] = running[...] * fade + dot(values, weights.astype(BF16), ((0,), (0,)))
        top[...] = higher
        return 0

    lax.fori_loop(span[0], span[1], step, 0)
    mixed = running[...] / total[...]
    turned_ref[...] = mixed.astype(BF16)
    store_heads(out_ref, mixed, heads, queries)
    log_ref[...] = top[...] + jnp.log2(total[...])


def attend(span, query, key_value, low, high, heads, scale):
    queries = query.shape[0]
    count = heads * queries
    line = whole((1, count))
    return call(
        lambda *refs: attend_kernel(heads, queries, scale, *refs),
        "attend",
        4 * count * key_value.shape[0] * HD,
        2 * key_value.size + 6 * query.size,
        count * key_value.shape[0],
        out_shape=[
            jax.ShapeDtypeStruct(query.shape, BF16),
            jax.ShapeDtypeStruct((HD, count), BF16),
            jax.ShapeDtypeStruct((1, count), F32),
        ],
        grid_spec=pltpu.PrefetchScalarGridSpec(
            num_scalar_prefetch=1,
            grid=(1,),
            in_specs=[whole(query.shape), whole(key_value.shape), line, line],
            out_specs=[whole(query.shape), whole((HD, count)), line],
            scratch_shapes=[
                pltpu.VMEM((count, HD), BF16),
                pltpu.VMEM((1, count), F32),
                pltpu.VMEM((1, count), F32),
                pltpu.VMEM((HD, count), F32),
            ],
        ),
    )(span, query, key_value, low, high)


def attend_back_kernel(heads, queries, scale, span, q_ref, kv_ref, weight_ref, mixed_ref, log_ref,
                       low_ref, high_ref, p0_ref, p1_ref, p2_ref, p3_ref,
                       dq_ref, dkv_ref, branch_ref, rows, grads, delta, turned):
    count = heads * queries
    mine = queries // 4
    for s, piece in enumerate((p0_ref, p1_ref, p2_ref, p3_ref)):
        at = pl.multiple_of(lax.rem(span[2] + 4 - s, 4) * mine, mine)
        branch_ref[pl.ds(at, mine), :] = piece[...]
    mixed_grad = dot(branch_ref[...], weight_ref[...], ((1,), (0,))).astype(BF16).astype(F32)
    for h in range(heads):
        here = slice(h * queries, (h + 1) * queries)
        grads[:, here] = mixed_grad[:, h * HD : (h + 1) * HD].T.astype(BF16)
    delta[...] = jnp.sum(
        grads[...].astype(F32) * mixed_ref[...].astype(F32), axis=0, keepdims=True
    )
    rows[...] = by_heads(q_ref[...], heads)
    turned[...] = jnp.zeros_like(turned)
    dkv_ref[...] = jnp.zeros_like(dkv_ref)

    def step(i, _):
        start = pl.multiple_of(i * TILE, TILE)
        keys = kv_ref[pl.ds(start, TILE), :HD]
        values = kv_ref[pl.ds(start, TILE), HD:]
        scores = dot(keys, rows[...], ((1,), (1,))) * (scale * LOG2E) - log_ref[...]
        scores = jnp.where(reach(start, low_ref, high_ref, count), scores, MASKED)
        probs = jnp.exp2(scores)
        prob_grad = dot(values, grads[...], ((1,), (0,)))
        score_grad = (probs * (prob_grad - delta[...])).astype(BF16)
        key_grad = (dot(score_grad, rows[...], ((1,), (0,))) * scale).astype(BF16)
        value_grad = dot(probs.astype(BF16), grads[...], ((1,), (1,))).astype(BF16)
        for k in range(TILE // queries):
            here = slice(k * queries, (k + 1) * queries)
            dkv_ref[i * (TILE // queries) + k, :, :HD] = key_grad[here]
            dkv_ref[i * (TILE // queries) + k, :, HD:] = value_grad[here]
        turned[...] += dot(keys, score_grad, ((0,), (0,)))
        return 0

    lax.fori_loop(span[0], span[1], step, 0)
    store_heads(dq_ref, turned[...] * scale, heads, queries)


def attend_back(span, query, key_value, weight, mixed_turned, log_total, low, high, pieces,
                heads, scale):
    queries = query.shape[0]
    width = weight.shape[0]
    count = heads * queries
    line = whole((1, count))
    kv_shape = (key_value.shape[0] // queries, queries, 2 * HD)
    return call(
        lambda *refs: attend_back_kernel(heads, queries, scale, *refs),
        "attend_back",
        100 * count * key_value.shape[0] * HD,
        4 * key_value.size + 6 * query.size + 2 * weight.size,
        count * key_value.shape[0],
        out_shape=[
            jax.ShapeDtypeStruct(query.shape, F32),
            jax.ShapeDtypeStruct(kv_shape, BF16),
            jax.ShapeDtypeStruct((queries, width), BF16),
        ],
        grid_spec=pltpu.PrefetchScalarGridSpec(
            num_scalar_prefetch=1,
            grid=(1,),
            in_specs=[
                whole(query.shape), whole(key_value.shape), whole(weight.shape),
                whole((HD, count)), line, line, line, *[whole(p.shape) for p in pieces],
            ],
            out_specs=[whole(query.shape), whole(kv_shape), whole((queries, width))],
            scratch_shapes=[
                pltpu.VMEM((count, HD), BF16),
                pltpu.VMEM((HD, count), BF16),
                pltpu.VMEM((1, count), F32),
                pltpu.VMEM((HD, count), F32),
            ],
        ),
    )(span, query, key_value, weight, mixed_turned, log_total, low, high, *pieces)


def hidden_kernel(half, part, step, own_ref, other_ref, grad_own_ref, grad_other_ref, gate_ref,
                  up_ref, down_ref, rows_ref, hid_ref, dgate_ref, dup_ref, back_own_ref,
                  back_other_ref, unit, grad):
    at = pl.program_id(0)
    steps = part // step

    @pl.when(at == 0)
    def _():
        unit[:half] = own_ref[...]
        unit[half:] = other_ref[...]
        grad[:half] = grad_own_ref[...]
        grad[half:] = grad_other_ref[...]

    @pl.when(at < steps)
    def _():
        here = pl.ds(pl.multiple_of(jnp.minimum(at, steps - 1) * step, step), step)
        gate = dot(unit[...], gate_ref[...], ((1,), (0,)))
        up = dot(unit[...], up_ref[...], ((1,), (0,)))
        sigmoid = jax.nn.sigmoid(gate)
        activated = gate * sigmoid
        hid_ref[:, here] = (activated * up).astype(BF16)
        hidden_grad = dot(grad[...], down_ref[...], ((1,), (0,)))
        dgate_ref[:, here] = (
            hidden_grad * up * sigmoid * (1.0 + gate * (1.0 - sigmoid))
        ).astype(BF16)
        dup_ref[:, here] = (hidden_grad * activated).astype(BF16)

    @pl.when(at >= steps)
    def _():
        full = dot(dgate_ref[...], rows_ref[:, :part], ((1,), (1,)))
        full += dot(dup_ref[...], rows_ref[:, part:], ((1,), (1,)))
        back_own_ref[...] = full[:half]
        back_other_ref[...] = full[half:].astype(BF16)


def hidden_units(units, grads, weight, part):
    half, width = units[0].shape
    count = 2 * half
    step, rows = 256, 512
    steps = part // step
    block = lambda which: pl.BlockSpec(
        (width, step), lambda j: (0, which * steps + jnp.minimum(j, steps - 1))
    )
    back = pl.BlockSpec((half, rows), lambda j: (0, jnp.maximum(j - steps, 0)))
    return call(
        lambda *refs: hidden_kernel(half, part, step, *refs),
        "hidden_units",
        10 * count * width * part,
        2 * weight.size + 4 * width * part + 4 * count * width,
        count * part,
        grid=(steps + width // rows,),
        in_specs=[whole((half, width))] * 4
        + [block(0), block(1), block(2)]
        + [pl.BlockSpec((rows, 2 * part), lambda j: (jnp.maximum(j - steps, 0), 0))],
        out_specs=[whole((count, part))] * 3 + [back, back],
        out_shape=[jax.ShapeDtypeStruct((count, part), BF16)] * 3
        + [
            jax.ShapeDtypeStruct((half, width), F32),
            jax.ShapeDtypeStruct((half, width), BF16),
        ],
        scratch_shapes=[pltpu.VMEM((count, width), BF16)] * 2,
    )(*units, *grads, weight, weight, weight, weight)


def weight_grad_kernel(half, part, own_ref, other_ref, grad_own_ref, grad_other_ref, dgate_ref,
                       dup_ref, hid_ref, out_ref):
    unit = jnp.concatenate([own_ref[...], other_ref[...]], axis=0)
    grad = jnp.concatenate([grad_own_ref[...], grad_other_ref[...]], axis=0)
    out_ref[:, :part] = dot(unit, dgate_ref[...], ((0,), (0,))).astype(BF16)
    out_ref[:, part : 2 * part] = dot(unit, dup_ref[...], ((0,), (0,))).astype(BF16)
    out_ref[:, 2 * part :] = dot(grad, hid_ref[...], ((0,), (0,))).astype(BF16)


def weight_grad(units, grads, dgate, dup, hid):
    half, width = units[0].shape
    count, part = hid.shape
    step = 256
    column = pl.BlockSpec((half, step), lambda j: (0, j))
    return call(
        lambda *refs: weight_grad_kernel(half, part, *refs),
        "weight_grad",
        6 * count * width * part,
        6 * width * part + 8 * half * width,
        grid=(width // step,),
        in_specs=[column] * 4 + [whole(dgate.shape), whole(dup.shape), whole(hid.shape)],
        out_specs=pl.BlockSpec((step, 3 * part), lambda j: (j, 0)),
        out_shape=jax.ShapeDtypeStruct((width, 3 * part), BF16),
    )(*units, *grads, dgate, dup, hid)


def both_half_rows(block, core, here_ref, there_ref, columns):
    half = here_ref.shape[1]
    for p in range(here_ref.shape[0]):
        low, high = (block[(2 * p + k) * half : (2 * p + k + 1) * half] for k in (0, 1))
        here_ref[p, :, columns] = jnp.where(core == 0, low, high)
        there_ref[p, :, columns] = jnp.where(core == 0, high, low).astype(BF16)


def input_grad_kernel(spot, got_ref, pre_ref, query_ref, kv_ref, unit_ref, cos_ref, sin_ref,
                      p0_ref, p1_ref, p2_ref, p3_ref, here_ref, there_ref, kv_pre, part):
    mine = p0_ref.shape[0]

    @pl.when(pl.program_id(0) == 0)
    def _():
        total = jnp.sum(got_ref[...].astype(F32), axis=0)
        key = total[:, :HD]
        key = key * cos_ref[...] + pltpu.roll(key, HD // 2, 1) * sin_ref[...]
        kv_pre[:, :HD] = key.astype(BF16)
        kv_pre[:, HD:] = total[:, HD:].astype(BF16)

    part[...] = dot(pre_ref[...], query_ref[...], ((1,), (1,))) + dot(
        kv_pre[...], kv_ref[...], ((1,), (1,))
    )
    for s, piece in enumerate((p0_ref, p1_ref, p2_ref, p3_ref)):
        at = pl.multiple_of(lax.rem(spot[1] + 4 - s, 4) * mine, mine)
        piece[...] = part[pl.ds(at, mine), :].astype(BF16)
    block = dot(unit_ref[...], kv_pre[...], ((0,), (0,)))
    both_half_rows(block, spot[0], here_ref, there_ref, slice(0, 2 * HD))


def input_grad_parts(spot, got, query_pre, weight_query, weight_kv, unit, cosine, sine):
    planes, queries, pair = got.shape
    width, wide = weight_query.shape[0], query_pre.shape[1]
    rows, step, mine = width // (2 * planes), 512, queries // 4
    out = pl.BlockSpec((step // (2 * rows), rows, pair), lambda j, *_: (j, 0, 0))
    piece = pl.BlockSpec((mine, step), lambda j, *_: (0, j))
    return call(
        input_grad_kernel,
        "input_grad",
        60 * queries * width * (wide + 2 * pair),
        2 * (got.size + weight_query.size + weight_kv.size + 2 * unit.size),
        grid_spec=pltpu.PrefetchScalarGridSpec(
            num_scalar_prefetch=1,
            grid=(width // step,),
            in_specs=[
                whole(got.shape),
                whole(query_pre.shape),
                pl.BlockSpec((step, wide), lambda j, *_: (j, 0)),
                pl.BlockSpec((step, pair), lambda j, *_: (j, 0)),
                pl.BlockSpec((queries, step), lambda j, *_: (0, j)),
                whole(cosine.shape),
                whole(sine.shape),
            ],
            out_specs=[piece] * 4 + [out, out],
            scratch_shapes=[pltpu.VMEM((queries, pair), BF16), pltpu.VMEM((queries, step), F32)],
        ),
        out_shape=[jax.ShapeDtypeStruct((mine, width), BF16)] * 4
        + [
            jax.ShapeDtypeStruct((planes, rows, pair), F32),
            jax.ShapeDtypeStruct((planes, rows, pair), BF16),
        ],
    )(spot, got, query_pre, weight_query, weight_kv, unit, cosine, sine)


def spread(piece, xl, core):
    both = ordered(xl, piece, flip(piece, "xl"), 0)
    return ordered(core, both[None], flip(both, "c")[None], 0)


def over_mp(value):
    turned = [lax.ppermute(value, MP, [(i, (i + s) % 4) for i in range(4)]) for s in (1, 2, 3)]
    return sum(turned, value)


def on_device(
    tokens,
    segment_ids,
    skip_mask,
    norm1_gain,
    w_query,
    w_key,
    w_value,
    w_out,
    norm2_gain,
    w_gate,
    w_up,
    w_down,
    cotangent,
):
    local, width = tokens.shape[1:]
    documents = skip_mask.shape[1]
    xh, xl, core = lax.axis_index("xh"), lax.axis_index("xl"), lax.axis_index("c")
    chip = lax.axis_index(X4)
    plane = lax.axis_index(ZY)
    planes = lax.axis_size(ZY)
    queries = 2 * local
    mine = queries // 4
    every = planes * queries
    offset = plane * queries
    heads = w_query.shape[1] // HD
    wide = heads * HD
    scale = 1.0 / math.sqrt(HD)
    rows = w_query.shape[0]
    hidden_local = w_gate.shape[1]
    part = (hidden_local // 128 + 1) // 2 * 128
    lead = hidden_local - part
    spare = part - lead

    gain_one = norm1_gain.astype(F32)[:, None]
    gain_two = norm2_gain.astype(F32)[:, None]

    with jax.named_scope("attn_weights"):
        scaled = lambda w: (gain_one * w.astype(F32)).astype(BF16)
        own_heads = jnp.concatenate(
            [scaled(w_key), scaled(w_value), scaled(w_query), w_out.T], axis=1
        )
        half_heads = jnp.where(core == xh, own_heads, swap(own_heads))
        at_query, at_out = 2 * HD, 2 * HD + wide
        wide_weight = lax.all_gather(half_heads[:, at_query:], ("z", "y", "c"), axis=0, tiled=True)
        half_kv = from_everyone(half_heads[:, :at_query], ZY)
        pair_kv = ordered(core, half_kv[:, None], flip(half_kv, "c")[:, None], 1)
        weight_kv = pair_kv.reshape(width, at_query)

    with jax.named_scope("first_norm"):
        tokens_own = lax.dynamic_index_in_dim(tokens, core, 0, keepdims=False)
        tokens_all = ordered(xh, tokens_own, flip(tokens_own, "xh"), 0)
        unit_all = unit_scale(tokens_all.astype(F32))[0].astype(BF16)
        x_mine = lax.dynamic_slice_in_dim(tokens_own, xl * mine, mine).astype(F32)
        first_unit, first_factor = unit_scale(x_mine)

    with jax.named_scope("layout"):
        segment_own = lax.dynamic_index_in_dim(segment_ids, core, 0, keepdims=False)
        skip_own = lax.dynamic_index_in_dim(skip_mask, core, 0, keepdims=False)
        place, start, last, keep = layout(segment_own, skip_own, documents)
        here = lambda a: lax.dynamic_slice_in_dim(a, offset, queries)
        low, high = here(start), here(last)
        span = jnp.stack([low[0] // TILE, (high[-1] + TILE - 1) // TILE, chip])
        low, high = (jnp.tile(a, heads)[None] for a in (low, high))
        keep_here = here(keep).reshape(4, mine, 1)
        keep_mine = lax.dynamic_index_in_dim(keep_here, chip, 0, keepdims=False)
        cosine, sine = rope_tables(here(place))

    with jax.named_scope("project"):
        raw = dot(unit_all, weight_kv, ((1,), (0,)))
        key = rotate(raw[:, :HD].reshape(queries, 1, HD), cosine, sine)[:, 0]
        key_value = jnp.concatenate([key, raw[:, HD:]], axis=1).astype(BF16)
        everyone = from_everyone(key_value, ZY).reshape(every, 2 * HD)
        weight_query, weight_out = wide_weight[:, :wide], wide_weight[:, wide:]
        raw = dot(unit_all, weight_query, ((1,), (0,)))
        query = rotate(raw.reshape(queries, heads, HD), cosine, sine).astype(BF16)
        query = query.reshape(queries, wide)

    with jax.named_scope("ffn_weights"):
        own_hidden = [
            (gain_two * w_gate.astype(F32)).astype(BF16),
            (gain_two * w_up.astype(F32)).astype(BF16),
            w_down.T,
        ]

        def columns(which):
            blank = (which == 1) & (lax.broadcasted_iota(jnp.int32, (rows, part), 1) < spare)
            shares = []
            for w in own_hidden:
                share = jnp.where(which == 0, w[:, :part], w[:, lead:])
                shares.append(jnp.where(blank, jnp.zeros_like(share), share))
            return jnp.concatenate(shares, axis=1)

        pair_rows = ordered(xh, columns(xh), flip(after(columns(1 - xh), weight_kv), "xh"), 0)
        hidden_weight = lax.all_gather(after(pair_rows, key_value), ZY, axis=0, tiled=True)

    with jax.named_scope("cotangent"):
        grad_local = lax.dynamic_index_in_dim(cotangent, core, 0, keepdims=False)
        upstream = lax.dynamic_slice_in_dim(grad_local, xl * mine, mine).astype(F32)
        grad_all = ordered(xh, grad_local, flip(after(grad_local, key_value), "xh"), 0)
        grad_kept = (keep_here * grad_all.reshape(4, mine, width).astype(F32)).astype(BF16)
        grad_own = jnp.concatenate(behind(grad_kept, chip), axis=0)
        ffn_grads = (grad_own, flip(grad_own, "c"))

    with jax.named_scope("attend"):
        mixed, mixed_turned, log_total = attend(
            span, after(query, ffn_grads[1]), everyone, low, high, heads, scale
        )

    with jax.named_scope("branch"):
        partial = dot(mixed, weight_out, ((1,), (1,))).astype(BF16)
        branch = ring_sum(behind(partial.reshape(4, mine, width), chip))
        middle = x_mine + keep_mine * branch
        second_unit, second_factor = unit_scale(middle)
        unit_own = jnp.concatenate(ring_gather(second_unit.astype(BF16)), axis=0)
        units = (unit_own, flip(unit_own, "c"))

    def own_sum(own_part, other_part):
        both = (own_part + flip(other_part, "c").astype(F32)).astype(BF16)
        return both, ring_sum(list(both.reshape(4, mine, width)))

    with jax.named_scope("ffn"):
        hidden, gate_grad, up_grad, own_part, other_part = hidden_units(
            units, ffn_grads, hidden_weight, part
        )
        both, scaled_two = own_sum(own_part, other_part)
        hidden_weight_grad = weight_grad(
            units, ffn_grads, gate_grad, up_grad, after(hidden, both)
        )
        hidden_owned = lax.psum_scatter(hidden_weight_grad, ZY, scatter_dimension=0, tiled=True)
        middle_grad = upstream + second_factor * (
            scaled_two - second_unit * jnp.mean(scaled_two * second_unit, axis=1, keepdims=True)
        )
        pieces = ring_gather((keep_mine * middle_grad).astype(BF16))

    with jax.named_scope("attend_back"):
        query_grad, kv_grad, branch_grad = attend_back(
            span, query, everyone, weight_out, mixed_turned, log_total, low, high, pieces,
            heads, scale,
        )
        owned = exchange(kv_grad, ZY)
        query_pre = rotate(query_grad.reshape(queries, heads, HD), cosine, -sine)
        query_pre = query_pre.astype(BF16).reshape(queries, wide)
        cos_rows, sin_rows = cosine[:, 0], sine[:, 0]
        turn_back = [jnp.concatenate(t, axis=1) for t in ((cos_rows, cos_rows), (sin_rows, -sin_rows))]
        *input_parts, kv_here, kv_there = input_grad_parts(
            jnp.stack([core, chip]), owned, query_pre, wide_weight, weight_kv, unit_all, *turn_back
        )

    with jax.named_scope("ffn_grads"):
        owned_pair = hidden_owned.reshape(2, rows, 3 * part)
        kept = jnp.where(xh == 0, owned_pair[0], owned_pair[1])
        sent = flip(jnp.where(xh == 0, owned_pair[1], owned_pair[0]), "xh")

    def owned_half(grad):
        pair = grad.reshape(planes, 2, rows, grad.shape[-1])
        here_half = jnp.where(core == 0, pair[:, 0], pair[:, 1])
        there_half = jnp.where(core == 0, pair[:, 1], pair[:, 0])
        return (here_half + flip(there_half.astype(BF16), "c").astype(F32)).astype(BF16)

    def over_planes(half):
        return exchange(half, ZY).astype(F32).sum(axis=0)

    with jax.named_scope("head_grads"):
        query_half = owned_half(dot(unit_all, query_pre, ((0,), (0,))))
        out_half = owned_half(dot(branch_grad, mixed, ((0,), (0,))))
        wide_half = jnp.concatenate([query_half, out_half], axis=2)
        wide_got = exchange(after(wide_half, owned), ZY)
        wide_owned = wide_got.astype(F32).sum(axis=0)
        kv_half = (kv_here + flip(kv_there, "c").astype(F32)).astype(BF16)
        kv_got = exchange(after(kv_half, wide_got), ZY)
        kv_owned = kv_got.astype(F32).sum(axis=0)
        summed = jnp.concatenate([kv_owned, wide_owned], axis=1)
        heads_owned = jnp.where(core == xh, summed, swap(summed.astype(BF16)).astype(F32))
        query_owned = heads_owned[:, at_query:at_out]
        key_owned, value_owned = heads_owned[:, :HD], heads_owned[:, HD:at_query]
        row_sum = lambda *pairs: sum(
            jnp.sum(g * w.astype(F32), axis=1, keepdims=True) for g, w in pairs
        )
        gain_one_sum = row_sum((query_owned, w_query), (key_owned, w_key), (value_owned, w_value))

    with jax.named_scope("result"):
        down = hidden_weight[:, 2 * part :]
        partial = dot(after(hidden, kv_grad), down, ((1,), (1,)))
        feedforward = own_sum(partial[:queries], partial[queries:].astype(BF16))[1]
        result = spread((middle + keep_mine * feedforward).astype(BF16), xl, core)

    with jax.named_scope("input_grad"):
        late_parts = lax.optimization_barrier((*input_parts, wide_got))[:-1]
        late_parts = ring_parts(list(late_parts))
        late_parts = lax.optimization_barrier((*late_parts, kv_got))[:-1]
        scaled_one = sum(a.astype(F32) for a in late_parts)
        input_grad = middle_grad + first_factor * (
            scaled_one - first_unit * jnp.mean(scaled_one * first_unit, axis=1, keepdims=True)
        )
        input_grad = spread(input_grad.astype(BF16), xl, core)

    with jax.named_scope("ffn_grads"):
        low_part = pick(True, xh, kept, sent).astype(F32)
        high_part = pick(False, xh, kept, sent).astype(F32)
        gate_owned, up_owned, down_owned = (
            jnp.concatenate(
                [low_part[:, i * part : (i + 1) * part], high_part[:, i * part + spare : (i + 1) * part]],
                axis=1,
            )
            for i in range(3)
        )
        gain_two_sum = row_sum((gate_owned, w_gate), (up_owned, w_up))

    with jax.named_scope("gain_grads"):
        gain_grads = over_mp(jnp.concatenate([gain_one_sum, gain_two_sum], axis=1))

    return (
        result,
        input_grad,
        gain_grads[:, 0],
        gain_one * query_owned,
        gain_one * key_owned,
        gain_one * value_owned,
        heads_owned[:, at_out:].T,
        gain_grads[:, 1],
        gain_two * gate_owned,
        gain_two * up_owned,
        down_owned.T,
    )


def solution(mesh):
    split = Mesh(mesh.devices.reshape(4, 4, 2, 2, 2), AXES)
    token = P(None, DP, None)
    by_row = P(DP, MP)
    by_column = P(MP, DP)
    in_specs = (
        token, P(), P(), P(DP), by_row, by_row, by_row, by_column,
        P(DP), by_row, by_row, by_column, token,
    )
    out_specs = (
        token, token, P(DP), by_row, by_row, by_row, by_column,
        P(DP), by_row, by_row, by_column,
    )
    return jax.shard_map(
        on_device, mesh=split, in_specs=in_specs, out_specs=out_specs, check_vma=False
    )
```

```python
import math

import jax
import jax.numpy as jnp
from jax import lax
from jax.experimental import pallas as pl
from jax.experimental.pallas import tpu as pltpu
from jax.sharding import Mesh
from jax.sharding import PartitionSpec as P

HD = 128
BLOCK = 256
EPSILON = 1e-05
MASKED = -1e30
FLOOR = -1e29
LOG2E = 1.4426950408889634
TILE = 512
VMEM_LIMIT = 56 * 1024 * 1024

AXES = ("z", "y", "xh", "xl", "c")
DP = ("z", "y", "xh")
MP = ("xl", "c")
ZY = ("z", "y")
X4 = ("xh", "xl")
F32 = jnp.float32
BF16 = jnp.bfloat16


def after(value, *others):
    return lax.optimization_barrier((value, *others))[0]


def exchange(value, axes):
    return lax.all_to_all(value, axes, split_axis=0, concat_axis=0, tiled=True)


def from_everyone(value, axes):
    return exchange(jnp.broadcast_to(value, (lax.axis_size(axes), *value.shape)), axes)


def flip(value, axis):
    return lax.ppermute(value, axis, [(0, 1), (1, 0)])


def swap(value):
    return lax.ppermute(value, ("xh", "c"), [(1, 2), (2, 1)])


def turn(value, step):
    return lax.ppermute(value, X4, [(i, (i + step) % 4) for i in range(4)])


def ring_gather(block):
    far = turn(block, 2)
    return [block, turn(block, 1), far, turn(block, 3)]


def ring_parts(pieces):
    far = turn(pieces[2], -2)
    return [pieces[0], *(turn(pieces[s], -s) for s in (1, 3)), far]


def ring_sum(pieces):
    return sum(a.astype(F32) for a in ring_parts(pieces))


def behind(blocks, chip):
    return [lax.dynamic_index_in_dim(blocks, (chip - s) % 4, 0, keepdims=False) for s in range(4)]


def pick(first, when, own, other):
    return jnp.where(when == 0, own, other) if first else jnp.where(when == 0, other, own)


def ordered(when, own, other, axis):
    return jnp.concatenate([pick(True, when, own, other), pick(False, when, own, other)], axis=axis)


def rope_tables(place):
    half = HD // 2
    rates = jnp.exp(jnp.arange(half, dtype=F32) * (-2.0 * math.log(10000.0) / HD))
    angles = place.astype(F32)[:, None] * rates[None, :]
    return jnp.cos(angles)[:, None, :], jnp.sin(angles)[:, None, :]


def rotate(values, cosine, sine):
    half = HD // 2
    first, second = values[..., :half], values[..., half:]
    return jnp.concatenate(
        [first * cosine - second * sine, second * cosine + first * sine], axis=-1
    )


def layout(segments, skips, documents):
    count = segments.shape[0]
    labels = jnp.arange(documents, dtype=jnp.int32)
    member = segments[:, None] == labels[None, :]
    starts = jnp.sum((segments[:, None] < labels[None, :]).astype(jnp.int32), axis=0)
    ends = jnp.sum((segments[:, None] <= labels[None, :]).astype(jnp.int32), axis=0)
    start = jnp.sum(jnp.where(member, starts[None, :], 0), axis=1)
    end = jnp.sum(jnp.where(member, ends[None, :], 0), axis=1)
    place = jnp.arange(count, dtype=jnp.int32) - start
    keep = 1.0 - jnp.sum(jnp.where(member, skips[None, :], 0), axis=1).astype(F32)
    last = jnp.minimum(start + (place // BLOCK + 1) * BLOCK, end)
    return place, start, last, keep


def unit_scale(values):
    factor = lax.rsqrt(jnp.mean(values * values, axis=1, keepdims=True) + EPSILON)
    return values * factor, factor


def dot(a, b, dims):
    return lax.dot_general(a, b, (dims, ((), ())), preferred_element_type=F32)


def whole(shape):
    return pl.BlockSpec(shape, lambda *_: (0,) * len(shape))


def call(kernel, name, flops, moved, exps=0, **options):
    params = pltpu.CompilerParams(vmem_limit_bytes=VMEM_LIMIT)
    cost = pl.CostEstimate(flops=flops, bytes_accessed=moved, transcendentals=exps)
    return pl.pallas_call(
        kernel, name=name, compiler_params=params, cost_estimate=cost, **options
    )


def by_heads(block, heads):
    return jnp.concatenate([block[:, h * HD : (h + 1) * HD] for h in range(heads)], axis=0)


def store_heads(out_ref, turned, heads, queries):
    for h in range(heads):
        piece = turned[:, h * queries : (h + 1) * queries]
        out_ref[:, h * HD : (h + 1) * HD] = piece.T.astype(out_ref.dtype)


def reach(start, low_ref, high_ref, count):
    spot = start + lax.broadcasted_iota(jnp.int32, (TILE, count), 0)
    return (spot >= low_ref[...]) & (spot < high_ref[...])


def attend_kernel(heads, queries, scale, span, q_ref, kv_ref, low_ref, high_ref,
                  out_ref, turned_ref, log_ref, rows, top, total, running):
    count = heads * queries
    rows[...] = by_heads(q_ref[...], heads)
    top[...] = jnp.full_like(top, FLOOR)
    total[...] = jnp.zeros_like(total)
    running[...] = jnp.zeros_like(running)

    def step(i, _):
        start = pl.multiple_of(i * TILE, TILE)
        keys = kv_ref[pl.ds(start, TILE), :HD]
        values = kv_ref[pl.ds(start, TILE), HD:]
        scores = dot(keys, rows[...], ((1,), (1,))) * (scale * LOG2E)
        scores = jnp.where(reach(start, low_ref, high_ref, count), scores, MASKED)
        higher = jnp.maximum(top[...], jnp.max(scores, axis=0, keepdims=True))
        weights = jnp.exp2(scores - higher)
        fade = jnp.exp2(top[...] - higher)
        total[...] = total[...] * fade + jnp.sum(weights, axis=0, keepdims=True)
        running[...] = running[...] * fade + dot(values, weights.astype(BF16), ((0,), (0,)))
        top[...] = higher
        return 0

    lax.fori_loop(span[0], span[1], step, 0)
    mixed = running[...] / total[...]
    turned_ref[...] = mixed.astype(BF16)
    store_heads(out_ref, mixed, heads, queries)
    log_ref[...] = top[...] + jnp.log2(total[...])


def attend(span, query, key_value, low, high, heads, scale):
    queries = query.shape[0]
    count = heads * queries
    line = whole((1, count))
    return call(
        lambda *refs: attend_kernel(heads, queries, scale, *refs),
        "attend",
        4 * count * key_value.shape[0] * HD,
        2 * key_value.size + 6 * query.size,
        count * key_value.shape[0],
        out_shape=[
            jax.ShapeDtypeStruct(query.shape, BF16),
            jax.ShapeDtypeStruct((HD, count), BF16),
            jax.ShapeDtypeStruct((1, count), F32),
        ],
        grid_spec=pltpu.PrefetchScalarGridSpec(
            num_scalar_prefetch=1,
            grid=(1,),
            in_specs=[whole(query.shape), whole(key_value.shape), line, line],
            out_specs=[whole(query.shape), whole((HD, count)), line],
            scratch_shapes=[
                pltpu.VMEM((count, HD), BF16),
                pltpu.VMEM((1, count), F32),
                pltpu.VMEM((1, count), F32),
                pltpu.VMEM((HD, count), F32),
            ],
        ),
    )(span, query, key_value, low, high)


def attend_back_kernel(heads, queries, scale, span, q_ref, kv_ref, weight_ref, mixed_ref, log_ref,
                       low_ref, high_ref, p0_ref, p1_ref, p2_ref, p3_ref,
                       dq_ref, dkv_ref, branch_ref, rows, grads, delta, turned):
    count = heads * queries
    mine = queries // 4
    for s, piece in enumerate((p0_ref, p1_ref, p2_ref, p3_ref)):
        at = pl.multiple_of(lax.rem(span[2] + 4 - s, 4) * mine, mine)
        branch_ref[pl.ds(at, mine), :] = piece[...]
    mixed_grad = dot(branch_ref[...], weight_ref[...], ((1,), (0,))).astype(BF16).astype(F32)
    for h in range(heads):
        here = slice(h * queries, (h + 1) * queries)
        grads[:, here] = mixed_grad[:, h * HD : (h + 1) * HD].T.astype(BF16)
    delta[...] = jnp.sum(
        grads[...].astype(F32) * mixed_ref[...].astype(F32), axis=0, keepdims=True
    )
    rows[...] = by_heads(q_ref[...], heads)
    turned[...] = jnp.zeros_like(turned)
    dkv_ref[...] = jnp.zeros_like(dkv_ref)

    def step(i, _):
        start = pl.multiple_of(i * TILE, TILE)
        keys = kv_ref[pl.ds(start, TILE), :HD]
        values = kv_ref[pl.ds(start, TILE), HD:]
        scores = dot(keys, rows[...], ((1,), (1,))) * (scale * LOG2E) - log_ref[...]
        scores = jnp.where(reach(start, low_ref, high_ref, count), scores, MASKED)
        probs = jnp.exp2(scores)
        prob_grad = dot(values, grads[...], ((1,), (0,)))
        score_grad = (probs * (prob_grad - delta[...])).astype(BF16)
        key_grad = (dot(score_grad, rows[...], ((1,), (0,))) * scale).astype(BF16)
        value_grad = dot(probs.astype(BF16), grads[...], ((1,), (1,))).astype(BF16)
        for k in range(TILE // queries):
            here = slice(k * queries, (k + 1) * queries)
            dkv_ref[i * (TILE // queries) + k, :, :HD] = key_grad[here]
            dkv_ref[i * (TILE // queries) + k, :, HD:] = value_grad[here]
        turned[...] += dot(keys, score_grad, ((0,), (0,)))
        return 0

    lax.fori_loop(span[0], span[1], step, 0)
    store_heads(dq_ref, turned[...] * scale, heads, queries)


def attend_back(span, query, key_value, weight, mixed_turned, log_total, low, high, pieces,
                heads, scale):
    queries = query.shape[0]
    width = weight.shape[0]
    count = heads * queries
    line = whole((1, count))
    kv_shape = (key_value.shape[0] // queries, queries, 2 * HD)
    return call(
        lambda *refs: attend_back_kernel(heads, queries, scale, *refs),
        "attend_back",
        100 * count * key_value.shape[0] * HD,
        4 * key_value.size + 6 * query.size + 2 * weight.size,
        count * key_value.shape[0],
        out_shape=[
            jax.ShapeDtypeStruct(query.shape, F32),
            jax.ShapeDtypeStruct(kv_shape, BF16),
            jax.ShapeDtypeStruct((queries, width), BF16),
        ],
        grid_spec=pltpu.PrefetchScalarGridSpec(
            num_scalar_prefetch=1,
            grid=(1,),
            in_specs=[
                whole(query.shape), whole(key_value.shape), whole(weight.shape),
                whole((HD, count)), line, line, line, *[whole(p.shape) for p in pieces],
            ],
            out_specs=[whole(query.shape), whole(kv_shape), whole((queries, width))],
            scratch_shapes=[
                pltpu.VMEM((count, HD), BF16),
                pltpu.VMEM((HD, count), BF16),
                pltpu.VMEM((1, count), F32),
                pltpu.VMEM((HD, count), F32),
            ],
        ),
    )(span, query, key_value, weight, mixed_turned, log_total, low, high, *pieces)


def hidden_kernel(half, part, step, own_ref, other_ref, grad_own_ref, grad_other_ref, gate_ref,
                  up_ref, down_ref, rows_ref, hid_ref, dgate_ref, dup_ref, back_own_ref,
                  back_other_ref, unit, grad):
    at = pl.program_id(0)
    steps = part // step

    @pl.when(at == 0)
    def _():
        unit[:half] = own_ref[...]
        unit[half:] = other_ref[...]
        grad[:half] = grad_own_ref[...]
        grad[half:] = grad_other_ref[...]

    @pl.when(at < steps)
    def _():
        here = pl.ds(pl.multiple_of(jnp.minimum(at, steps - 1) * step, step), step)
        gate = dot(unit[...], gate_ref[...], ((1,), (0,)))
        up = dot(unit[...], up_ref[...], ((1,), (0,)))
        sigmoid = jax.nn.sigmoid(gate)
        activated = gate * sigmoid
        hid_ref[:, here] = (activated * up).astype(BF16)
        hidden_grad = dot(grad[...], down_ref[...], ((1,), (0,)))
        dgate_ref[:, here] = (
            hidden_grad * up * sigmoid * (1.0 + gate * (1.0 - sigmoid))
        ).astype(BF16)
        dup_ref[:, here] = (hidden_grad * activated).astype(BF16)

    @pl.when(at >= steps)
    def _():
        full = dot(dgate_ref[...], rows_ref[:, :part], ((1,), (1,)))
        full += dot(dup_ref[...], rows_ref[:, part:], ((1,), (1,)))
        back_own_ref[...] = full[:half]
        back_other_ref[...] = full[half:].astype(BF16)


def hidden_units(units, grads, weight, part):
    half, width = units[0].shape
    count = 2 * half
    step, rows = 256, 512
    steps = part // step
    block = lambda which: pl.BlockSpec(
        (width, step), lambda j: (0, which * steps + jnp.minimum(j, steps - 1))
    )
    back = pl.BlockSpec((half, rows), lambda j: (0, jnp.maximum(j - steps, 0)))
    return call(
        lambda *refs: hidden_kernel(half, part, step, *refs),
        "hidden_units",
        10 * count * width * part,
        2 * weight.size + 4 * width * part + 4 * count * width,
        count * part,
        grid=(steps + width // rows,),
        in_specs=[whole((half, width))] * 4
        + [block(0), block(1), block(2)]
        + [pl.BlockSpec((rows, 2 * part), lambda j: (jnp.maximum(j - steps, 0), 0))],
        out_specs=[whole((count, part))] * 3 + [back, back],
        out_shape=[jax.ShapeDtypeStruct((count, part), BF16)] * 3
        + [
            jax.ShapeDtypeStruct((half, width), F32),
            jax.ShapeDtypeStruct((half, width), BF16),
        ],
        scratch_shapes=[pltpu.VMEM((count, width), BF16)] * 2,
    )(*units, *grads, weight, weight, weight, weight)


def weight_grad_kernel(half, part, own_ref, other_ref, grad_own_ref, grad_other_ref, dgate_ref,
                       dup_ref, hid_ref, out_ref):
    unit = jnp.concatenate([own_ref[...], other_ref[...]], axis=0)
    grad = jnp.concatenate([grad_own_ref[...], grad_other_ref[...]], axis=0)
    out_ref[:, :part] = dot(unit, dgate_ref[...], ((0,), (0,))).astype(BF16)
    out_ref[:, part : 2 * part] = dot(unit, dup_ref[...], ((0,), (0,))).astype(BF16)
    out_ref[:, 2 * part :] = dot(grad, hid_ref[...], ((0,), (0,))).astype(BF16)


def weight_grad(units, grads, dgate, dup, hid):
    half, width = units[0].shape
    count, part = hid.shape
    step = 256
    column = pl.BlockSpec((half, step), lambda j: (0, j))
    return call(
        lambda *refs: weight_grad_kernel(half, part, *refs),
        "weight_grad",
        6 * count * width * part,
        6 * width * part + 8 * half * width,
        grid=(width // step,),
        in_specs=[column] * 4 + [whole(dgate.shape), whole(dup.shape), whole(hid.shape)],
        out_specs=pl.BlockSpec((step, 3 * part), lambda j: (j, 0)),
        out_shape=jax.ShapeDtypeStruct((width, 3 * part), BF16),
    )(*units, *grads, dgate, dup, hid)


def both_half_rows(block, core, here_ref, there_ref, columns):
    half = here_ref.shape[1]
    for p in range(here_ref.shape[0]):
        low, high = (block[(2 * p + k) * half : (2 * p + k + 1) * half] for k in (0, 1))
        here_ref[p, :, columns] = jnp.where(core == 0, low, high)
        there_ref[p, :, columns] = jnp.where(core == 0, high, low).astype(BF16)


def input_grad_kernel(spot, got_ref, pre_ref, query_ref, kv_ref, unit_ref, cos_ref, sin_ref,
                      p0_ref, p1_ref, p2_ref, p3_ref, here_ref, there_ref, kv_pre, part):
    mine = p0_ref.shape[0]

    @pl.when(pl.program_id(0) == 0)
    def _():
        total = jnp.sum(got_ref[...].astype(F32), axis=0)
        key = total[:, :HD]
        key = key * cos_ref[...] + pltpu.roll(key, HD // 2, 1) * sin_ref[...]
        kv_pre[:, :HD] = key.astype(BF16)
        kv_pre[:, HD:] = total[:, HD:].astype(BF16)

    part[...] = dot(pre_ref[...], query_ref[...], ((1,), (1,))) + dot(
        kv_pre[...], kv_ref[...], ((1,), (1,))
    )
    for s, piece in enumerate((p0_ref, p1_ref, p2_ref, p3_ref)):
        at = pl.multiple_of(lax.rem(spot[1] + 4 - s, 4) * mine, mine)
        piece[...] = part[pl.ds(at, mine), :].astype(BF16)
    block = dot(unit_ref[...], kv_pre[...], ((0,), (0,)))
    both_half_rows(block, spot[0], here_ref, there_ref, slice(0, 2 * HD))


def input_grad_parts(spot, got, query_pre, weight_query, weight_kv, unit, cosine, sine):
    planes, queries, pair = got.shape
    width, wide = weight_query.shape[0], query_pre.shape[1]
    rows, step, mine = width // (2 * planes), 512, queries // 4
    out = pl.BlockSpec((step // (2 * rows), rows, pair), lambda j, *_: (j, 0, 0))
    piece = pl.BlockSpec((mine, step), lambda j, *_: (0, j))
    return call(
        input_grad_kernel,
        "input_grad",
        60 * queries * width * (wide + 2 * pair),
        2 * (got.size + weight_query.size + weight_kv.size + 2 * unit.size),
        grid_spec=pltpu.PrefetchScalarGridSpec(
            num_scalar_prefetch=1,
            grid=(width // step,),
            in_specs=[
                whole(got.shape),
                whole(query_pre.shape),
                pl.BlockSpec((step, wide), lambda j, *_: (j, 0)),
                pl.BlockSpec((step, pair), lambda j, *_: (j, 0)),
                pl.BlockSpec((queries, step), lambda j, *_: (0, j)),
                whole(cosine.shape),
                whole(sine.shape),
            ],
            out_specs=[piece] * 4 + [out, out],
            scratch_shapes=[pltpu.VMEM((queries, pair), BF16), pltpu.VMEM((queries, step), F32)],
        ),
        out_shape=[jax.ShapeDtypeStruct((mine, width), BF16)] * 4
        + [
            jax.ShapeDtypeStruct((planes, rows, pair), F32),
            jax.ShapeDtypeStruct((planes, rows, pair), BF16),
        ],
    )(spot, got, query_pre, weight_query, weight_kv, unit, cosine, sine)


def spread(piece, xl, core):
    both = ordered(xl, piece, flip(piece, "xl"), 0)
    return ordered(core, both[None], flip(both, "c")[None], 0)


def over_mp(value):
    turned = [lax.ppermute(value, MP, [(i, (i + s) % 4) for i in range(4)]) for s in (1, 2, 3)]
    return sum(turned, value)


def on_device(
    tokens,
    segment_ids,
    skip_mask,
    norm1_gain,
    w_query,
    w_key,
    w_value,
    w_out,
    norm2_gain,
    w_gate,
    w_up,
    w_down,
    cotangent,
):
    local, width = tokens.shape[1:]
    documents = skip_mask.shape[1]
    xh, xl, core = lax.axis_index("xh"), lax.axis_index("xl"), lax.axis_index("c")
    chip = lax.axis_index(X4)
    plane = lax.axis_index(ZY)
    planes = lax.axis_size(ZY)
    queries = 2 * local
    mine = queries // 4
    every = planes * queries
    offset = plane * queries
    heads = w_query.shape[1] // HD
    wide = heads * HD
    scale = 1.0 / math.sqrt(HD)
    rows = w_query.shape[0]
    hidden_local = w_gate.shape[1]
    part = (hidden_local // 128 + 1) // 2 * 128
    lead = hidden_local - part
    spare = part - lead

    gain_one = norm1_gain.astype(F32)[:, None]
    gain_two = norm2_gain.astype(F32)[:, None]

    with jax.named_scope("attn_weights"):
        scaled = lambda w: (gain_one * w.astype(F32)).astype(BF16)
        own_heads = jnp.concatenate(
            [scaled(w_key), scaled(w_value), scaled(w_query), w_out.T], axis=1
        )
        half_heads = jnp.where(core == xh, own_heads, swap(own_heads))
        at_query, at_out = 2 * HD, 2 * HD + wide
        wide_weight = lax.all_gather(half_heads[:, at_query:], ("z", "y", "c"), axis=0, tiled=True)
        half_kv = from_everyone(half_heads[:, :at_query], ZY)
        pair_kv = ordered(core, half_kv[:, None], flip(half_kv, "c")[:, None], 1)
        weight_kv = pair_kv.reshape(width, at_query)

    with jax.named_scope("first_norm"):
        tokens_own = lax.dynamic_index_in_dim(tokens, core, 0, keepdims=False)
        tokens_all = ordered(xh, tokens_own, flip(tokens_own, "xh"), 0)
        unit_all = unit_scale(tokens_all.astype(F32))[0].astype(BF16)
        x_mine = lax.dynamic_slice_in_dim(tokens_own, xl * mine, mine).astype(F32)
        first_unit, first_factor = unit_scale(x_mine)

    with jax.named_scope("layout"):
        segment_own = lax.dynamic_index_in_dim(segment_ids, core, 0, keepdims=False)
        skip_own = lax.dynamic_index_in_dim(skip_mask, core, 0, keepdims=False)
        place, start, last, keep = layout(segment_own, skip_own, documents)
        here = lambda a: lax.dynamic_slice_in_dim(a, offset, queries)
        low, high = here(start), here(last)
        span = jnp.stack([low[0] // TILE, (high[-1] + TILE - 1) // TILE, chip])
        low, high = (jnp.tile(a, heads)[None] for a in (low, high))
        keep_here = here(keep).reshape(4, mine, 1)
        keep_mine = lax.dynamic_index_in_dim(keep_here, chip, 0, keepdims=False)
        cosine, sine = rope_tables(here(place))

    with jax.named_scope("project"):
        raw = dot(unit_all, weight_kv, ((1,), (0,)))
        key = rotate(raw[:, :HD].reshape(queries, 1, HD), cosine, sine)[:, 0]
        key_value = jnp.concatenate([key, raw[:, HD:]], axis=1).astype(BF16)
        everyone = from_everyone(key_value, ZY).reshape(every, 2 * HD)
        weight_query, weight_out = wide_weight[:, :wide], wide_weight[:, wide:]
        raw = dot(unit_all, weight_query, ((1,), (0,)))
        query = rotate(raw.reshape(queries, heads, HD), cosine, sine).astype(BF16)
        query = query.reshape(queries, wide)

    with jax.named_scope("ffn_weights"):
        own_hidden = [
            (gain_two * w_gate.astype(F32)).astype(BF16),
            (gain_two * w_up.astype(F32)).astype(BF16),
            w_down.T,
        ]

        def columns(which):
            blank = (which == 1) & (lax.broadcasted_iota(jnp.int32, (rows, part), 1) < spare)
            shares = []
            for w in own_hidden:
                share = jnp.where(which == 0, w[:, :part], w[:, lead:])
                shares.append(jnp.where(blank, jnp.zeros_like(share), share))
            return jnp.concatenate(shares, axis=1)

        pair_rows = ordered(xh, columns(xh), flip(after(columns(1 - xh), weight_kv), "xh"), 0)
        hidden_weight = lax.all_gather(after(pair_rows, key_value), ZY, axis=0, tiled=True)

    with jax.named_scope("cotangent"):
        grad_local = lax.dynamic_index_in_dim(cotangent, core, 0, keepdims=False)
        upstream = lax.dynamic_slice_in_dim(grad_local, xl * mine, mine).astype(F32)
        grad_all = ordered(xh, grad_local, flip(after(grad_local, key_value), "xh"), 0)
        grad_kept = (keep_here * grad_all.reshape(4, mine, width).astype(F32)).astype(BF16)
        grad_own = jnp.concatenate(behind(grad_kept, chip), axis=0)
        ffn_grads = (grad_own, flip(grad_own, "c"))

    with jax.named_scope("attend"):
        mixed, mixed_turned, log_total = attend(
            span, after(query, ffn_grads[1]), everyone, low, high, heads, scale
        )

    with jax.named_scope("branch"):
        partial = dot(mixed, weight_out, ((1,), (1,))).astype(BF16)
        branch = ring_sum(behind(partial.reshape(4, mine, width), chip))
        middle = x_mine + keep_mine * branch
        second_unit, second_factor = unit_scale(middle)
        unit_own = jnp.concatenate(ring_gather(second_unit.astype(BF16)), axis=0)
        units = (unit_own, flip(unit_own, "c"))

    def own_sum(own_part, other_part):
        both = (own_part + flip(other_part, "c").astype(F32)).astype(BF16)
        return both, ring_sum(list(both.reshape(4, mine, width)))

    with jax.named_scope("ffn"):
        hidden, gate_grad, up_grad, own_part, other_part = hidden_units(
            units, ffn_grads, hidden_weight, part
        )
        both, scaled_two = own_sum(own_part, other_part)
        hidden_weight_grad = weight_grad(
            units, ffn_grads, gate_grad, up_grad, after(hidden, both)
        )
        hidden_owned = lax.psum_scatter(hidden_weight_grad, ZY, scatter_dimension=0, tiled=True)
        middle_grad = upstream + second_factor * (
            scaled_two - second_unit * jnp.mean(scaled_two * second_unit, axis=1, keepdims=True)
        )
        pieces = ring_gather((keep_mine * middle_grad).astype(BF16))

    with jax.named_scope("attend_back"):
        query_grad, kv_grad, branch_grad = attend_back(
            span, query, everyone, weight_out, mixed_turned, log_total, low, high, pieces,
            heads, scale,
        )
        owned = exchange(kv_grad, ZY)
        query_pre = rotate(query_grad.reshape(queries, heads, HD), cosine, -sine)
        query_pre = query_pre.astype(BF16).reshape(queries, wide)
        cos_rows, sin_rows = cosine[:, 0], sine[:, 0]
        turn_back = [jnp.concatenate(t, axis=1) for t in ((cos_rows, cos_rows), (sin_rows, -sin_rows))]
        *input_parts, kv_here, kv_there = input_grad_parts(
            jnp.stack([core, chip]), owned, query_pre, wide_weight, weight_kv, unit_all, *turn_back
        )

    with jax.named_scope("ffn_grads"):
        owned_pair = hidden_owned.reshape(2, rows, 3 * part)
        kept = jnp.where(xh == 0, owned_pair[0], owned_pair[1])
        sent = flip(jnp.where(xh == 0, owned_pair[1], owned_pair[0]), "xh")

    def owned_half(grad):
        pair = grad.reshape(planes, 2, rows, grad.shape[-1])
        here_half = jnp.where(core == 0, pair[:, 0], pair[:, 1])
        there_half = jnp.where(core == 0, pair[:, 1], pair[:, 0])
        return (here_half + flip(there_half.astype(BF16), "c").astype(F32)).astype(BF16)

    def over_planes(half):
        return exchange(half, ZY).astype(F32).sum(axis=0)

    with jax.named_scope("head_grads"):
        query_half = owned_half(dot(unit_all, query_pre, ((0,), (0,))))
        out_half = owned_half(dot(branch_grad, mixed, ((0,), (0,))))
        wide_half = jnp.concatenate([query_half, out_half], axis=2)
        wide_got = exchange(after(wide_half, owned), ZY)
        wide_owned = wide_got.astype(F32).sum(axis=0)
        kv_half = (kv_here + flip(kv_there, "c").astype(F32)).astype(BF16)
        kv_got = exchange(after(kv_half, wide_got), ZY)
        kv_owned = kv_got.astype(F32).sum(axis=0)
        summed = jnp.concatenate([kv_owned, wide_owned], axis=1)
        heads_owned = jnp.where(core == xh, summed, swap(summed.astype(BF16)).astype(F32))
        query_owned = heads_owned[:, at_query:at_out]
        key_owned, value_owned = heads_owned[:, :HD], heads_owned[:, HD:at_query]
        row_sum = lambda *pairs: sum(
            jnp.sum(g * w.astype(F32), axis=1, keepdims=True) for g, w in pairs
        )
        gain_one_sum = row_sum((query_owned, w_query), (key_owned, w_key), (value_owned, w_value))

    with jax.named_scope("result"):
        down = hidden_weight[:, 2 * part :]
        partial = dot(after(hidden, kv_grad), down, ((1,), (1,)))
        feedforward = own_sum(partial[:queries], partial[queries:].astype(BF16))[1]
        result = spread((middle + keep_mine * feedforward).astype(BF16), xl, core)

    with jax.named_scope("input_grad"):
        late_parts = lax.optimization_barrier((*input_parts, wide_got))[:-1]
        late_parts = ring_parts(list(late_parts))
        scaled_one = sum(a.astype(F32) for a in late_parts)
        input_grad = middle_grad + first_factor * (
            scaled_one - first_unit * jnp.mean(scaled_one * first_unit, axis=1, keepdims=True)
        )
        input_grad = spread(input_grad.astype(BF16), xl, core)

    with jax.named_scope("ffn_grads"):
        low_part = pick(True, xh, kept, sent).astype(F32)
        high_part = pick(False, xh, kept, sent).astype(F32)
        gate_owned, up_owned, down_owned = (
            jnp.concatenate(
                [low_part[:, i * part : (i + 1) * part], high_part[:, i * part + spare : (i + 1) * part]],
                axis=1,
            )
            for i in range(3)
        )
        gain_two_sum = row_sum((gate_owned, w_gate), (up_owned, w_up))

    with jax.named_scope("gain_grads"):
        gain_grads = over_mp(jnp.concatenate([gain_one_sum, gain_two_sum], axis=1))

    return (
        result,
        input_grad,
        gain_grads[:, 0],
        gain_one * query_owned,
        gain_one * key_owned,
        gain_one * value_owned,
        heads_owned[:, at_out:].T,
        gain_grads[:, 1],
        gain_two * gate_owned,
        gain_two * up_owned,
        down_owned.T,
    )


def solution(mesh):
    split = Mesh(mesh.devices.reshape(4, 4, 2, 2, 2), AXES)
    token = P(None, DP, None)
    by_row = P(DP, MP)
    by_column = P(MP, DP)
    in_specs = (
        token, P(), P(), P(DP), by_row, by_row, by_row, by_column,
        P(DP), by_row, by_row, by_column, token,
    )
    out_specs = (
        token, token, P(DP), by_row, by_row, by_row, by_column,
        P(DP), by_row, by_row, by_column,
    )
    return jax.shard_map(
        on_device, mesh=split, in_specs=in_specs, out_specs=out_specs, check_vma=False
    )
```

```python
import math

import jax
import jax.numpy as jnp
from jax import lax
from jax.experimental import pallas as pl
from jax.experimental.pallas import tpu as pltpu
from jax.sharding import Mesh
from jax.sharding import PartitionSpec as P

HD = 128
BLOCK = 256
EPSILON = 1e-05
MASKED = -1e30
FLOOR = -1e29
LOG2E = 1.4426950408889634
TILE = 512
VMEM_LIMIT = 56 * 1024 * 1024

AXES = ("z", "y", "xh", "xl", "c")
DP = ("z", "y", "xh")
MP = ("xl", "c")
ZY = ("z", "y")
X4 = ("xh", "xl")
F32 = jnp.float32
BF16 = jnp.bfloat16


def after(value, *others):
    return lax.optimization_barrier((value, *others))[0]


def exchange(value, axes):
    return lax.all_to_all(value, axes, split_axis=0, concat_axis=0, tiled=True)


def from_everyone(value, axes):
    return exchange(jnp.broadcast_to(value, (lax.axis_size(axes), *value.shape)), axes)


def flip(value, axis):
    return lax.ppermute(value, axis, [(0, 1), (1, 0)])


def swap(value):
    return lax.ppermute(value, ("xh", "c"), [(1, 2), (2, 1)])


def turn(value, step):
    return lax.ppermute(value, X4, [(i, (i + step) % 4) for i in range(4)])


def ring_gather(block):
    far = turn(block, 2)
    return [block, turn(block, 1), far, turn(block, 3)]


def ring_parts(pieces):
    far = turn(pieces[2], -2)
    return [pieces[0], *(turn(pieces[s], -s) for s in (1, 3)), far]


def ring_sum(pieces):
    return sum(a.astype(F32) for a in ring_parts(pieces))


def behind(blocks, chip):
    return [lax.dynamic_index_in_dim(blocks, (chip - s) % 4, 0, keepdims=False) for s in range(4)]


def pick(first, when, own, other):
    return jnp.where(when == 0, own, other) if first else jnp.where(when == 0, other, own)


def ordered(when, own, other, axis):
    return jnp.concatenate([pick(True, when, own, other), pick(False, when, own, other)], axis=axis)


def rope_tables(place):
    half = HD // 2
    rates = jnp.exp(jnp.arange(half, dtype=F32) * (-2.0 * math.log(10000.0) / HD))
    angles = place.astype(F32)[:, None] * rates[None, :]
    return jnp.cos(angles)[:, None, :], jnp.sin(angles)[:, None, :]


def rotate(values, cosine, sine):
    half = HD // 2
    first, second = values[..., :half], values[..., half:]
    return jnp.concatenate(
        [first * cosine - second * sine, second * cosine + first * sine], axis=-1
    )


def layout(segments, skips, documents):
    count = segments.shape[0]
    labels = jnp.arange(documents, dtype=jnp.int32)
    member = segments[:, None] == labels[None, :]
    starts = jnp.sum((segments[:, None] < labels[None, :]).astype(jnp.int32), axis=0)
    ends = jnp.sum((segments[:, None] <= labels[None, :]).astype(jnp.int32), axis=0)
    start = jnp.sum(jnp.where(member, starts[None, :], 0), axis=1)
    end = jnp.sum(jnp.where(member, ends[None, :], 0), axis=1)
    place = jnp.arange(count, dtype=jnp.int32) - start
    keep = 1.0 - jnp.sum(jnp.where(member, skips[None, :], 0), axis=1).astype(F32)
    last = jnp.minimum(start + (place // BLOCK + 1) * BLOCK, end)
    return place, start, last, keep


def unit_scale(values):
    factor = lax.rsqrt(jnp.mean(values * values, axis=1, keepdims=True) + EPSILON)
    return values * factor, factor


def dot(a, b, dims):
    return lax.dot_general(a, b, (dims, ((), ())), preferred_element_type=F32)


def whole(shape):
    return pl.BlockSpec(shape, lambda *_: (0,) * len(shape))


def call(kernel, name, flops, moved, exps=0, **options):
    params = pltpu.CompilerParams(vmem_limit_bytes=VMEM_LIMIT)
    cost = pl.CostEstimate(flops=flops, bytes_accessed=moved, transcendentals=exps)
    return pl.pallas_call(
        kernel, name=name, compiler_params=params, cost_estimate=cost, **options
    )


def by_heads(block, heads):
    return jnp.concatenate([block[:, h * HD : (h + 1) * HD] for h in range(heads)], axis=0)


def store_heads(out_ref, turned, heads, queries):
    for h in range(heads):
        piece = turned[:, h * queries : (h + 1) * queries]
        out_ref[:, h * HD : (h + 1) * HD] = piece.T.astype(out_ref.dtype)


def reach(start, low_ref, high_ref, count):
    spot = start + lax.broadcasted_iota(jnp.int32, (TILE, count), 0)
    return (spot >= low_ref[...]) & (spot < high_ref[...])


def attend_kernel(heads, queries, scale, span, q_ref, kv_ref, low_ref, high_ref,
                  out_ref, turned_ref, log_ref, rows, top, total, running):
    count = heads * queries
    rows[...] = by_heads(q_ref[...], heads)
    top[...] = jnp.full_like(top, FLOOR)
    total[...] = jnp.zeros_like(total)
    running[...] = jnp.zeros_like(running)

    def step(i, _):
        start = pl.multiple_of(i * TILE, TILE)
        keys = kv_ref[pl.ds(start, TILE), :HD]
        values = kv_ref[pl.ds(start, TILE), HD:]
        scores = dot(keys, rows[...], ((1,), (1,))) * (scale * LOG2E)
        scores = jnp.where(reach(start, low_ref, high_ref, count), scores, MASKED)
        higher = jnp.maximum(top[...], jnp.max(scores, axis=0, keepdims=True))
        weights = jnp.exp2(scores - higher)
        fade = jnp.exp2(top[...] - higher)
        total[...] = total[...] * fade + jnp.sum(weights, axis=0, keepdims=True)
        running[...] = running[...] * fade + dot(values, weights.astype(BF16), ((0,), (0,)))
        top[...] = higher
        return 0

    lax.fori_loop(span[0], span[1], step, 0)
    mixed = running[...] / total[...]
    turned_ref[...] = mixed.astype(BF16)
    store_heads(out_ref, mixed, heads, queries)
    log_ref[...] = top[...] + jnp.log2(total[...])


def attend(span, query, key_value, low, high, heads, scale):
    queries = query.shape[0]
    count = heads * queries
    line = whole((1, count))
    return call(
        lambda *refs: attend_kernel(heads, queries, scale, *refs),
        "attend",
        4 * count * key_value.shape[0] * HD,
        2 * key_value.size + 6 * query.size,
        count * key_value.shape[0],
        out_shape=[
            jax.ShapeDtypeStruct(query.shape, BF16),
            jax.ShapeDtypeStruct((HD, count), BF16),
            jax.ShapeDtypeStruct((1, count), F32),
        ],
        grid_spec=pltpu.PrefetchScalarGridSpec(
            num_scalar_prefetch=1,
            grid=(1,),
            in_specs=[whole(query.shape), whole(key_value.shape), line, line],
            out_specs=[whole(query.shape), whole((HD, count)), line],
            scratch_shapes=[
                pltpu.VMEM((count, HD), BF16),
                pltpu.VMEM((1, count), F32),
                pltpu.VMEM((1, count), F32),
                pltpu.VMEM((HD, count), F32),
            ],
        ),
    )(span, query, key_value, low, high)


def attend_back_kernel(heads, queries, scale, span, q_ref, kv_ref, weight_ref, mixed_ref, log_ref,
                       low_ref, high_ref, p0_ref, p1_ref, p2_ref, p3_ref,
                       dq_ref, dkv_ref, branch_ref, rows, grads, delta, turned):
    count = heads * queries
    mine = queries // 4
    for s, piece in enumerate((p0_ref, p1_ref, p2_ref, p3_ref)):
        at = pl.multiple_of(lax.rem(span[2] + 4 - s, 4) * mine, mine)
        branch_ref[pl.ds(at, mine), :] = piece[...]
    mixed_grad = dot(branch_ref[...], weight_ref[...], ((1,), (0,))).astype(BF16).astype(F32)
    for h in range(heads):
        here = slice(h * queries, (h + 1) * queries)
        grads[:, here] = mixed_grad[:, h * HD : (h + 1) * HD].T.astype(BF16)
    delta[...] = jnp.sum(
        grads[...].astype(F32) * mixed_ref[...].astype(F32), axis=0, keepdims=True
    )
    rows[...] = by_heads(q_ref[...], heads)
    turned[...] = jnp.zeros_like(turned)
    dkv_ref[...] = jnp.zeros_like(dkv_ref)

    def step(i, _):
        start = pl.multiple_of(i * TILE, TILE)
        keys = kv_ref[pl.ds(start, TILE), :HD]
        values = kv_ref[pl.ds(start, TILE), HD:]
        scores = dot(keys, rows[...], ((1,), (1,))) * (scale * LOG2E) - log_ref[...]
        scores = jnp.where(reach(start, low_ref, high_ref, count), scores, MASKED)
        probs = jnp.exp2(scores)
        prob_grad = dot(values, grads[...], ((1,), (0,)))
        score_grad = (probs * (prob_grad - delta[...])).astype(BF16)
        key_grad = (dot(score_grad, rows[...], ((1,), (0,))) * scale).astype(BF16)
        value_grad = dot(probs.astype(BF16), grads[...], ((1,), (1,))).astype(BF16)
        for k in range(TILE // queries):
            here = slice(k * queries, (k + 1) * queries)
            dkv_ref[i * (TILE // queries) + k, :, :HD] = key_grad[here]
            dkv_ref[i * (TILE // queries) + k, :, HD:] = value_grad[here]
        turned[...] += dot(keys, score_grad, ((0,), (0,)))
        return 0

    lax.fori_loop(span[0], span[1], step, 0)
    store_heads(dq_ref, turned[...] * scale, heads, queries)


def attend_back(span, query, key_value, weight, mixed_turned, log_total, low, high, pieces,
                heads, scale):
    queries = query.shape[0]
    width = weight.shape[0]
    count = heads * queries
    line = whole((1, count))
    kv_shape = (key_value.shape[0] // queries, queries, 2 * HD)
    return call(
        lambda *refs: attend_back_kernel(heads, queries, scale, *refs),
        "attend_back",
        100 * count * key_value.shape[0] * HD,
        4 * key_value.size + 6 * query.size + 2 * weight.size,
        count * key_value.shape[0],
        out_shape=[
            jax.ShapeDtypeStruct(query.shape, F32),
            jax.ShapeDtypeStruct(kv_shape, BF16),
            jax.ShapeDtypeStruct((queries, width), BF16),
        ],
        grid_spec=pltpu.PrefetchScalarGridSpec(
            num_scalar_prefetch=1,
            grid=(1,),
            in_specs=[
                whole(query.shape), whole(key_value.shape), whole(weight.shape),
                whole((HD, count)), line, line, line, *[whole(p.shape) for p in pieces],
            ],
            out_specs=[whole(query.shape), whole(kv_shape), whole((queries, width))],
            scratch_shapes=[
                pltpu.VMEM((count, HD), BF16),
                pltpu.VMEM((HD, count), BF16),
                pltpu.VMEM((1, count), F32),
                pltpu.VMEM((HD, count), F32),
            ],
        ),
    )(span, query, key_value, weight, mixed_turned, log_total, low, high, *pieces)


def hidden_kernel(half, part, step, own_ref, other_ref, grad_own_ref, grad_other_ref, gate_ref,
                  up_ref, down_ref, rows_ref, hid_ref, dgate_ref, dup_ref, back_own_ref,
                  back_other_ref, unit, grad):
    at = pl.program_id(0)
    steps = part // step

    @pl.when(at == 0)
    def _():
        unit[:half] = own_ref[...]
        unit[half:] = other_ref[...]
        grad[:half] = grad_own_ref[...]
        grad[half:] = grad_other_ref[...]

    @pl.when(at < steps)
    def _():
        here = pl.ds(pl.multiple_of(jnp.minimum(at, steps - 1) * step, step), step)
        gate = dot(unit[...], gate_ref[...], ((1,), (0,)))
        up = dot(unit[...], up_ref[...], ((1,), (0,)))
        sigmoid = jax.nn.sigmoid(gate)
        activated = gate * sigmoid
        hid_ref[:, here] = (activated * up).astype(BF16)
        hidden_grad = dot(grad[...], down_ref[...], ((1,), (0,)))
        dgate_ref[:, here] = (
            hidden_grad * up * sigmoid * (1.0 + gate * (1.0 - sigmoid))
        ).astype(BF16)
        dup_ref[:, here] = (hidden_grad * activated).astype(BF16)

    @pl.when(at >= steps)
    def _():
        full = dot(dgate_ref[...], rows_ref[:, :part], ((1,), (1,)))
        full += dot(dup_ref[...], rows_ref[:, part:], ((1,), (1,)))
        back_own_ref[...] = full[:half]
        back_other_ref[...] = full[half:].astype(BF16)


def hidden_units(units, grads, weight, part):
    half, width = units[0].shape
    count = 2 * half
    step, rows = 256, 512
    steps = part // step
    block = lambda which: pl.BlockSpec(
        (width, step), lambda j: (0, which * steps + jnp.minimum(j, steps - 1))
    )
    back = pl.BlockSpec((half, rows), lambda j: (0, jnp.maximum(j - steps, 0)))
    return call(
        lambda *refs: hidden_kernel(half, part, step, *refs),
        "hidden_units",
        10 * count * width * part,
        2 * weight.size + 4 * width * part + 4 * count * width,
        count * part,
        grid=(steps + width // rows,),
        in_specs=[whole((half, width))] * 4
        + [block(0), block(1), block(2)]
        + [pl.BlockSpec((rows, 2 * part), lambda j: (jnp.maximum(j - steps, 0), 0))],
        out_specs=[whole((count, part))] * 3 + [back, back],
        out_shape=[jax.ShapeDtypeStruct((count, part), BF16)] * 3
        + [
            jax.ShapeDtypeStruct((half, width), F32),
            jax.ShapeDtypeStruct((half, width), BF16),
        ],
        scratch_shapes=[pltpu.VMEM((count, width), BF16)] * 2,
    )(*units, *grads, weight, weight, weight, weight)


def weight_grad_kernel(half, part, own_ref, other_ref, grad_own_ref, grad_other_ref, dgate_ref,
                       dup_ref, hid_ref, out_ref):
    unit = jnp.concatenate([own_ref[...], other_ref[...]], axis=0)
    grad = jnp.concatenate([grad_own_ref[...], grad_other_ref[...]], axis=0)
    out_ref[:, :part] = dot(unit, dgate_ref[...], ((0,), (0,))).astype(BF16)
    out_ref[:, part : 2 * part] = dot(unit, dup_ref[...], ((0,), (0,))).astype(BF16)
    out_ref[:, 2 * part :] = dot(grad, hid_ref[...], ((0,), (0,))).astype(BF16)


def weight_grad(units, grads, dgate, dup, hid):
    half, width = units[0].shape
    count, part = hid.shape
    step = 256
    column = pl.BlockSpec((half, step), lambda j: (0, j))
    return call(
        lambda *refs: weight_grad_kernel(half, part, *refs),
        "weight_grad",
        6 * count * width * part,
        6 * width * part + 8 * half * width,
        grid=(width // step,),
        in_specs=[column] * 4 + [whole(dgate.shape), whole(dup.shape), whole(hid.shape)],
        out_specs=pl.BlockSpec((step, 3 * part), lambda j: (j, 0)),
        out_shape=jax.ShapeDtypeStruct((width, 3 * part), BF16),
    )(*units, *grads, dgate, dup, hid)


def both_half_rows(block, core, here_ref, there_ref, columns):
    half = here_ref.shape[1]
    for p in range(here_ref.shape[0]):
        low, high = (block[(2 * p + k) * half : (2 * p + k + 1) * half] for k in (0, 1))
        here_ref[p, :, columns] = jnp.where(core == 0, low, high)
        there_ref[p, :, columns] = jnp.where(core == 0, high, low).astype(BF16)


def input_grad_kernel(spot, got_ref, pre_ref, query_ref, kv_ref, unit_ref, cos_ref, sin_ref,
                      p0_ref, p1_ref, p2_ref, p3_ref, here_ref, there_ref, kv_pre, part):
    mine = p0_ref.shape[0]

    @pl.when(pl.program_id(0) == 0)
    def _():
        total = jnp.sum(got_ref[...].astype(F32), axis=0)
        key = total[:, :HD]
        key = key * cos_ref[...] + pltpu.roll(key, HD // 2, 1) * sin_ref[...]
        kv_pre[:, :HD] = key.astype(BF16)
        kv_pre[:, HD:] = total[:, HD:].astype(BF16)

    part[...] = dot(pre_ref[...], query_ref[...], ((1,), (1,))) + dot(
        kv_pre[...], kv_ref[...], ((1,), (1,))
    )
    for s, piece in enumerate((p0_ref, p1_ref, p2_ref, p3_ref)):
        at = pl.multiple_of(lax.rem(spot[1] + 4 - s, 4) * mine, mine)
        piece[...] = part[pl.ds(at, mine), :].astype(BF16)
    block = dot(unit_ref[...], kv_pre[...], ((0,), (0,)))
    both_half_rows(block, spot[0], here_ref, there_ref, slice(0, 2 * HD))


def input_grad_parts(spot, got, query_pre, weight_query, weight_kv, unit, cosine, sine):
    planes, queries, pair = got.shape
    width, wide = weight_query.shape[0], query_pre.shape[1]
    rows, step, mine = width // (2 * planes), 512, queries // 4
    out = pl.BlockSpec((step // (2 * rows), rows, pair), lambda j, *_: (j, 0, 0))
    piece = pl.BlockSpec((mine, step), lambda j, *_: (0, j))
    return call(
        input_grad_kernel,
        "input_grad",
        100 * queries * width * (wide + 2 * pair),
        2 * (got.size + weight_query.size + weight_kv.size + 2 * unit.size),
        grid_spec=pltpu.PrefetchScalarGridSpec(
            num_scalar_prefetch=1,
            grid=(width // step,),
            in_specs=[
                whole(got.shape),
                whole(query_pre.shape),
                pl.BlockSpec((step, wide), lambda j, *_: (j, 0)),
                pl.BlockSpec((step, pair), lambda j, *_: (j, 0)),
                pl.BlockSpec((queries, step), lambda j, *_: (0, j)),
                whole(cosine.shape),
                whole(sine.shape),
            ],
            out_specs=[piece] * 4 + [out, out],
            scratch_shapes=[pltpu.VMEM((queries, pair), BF16), pltpu.VMEM((queries, step), F32)],
        ),
        out_shape=[jax.ShapeDtypeStruct((mine, width), BF16)] * 4
        + [
            jax.ShapeDtypeStruct((planes, rows, pair), F32),
            jax.ShapeDtypeStruct((planes, rows, pair), BF16),
        ],
    )(spot, got, query_pre, weight_query, weight_kv, unit, cosine, sine)


def spread(piece, xl, core):
    both = ordered(xl, piece, flip(piece, "xl"), 0)
    return ordered(core, both[None], flip(both, "c")[None], 0)


def over_mp(value):
    turned = [lax.ppermute(value, MP, [(i, (i + s) % 4) for i in range(4)]) for s in (1, 2, 3)]
    return sum(turned, value)


def on_device(
    tokens,
    segment_ids,
    skip_mask,
    norm1_gain,
    w_query,
    w_key,
    w_value,
    w_out,
    norm2_gain,
    w_gate,
    w_up,
    w_down,
    cotangent,
):
    local, width = tokens.shape[1:]
    documents = skip_mask.shape[1]
    xh, xl, core = lax.axis_index("xh"), lax.axis_index("xl"), lax.axis_index("c")
    chip = lax.axis_index(X4)
    plane = lax.axis_index(ZY)
    planes = lax.axis_size(ZY)
    queries = 2 * local
    mine = queries // 4
    every = planes * queries
    offset = plane * queries
    heads = w_query.shape[1] // HD
    wide = heads * HD
    scale = 1.0 / math.sqrt(HD)
    rows = w_query.shape[0]
    hidden_local = w_gate.shape[1]
    part = (hidden_local // 128 + 1) // 2 * 128
    lead = hidden_local - part
    spare = part - lead

    gain_one = norm1_gain.astype(F32)[:, None]
    gain_two = norm2_gain.astype(F32)[:, None]

    with jax.named_scope("attn_weights"):
        scaled = lambda w: (gain_one * w.astype(F32)).astype(BF16)
        own_heads = jnp.concatenate(
            [scaled(w_key), scaled(w_value), scaled(w_query), w_out.T], axis=1
        )
        half_heads = jnp.where(core == xh, own_heads, swap(own_heads))
        at_query, at_out = 2 * HD, 2 * HD + wide
        wide_weight = lax.all_gather(half_heads[:, at_query:], ("z", "y", "c"), axis=0, tiled=True)
        half_kv = from_everyone(half_heads[:, :at_query], ZY)
        pair_kv = ordered(core, half_kv[:, None], flip(half_kv, "c")[:, None], 1)
        weight_kv = pair_kv.reshape(width, at_query)

    with jax.named_scope("first_norm"):
        tokens_own = lax.dynamic_index_in_dim(tokens, core, 0, keepdims=False)
        tokens_all = ordered(xh, tokens_own, flip(tokens_own, "xh"), 0)
        unit_all = unit_scale(tokens_all.astype(F32))[0].astype(BF16)
        x_mine = lax.dynamic_slice_in_dim(tokens_own, xl * mine, mine).astype(F32)
        first_unit, first_factor = unit_scale(x_mine)

    with jax.named_scope("layout"):
        segment_own = lax.dynamic_index_in_dim(segment_ids, core, 0, keepdims=False)
        skip_own = lax.dynamic_index_in_dim(skip_mask, core, 0, keepdims=False)
        place, start, last, keep = layout(segment_own, skip_own, documents)
        here = lambda a: lax.dynamic_slice_in_dim(a, offset, queries)
        low, high = here(start), here(last)
        span = jnp.stack([low[0] // TILE, (high[-1] + TILE - 1) // TILE, chip])
        low, high = (jnp.tile(a, heads)[None] for a in (low, high))
        keep_here = here(keep).reshape(4, mine, 1)
        keep_mine = lax.dynamic_index_in_dim(keep_here, chip, 0, keepdims=False)
        cosine, sine = rope_tables(here(place))

    with jax.named_scope("project"):
        raw = dot(unit_all, weight_kv, ((1,), (0,)))
        key = rotate(raw[:, :HD].reshape(queries, 1, HD), cosine, sine)[:, 0]
        key_value = jnp.concatenate([key, raw[:, HD:]], axis=1).astype(BF16)
        everyone = from_everyone(key_value, ZY).reshape(every, 2 * HD)
        weight_query, weight_out = wide_weight[:, :wide], wide_weight[:, wide:]
        raw = dot(unit_all, weight_query, ((1,), (0,)))
        query = rotate(raw.reshape(queries, heads, HD), cosine, sine).astype(BF16)
        query = query.reshape(queries, wide)

    with jax.named_scope("ffn_weights"):
        own_hidden = [
            (gain_two * w_gate.astype(F32)).astype(BF16),
            (gain_two * w_up.astype(F32)).astype(BF16),
            w_down.T,
        ]

        def columns(which):
            blank = (which == 1) & (lax.broadcasted_iota(jnp.int32, (rows, part), 1) < spare)
            shares = []
            for w in own_hidden:
                share = jnp.where(which == 0, w[:, :part], w[:, lead:])
                shares.append(jnp.where(blank, jnp.zeros_like(share), share))
            return jnp.concatenate(shares, axis=1)

        pair_rows = ordered(xh, columns(xh), flip(after(columns(1 - xh), weight_kv), "xh"), 0)
        hidden_weight = lax.all_gather(after(pair_rows, key_value), ZY, axis=0, tiled=True)

    with jax.named_scope("cotangent"):
        grad_local = lax.dynamic_index_in_dim(cotangent, core, 0, keepdims=False)
        upstream = lax.dynamic_slice_in_dim(grad_local, xl * mine, mine).astype(F32)
        grad_all = ordered(xh, grad_local, flip(after(grad_local, key_value), "xh"), 0)
        grad_kept = (keep_here * grad_all.reshape(4, mine, width).astype(F32)).astype(BF16)
        grad_own = jnp.concatenate(behind(grad_kept, chip), axis=0)
        ffn_grads = (grad_own, flip(grad_own, "c"))

    with jax.named_scope("attend"):
        mixed, mixed_turned, log_total = attend(
            span, after(query, ffn_grads[1]), everyone, low, high, heads, scale
        )

    with jax.named_scope("branch"):
        partial = dot(mixed, weight_out, ((1,), (1,))).astype(BF16)
        branch = ring_sum(behind(partial.reshape(4, mine, width), chip))
        middle = x_mine + keep_mine * branch
        second_unit, second_factor = unit_scale(middle)
        unit_own = jnp.concatenate(ring_gather(second_unit.astype(BF16)), axis=0)
        units = (unit_own, flip(unit_own, "c"))

    def own_sum(own_part, other_part):
        both = (own_part + flip(other_part, "c").astype(F32)).astype(BF16)
        return both, ring_sum(list(both.reshape(4, mine, width)))

    with jax.named_scope("ffn"):
        hidden, gate_grad, up_grad, own_part, other_part = hidden_units(
            units, ffn_grads, hidden_weight, part
        )
        both, scaled_two = own_sum(own_part, other_part)
        hidden_weight_grad = weight_grad(
            units, ffn_grads, gate_grad, up_grad, after(hidden, both)
        )
        hidden_owned = lax.psum_scatter(hidden_weight_grad, ZY, scatter_dimension=0, tiled=True)
        middle_grad = upstream + second_factor * (
            scaled_two - second_unit * jnp.mean(scaled_two * second_unit, axis=1, keepdims=True)
        )
        pieces = ring_gather((keep_mine * middle_grad).astype(BF16))

    with jax.named_scope("attend_back"):
        query_grad, kv_grad, branch_grad = attend_back(
            span, query, everyone, weight_out, mixed_turned, log_total, low, high, pieces,
            heads, scale,
        )
        owned = exchange(kv_grad, ZY)
        query_pre = rotate(query_grad.reshape(queries, heads, HD), cosine, -sine)
        query_pre = query_pre.astype(BF16).reshape(queries, wide)
        cos_rows, sin_rows = cosine[:, 0], sine[:, 0]
        turn_back = [jnp.concatenate(t, axis=1) for t in ((cos_rows, cos_rows), (sin_rows, -sin_rows))]
        *input_parts, kv_here, kv_there = input_grad_parts(
            jnp.stack([core, chip]), owned, query_pre, wide_weight, weight_kv, unit_all, *turn_back
        )

    with jax.named_scope("ffn_grads"):
        owned_pair = hidden_owned.reshape(2, rows, 3 * part)
        kept = jnp.where(xh == 0, owned_pair[0], owned_pair[1])
        sent = flip(jnp.where(xh == 0, owned_pair[1], owned_pair[0]), "xh")

    def owned_half(grad):
        pair = grad.reshape(planes, 2, rows, grad.shape[-1])
        here_half = jnp.where(core == 0, pair[:, 0], pair[:, 1])
        there_half = jnp.where(core == 0, pair[:, 1], pair[:, 0])
        return (here_half + flip(there_half.astype(BF16), "c").astype(F32)).astype(BF16)

    def over_planes(half):
        return exchange(half, ZY).astype(F32).sum(axis=0)

    with jax.named_scope("head_grads"):
        query_half = owned_half(dot(unit_all, query_pre, ((0,), (0,))))
        out_half = owned_half(dot(branch_grad, mixed, ((0,), (0,))))
        wide_half = jnp.concatenate([query_half, out_half], axis=2)
        wide_got = exchange(after(wide_half, owned), ZY)
        wide_owned = wide_got.astype(F32).sum(axis=0)
        kv_half = (kv_here + flip(kv_there, "c").astype(F32)).astype(BF16)
        kv_got = exchange(after(kv_half, wide_got), ZY)
        kv_owned = kv_got.astype(F32).sum(axis=0)
        summed = jnp.concatenate([kv_owned, wide_owned], axis=1)
        heads_owned = jnp.where(core == xh, summed, swap(summed.astype(BF16)).astype(F32))
        query_owned = heads_owned[:, at_query:at_out]
        key_owned, value_owned = heads_owned[:, :HD], heads_owned[:, HD:at_query]
        row_sum = lambda *pairs: sum(
            jnp.sum(g * w.astype(F32), axis=1, keepdims=True) for g, w in pairs
        )
        gain_one_sum = row_sum((query_owned, w_query), (key_owned, w_key), (value_owned, w_value))

    with jax.named_scope("result"):
        down = hidden_weight[:, 2 * part :]
        partial = dot(after(hidden, kv_grad), down, ((1,), (1,)))
        feedforward = own_sum(partial[:queries], partial[queries:].astype(BF16))[1]
        result = spread((middle + keep_mine * feedforward).astype(BF16), xl, core)

    with jax.named_scope("input_grad"):
        late_parts = lax.optimization_barrier((*input_parts, wide_got))[:-1]
        late_parts = ring_parts(list(late_parts))
        late_parts = lax.optimization_barrier((*late_parts, kv_got, sent))[:-2]
        scaled_one = sum(a.astype(F32) for a in late_parts)
        input_grad = middle_grad + first_factor * (
            scaled_one - first_unit * jnp.mean(scaled_one * first_unit, axis=1, keepdims=True)
        )
        input_grad = spread(input_grad.astype(BF16), xl, core)

    with jax.named_scope("ffn_grads"):
        low_part = pick(True, xh, kept, sent).astype(F32)
        high_part = pick(False, xh, kept, sent).astype(F32)
        gate_owned, up_owned, down_owned = (
            jnp.concatenate(
                [low_part[:, i * part : (i + 1) * part], high_part[:, i * part + spare : (i + 1) * part]],
                axis=1,
            )
            for i in range(3)
        )
        gain_two_sum = row_sum((gate_owned, w_gate), (up_owned, w_up))

    with jax.named_scope("gain_grads"):
        gain_grads = over_mp(jnp.concatenate([gain_one_sum, gain_two_sum], axis=1))

    return (
        result,
        input_grad,
        gain_grads[:, 0],
        gain_one * query_owned,
        gain_one * key_owned,
        gain_one * value_owned,
        heads_owned[:, at_out:].T,
        gain_grads[:, 1],
        gain_two * gate_owned,
        gain_two * up_owned,
        down_owned.T,
    )


def solution(mesh):
    split = Mesh(mesh.devices.reshape(4, 4, 2, 2, 2), AXES)
    token = P(None, DP, None)
    by_row = P(DP, MP)
    by_column = P(MP, DP)
    in_specs = (
        token, P(), P(), P(DP), by_row, by_row, by_row, by_column,
        P(DP), by_row, by_row, by_column, token,
    )
    out_specs = (
        token, token, P(DP), by_row, by_row, by_row, by_column,
        P(DP), by_row, by_row, by_column,
    )
    return jax.shard_map(
        on_device, mesh=split, in_specs=in_specs, out_specs=out_specs, check_vma=False
    )
```

```python
import math

import jax
import jax.numpy as jnp
from jax import lax
from jax.experimental import pallas as pl
from jax.experimental.pallas import tpu as pltpu
from jax.sharding import Mesh
from jax.sharding import PartitionSpec as P

HD = 128
BLOCK = 256
EPSILON = 1e-05
MASKED = -1e30
FLOOR = -1e29
LOG2E = 1.4426950408889634
TILE = 512
VMEM_LIMIT = 56 * 1024 * 1024

AXES = ("z", "y", "xh", "xl", "c")
DP = ("z", "y", "xh")
MP = ("xl", "c")
ZY = ("z", "y")
X4 = ("xh", "xl")
F32 = jnp.float32
BF16 = jnp.bfloat16


def after(value, *others):
    return lax.optimization_barrier((value, *others))[0]


def exchange(value, axes):
    return lax.all_to_all(value, axes, split_axis=0, concat_axis=0, tiled=True)


def from_everyone(value, axes):
    return exchange(jnp.broadcast_to(value, (lax.axis_size(axes), *value.shape)), axes)


def flip(value, axis):
    return lax.ppermute(value, axis, [(0, 1), (1, 0)])


def swap(value):
    return lax.ppermute(value, ("xh", "c"), [(1, 2), (2, 1)])


def turn(value, step):
    return lax.ppermute(value, X4, [(i, (i + step) % 4) for i in range(4)])


def ring_gather(block):
    far = turn(block, 2)
    return [block, turn(block, 1), far, turn(block, 3)]


def ring_parts(pieces):
    far = turn(pieces[2], -2)
    return [pieces[0], *(turn(pieces[s], -s) for s in (1, 3)), far]


def ring_sum(pieces):
    return sum(a.astype(F32) for a in ring_parts(pieces))


def behind(blocks, chip):
    return [lax.dynamic_index_in_dim(blocks, (chip - s) % 4, 0, keepdims=False) for s in range(4)]


def pick(first, when, own, other):
    return jnp.where(when == 0, own, other) if first else jnp.where(when == 0, other, own)


def ordered(when, own, other, axis):
    return jnp.concatenate([pick(True, when, own, other), pick(False, when, own, other)], axis=axis)


def rope_tables(place):
    half = HD // 2
    rates = jnp.exp(jnp.arange(half, dtype=F32) * (-2.0 * math.log(10000.0) / HD))
    angles = place.astype(F32)[:, None] * rates[None, :]
    return jnp.cos(angles)[:, None, :], jnp.sin(angles)[:, None, :]


def rotate(values, cosine, sine):
    half = HD // 2
    first, second = values[..., :half], values[..., half:]
    return jnp.concatenate(
        [first * cosine - second * sine, second * cosine + first * sine], axis=-1
    )


def layout(segments, skips, documents):
    count = segments.shape[0]
    labels = jnp.arange(documents, dtype=jnp.int32)
    member = segments[:, None] == labels[None, :]
    starts = jnp.sum((segments[:, None] < labels[None, :]).astype(jnp.int32), axis=0)
    ends = jnp.sum((segments[:, None] <= labels[None, :]).astype(jnp.int32), axis=0)
    start = jnp.sum(jnp.where(member, starts[None, :], 0), axis=1)
    end = jnp.sum(jnp.where(member, ends[None, :], 0), axis=1)
    place = jnp.arange(count, dtype=jnp.int32) - start
    keep = 1.0 - jnp.sum(jnp.where(member, skips[None, :], 0), axis=1).astype(F32)
    last = jnp.minimum(start + (place // BLOCK + 1) * BLOCK, end)
    return place, start, last, keep


def unit_scale(values):
    factor = lax.rsqrt(jnp.mean(values * values, axis=1, keepdims=True) + EPSILON)
    return values * factor, factor


def dot(a, b, dims):
    return lax.dot_general(a, b, (dims, ((), ())), preferred_element_type=F32)


def whole(shape):
    return pl.BlockSpec(shape, lambda *_: (0,) * len(shape))


def call(kernel, name, flops, moved, exps=0, **options):
    params = pltpu.CompilerParams(vmem_limit_bytes=VMEM_LIMIT)
    cost = pl.CostEstimate(flops=flops, bytes_accessed=moved, transcendentals=exps)
    return pl.pallas_call(
        kernel, name=name, compiler_params=params, cost_estimate=cost, **options
    )


def by_heads(block, heads):
    return jnp.concatenate([block[:, h * HD : (h + 1) * HD] for h in range(heads)], axis=0)


def store_heads(out_ref, turned, heads, queries):
    for h in range(heads):
        piece = turned[:, h * queries : (h + 1) * queries]
        out_ref[:, h * HD : (h + 1) * HD] = piece.T.astype(out_ref.dtype)


def reach(start, low_ref, high_ref, count):
    spot = start + lax.broadcasted_iota(jnp.int32, (TILE, count), 0)
    return (spot >= low_ref[...]) & (spot < high_ref[...])


def attend_kernel(heads, queries, scale, span, q_ref, kv_ref, low_ref, high_ref,
                  out_ref, turned_ref, log_ref, rows, top, total, running):
    count = heads * queries
    rows[...] = by_heads(q_ref[...], heads)
    top[...] = jnp.full_like(top, FLOOR)
    total[...] = jnp.zeros_like(total)
    running[...] = jnp.zeros_like(running)

    def step(i, _):
        start = pl.multiple_of(i * TILE, TILE)
        keys = kv_ref[pl.ds(start, TILE), :HD]
        values = kv_ref[pl.ds(start, TILE), HD:]
        scores = dot(keys, rows[...], ((1,), (1,))) * (scale * LOG2E)
        scores = jnp.where(reach(start, low_ref, high_ref, count), scores, MASKED)
        higher = jnp.maximum(top[...], jnp.max(scores, axis=0, keepdims=True))
        weights = jnp.exp2(scores - higher)
        fade = jnp.exp2(top[...] - higher)
        total[...] = total[...] * fade + jnp.sum(weights, axis=0, keepdims=True)
        running[...] = running[...] * fade + dot(values, weights.astype(BF16), ((0,), (0,)))
        top[...] = higher
        return 0

    lax.fori_loop(span[0], span[1], step, 0)
    mixed = running[...] / total[...]
    turned_ref[...] = mixed.astype(BF16)
    store_heads(out_ref, mixed, heads, queries)
    log_ref[...] = top[...] + jnp.log2(total[...])


def attend(span, query, key_value, low, high, heads, scale):
    queries = query.shape[0]
    count = heads * queries
    line = whole((1, count))
    return call(
        lambda *refs: attend_kernel(heads, queries, scale, *refs),
        "attend",
        4 * count * key_value.shape[0] * HD,
        2 * key_value.size + 6 * query.size,
        count * key_value.shape[0],
        out_shape=[
            jax.ShapeDtypeStruct(query.shape, BF16),
            jax.ShapeDtypeStruct((HD, count), BF16),
            jax.ShapeDtypeStruct((1, count), F32),
        ],
        grid_spec=pltpu.PrefetchScalarGridSpec(
            num_scalar_prefetch=1,
            grid=(1,),
            in_specs=[whole(query.shape), whole(key_value.shape), line, line],
            out_specs=[whole(query.shape), whole((HD, count)), line],
            scratch_shapes=[
                pltpu.VMEM((count, HD), BF16),
                pltpu.VMEM((1, count), F32),
                pltpu.VMEM((1, count), F32),
                pltpu.VMEM((HD, count), F32),
            ],
        ),
    )(span, query, key_value, low, high)


def attend_back_kernel(heads, queries, scale, span, q_ref, kv_ref, weight_ref, mixed_ref, log_ref,
                       low_ref, high_ref, p0_ref, p1_ref, p2_ref, p3_ref,
                       dq_ref, dkv_ref, branch_ref, rows, grads, delta, turned):
    count = heads * queries
    mine = queries // 4
    for s, piece in enumerate((p0_ref, p1_ref, p2_ref, p3_ref)):
        at = pl.multiple_of(lax.rem(span[2] + 4 - s, 4) * mine, mine)
        branch_ref[pl.ds(at, mine), :] = piece[...]
    mixed_grad = dot(branch_ref[...], weight_ref[...], ((1,), (0,))).astype(BF16).astype(F32)
    for h in range(heads):
        here = slice(h * queries, (h + 1) * queries)
        grads[:, here] = mixed_grad[:, h * HD : (h + 1) * HD].T.astype(BF16)
    delta[...] = jnp.sum(
        grads[...].astype(F32) * mixed_ref[...].astype(F32), axis=0, keepdims=True
    )
    rows[...] = by_heads(q_ref[...], heads)
    turned[...] = jnp.zeros_like(turned)
    dkv_ref[...] = jnp.zeros_like(dkv_ref)

    def step(i, _):
        start = pl.multiple_of(i * TILE, TILE)
        keys = kv_ref[pl.ds(start, TILE), :HD]
        values = kv_ref[pl.ds(start, TILE), HD:]
        scores = dot(keys, rows[...], ((1,), (1,))) * (scale * LOG2E) - log_ref[...]
        scores = jnp.where(reach(start, low_ref, high_ref, count), scores, MASKED)
        probs = jnp.exp2(scores)
        prob_grad = dot(values, grads[...], ((1,), (0,)))
        score_grad = (probs * (prob_grad - delta[...])).astype(BF16)
        key_grad = (dot(score_grad, rows[...], ((1,), (0,))) * scale).astype(BF16)
        value_grad = dot(probs.astype(BF16), grads[...], ((1,), (1,))).astype(BF16)
        for k in range(TILE // queries):
            here = slice(k * queries, (k + 1) * queries)
            dkv_ref[i * (TILE // queries) + k, :, :HD] = key_grad[here]
            dkv_ref[i * (TILE // queries) + k, :, HD:] = value_grad[here]
        turned[...] += dot(keys, score_grad, ((0,), (0,)))
        return 0

    lax.fori_loop(span[0], span[1], step, 0)
    store_heads(dq_ref, turned[...] * scale, heads, queries)


def attend_back(span, query, key_value, weight, mixed_turned, log_total, low, high, pieces,
                heads, scale):
    queries = query.shape[0]
    width = weight.shape[0]
    count = heads * queries
    line = whole((1, count))
    kv_shape = (key_value.shape[0] // queries, queries, 2 * HD)
    return call(
        lambda *refs: attend_back_kernel(heads, queries, scale, *refs),
        "attend_back",
        100 * count * key_value.shape[0] * HD,
        4 * key_value.size + 6 * query.size + 2 * weight.size,
        count * key_value.shape[0],
        out_shape=[
            jax.ShapeDtypeStruct(query.shape, F32),
            jax.ShapeDtypeStruct(kv_shape, BF16),
            jax.ShapeDtypeStruct((queries, width), BF16),
        ],
        grid_spec=pltpu.PrefetchScalarGridSpec(
            num_scalar_prefetch=1,
            grid=(1,),
            in_specs=[
                whole(query.shape), whole(key_value.shape), whole(weight.shape),
                whole((HD, count)), line, line, line, *[whole(p.shape) for p in pieces],
            ],
            out_specs=[whole(query.shape), whole(kv_shape), whole((queries, width))],
            scratch_shapes=[
                pltpu.VMEM((count, HD), BF16),
                pltpu.VMEM((HD, count), BF16),
                pltpu.VMEM((1, count), F32),
                pltpu.VMEM((HD, count), F32),
            ],
        ),
    )(span, query, key_value, weight, mixed_turned, log_total, low, high, *pieces)


def hidden_kernel(half, part, step, own_ref, other_ref, grad_own_ref, grad_other_ref, gate_ref,
                  up_ref, down_ref, rows_ref, hid_ref, dgate_ref, dup_ref, back_own_ref,
                  back_other_ref, unit, grad):
    at = pl.program_id(0)
    steps = part // step

    @pl.when(at == 0)
    def _():
        unit[:half] = own_ref[...]
        unit[half:] = other_ref[...]
        grad[:half] = grad_own_ref[...]
        grad[half:] = grad_other_ref[...]

    @pl.when(at < steps)
    def _():
        here = pl.ds(pl.multiple_of(jnp.minimum(at, steps - 1) * step, step), step)
        gate = dot(unit[...], gate_ref[...], ((1,), (0,)))
        up = dot(unit[...], up_ref[...], ((1,), (0,)))
        sigmoid = jax.nn.sigmoid(gate)
        activated = gate * sigmoid
        hid_ref[:, here] = (activated * up).astype(BF16)
        hidden_grad = dot(grad[...], down_ref[...], ((1,), (0,)))
        dgate_ref[:, here] = (
            hidden_grad * up * sigmoid * (1.0 + gate * (1.0 - sigmoid))
        ).astype(BF16)
        dup_ref[:, here] = (hidden_grad * activated).astype(BF16)

    @pl.when(at >= steps)
    def _():
        full = dot(dgate_ref[...], rows_ref[:, :part], ((1,), (1,)))
        full += dot(dup_ref[...], rows_ref[:, part:], ((1,), (1,)))
        back_own_ref[...] = full[:half].astype(BF16)
        back_other_ref[...] = full[half:].astype(BF16)


def hidden_units(units, grads, weight, part):
    half, width = units[0].shape
    count = 2 * half
    step, rows = 256, 512
    steps = part // step
    block = lambda which: pl.BlockSpec(
        (width, step), lambda j: (0, which * steps + jnp.minimum(j, steps - 1))
    )
    back = pl.BlockSpec((half, rows), lambda j: (0, jnp.maximum(j - steps, 0)))
    return call(
        lambda *refs: hidden_kernel(half, part, step, *refs),
        "hidden_units",
        10 * count * width * part,
        2 * weight.size + 4 * width * part + 4 * count * width,
        count * part,
        grid=(steps + width // rows,),
        in_specs=[whole((half, width))] * 4
        + [block(0), block(1), block(2)]
        + [pl.BlockSpec((rows, 2 * part), lambda j: (jnp.maximum(j - steps, 0), 0))],
        out_specs=[whole((count, part))] * 3 + [back, back],
        out_shape=[jax.ShapeDtypeStruct((count, part), BF16)] * 3
        + [
            jax.ShapeDtypeStruct((half, width), BF16),
            jax.ShapeDtypeStruct((half, width), BF16),
        ],
        scratch_shapes=[pltpu.VMEM((count, width), BF16)] * 2,
    )(*units, *grads, weight, weight, weight, weight)


def weight_grad_kernel(half, part, own_ref, other_ref, grad_own_ref, grad_other_ref, dgate_ref,
                       dup_ref, hid_ref, out_ref):
    unit = jnp.concatenate([own_ref[...], other_ref[...]], axis=0)
    grad = jnp.concatenate([grad_own_ref[...], grad_other_ref[...]], axis=0)
    out_ref[:, :part] = dot(unit, dgate_ref[...], ((0,), (0,))).astype(BF16)
    out_ref[:, part : 2 * part] = dot(unit, dup_ref[...], ((0,), (0,))).astype(BF16)
    out_ref[:, 2 * part :] = dot(grad, hid_ref[...], ((0,), (0,))).astype(BF16)


def weight_grad(units, grads, dgate, dup, hid):
    half, width = units[0].shape
    count, part = hid.shape
    step = 256
    column = pl.BlockSpec((half, step), lambda j: (0, j))
    return call(
        lambda *refs: weight_grad_kernel(half, part, *refs),
        "weight_grad",
        6 * count * width * part,
        6 * width * part + 8 * half * width,
        grid=(width // step,),
        in_specs=[column] * 4 + [whole(dgate.shape), whole(dup.shape), whole(hid.shape)],
        out_specs=pl.BlockSpec((step, 3 * part), lambda j: (j, 0)),
        out_shape=jax.ShapeDtypeStruct((width, 3 * part), BF16),
    )(*units, *grads, dgate, dup, hid)


def both_half_rows(block, core, here_ref, there_ref, columns):
    half = here_ref.shape[1]
    for p in range(here_ref.shape[0]):
        low, high = (block[(2 * p + k) * half : (2 * p + k + 1) * half] for k in (0, 1))
        here_ref[p, :, columns] = jnp.where(core == 0, low, high)
        there_ref[p, :, columns] = jnp.where(core == 0, high, low).astype(BF16)


def input_grad_kernel(spot, got_ref, pre_ref, query_ref, kv_ref, unit_ref, cos_ref, sin_ref,
                      p0_ref, p1_ref, p2_ref, p3_ref, here_ref, there_ref, kv_pre, part):
    mine = p0_ref.shape[0]

    @pl.when(pl.program_id(0) == 0)
    def _():
        total = jnp.sum(got_ref[...].astype(F32), axis=0)
        key = total[:, :HD]
        key = key * cos_ref[...] + pltpu.roll(key, HD // 2, 1) * sin_ref[...]
        kv_pre[:, :HD] = key.astype(BF16)
        kv_pre[:, HD:] = total[:, HD:].astype(BF16)

    part[...] = dot(pre_ref[...], query_ref[...], ((1,), (1,))) + dot(
        kv_pre[...], kv_ref[...], ((1,), (1,))
    )
    for s, piece in enumerate((p0_ref, p1_ref, p2_ref, p3_ref)):
        at = pl.multiple_of(lax.rem(spot[1] + 4 - s, 4) * mine, mine)
        piece[...] = part[pl.ds(at, mine), :].astype(BF16)
    block = dot(unit_ref[...], kv_pre[...], ((0,), (0,)))
    both_half_rows(block, spot[0], here_ref, there_ref, slice(0, 2 * HD))


def input_grad_parts(spot, got, query_pre, weight_query, weight_kv, unit, cosine, sine):
    planes, queries, pair = got.shape
    width, wide = weight_query.shape[0], query_pre.shape[1]
    rows, step, mine = width // (2 * planes), 512, queries // 4
    out = pl.BlockSpec((step // (2 * rows), rows, pair), lambda j, *_: (j, 0, 0))
    piece = pl.BlockSpec((mine, step), lambda j, *_: (0, j))
    return call(
        input_grad_kernel,
        "input_grad",
        60 * queries * width * (wide + 2 * pair),
        2 * (got.size + weight_query.size + weight_kv.size + 2 * unit.size),
        grid_spec=pltpu.PrefetchScalarGridSpec(
            num_scalar_prefetch=1,
            grid=(width // step,),
            in_specs=[
                whole(got.shape),
                whole(query_pre.shape),
                pl.BlockSpec((step, wide), lambda j, *_: (j, 0)),
                pl.BlockSpec((step, pair), lambda j, *_: (j, 0)),
                pl.BlockSpec((queries, step), lambda j, *_: (0, j)),
                whole(cosine.shape),
                whole(sine.shape),
            ],
            out_specs=[piece] * 4 + [out, out],
            scratch_shapes=[pltpu.VMEM((queries, pair), BF16), pltpu.VMEM((queries, step), F32)],
        ),
        out_shape=[jax.ShapeDtypeStruct((mine, width), BF16)] * 4
        + [
            jax.ShapeDtypeStruct((planes, rows, pair), F32),
            jax.ShapeDtypeStruct((planes, rows, pair), BF16),
        ],
    )(spot, got, query_pre, weight_query, weight_kv, unit, cosine, sine)


def spread(piece, xl, core):
    both = ordered(xl, piece, flip(piece, "xl"), 0)
    return ordered(core, both[None], flip(both, "c")[None], 0)


def over_mp(value):
    turned = [lax.ppermute(value, MP, [(i, (i + s) % 4) for i in range(4)]) for s in (1, 2, 3)]
    return sum(turned, value)


def on_device(
    tokens,
    segment_ids,
    skip_mask,
    norm1_gain,
    w_query,
    w_key,
    w_value,
    w_out,
    norm2_gain,
    w_gate,
    w_up,
    w_down,
    cotangent,
):
    local, width = tokens.shape[1:]
    documents = skip_mask.shape[1]
    xh, xl, core = lax.axis_index("xh"), lax.axis_index("xl"), lax.axis_index("c")
    chip = lax.axis_index(X4)
    plane = lax.axis_index(ZY)
    planes = lax.axis_size(ZY)
    queries = 2 * local
    mine = queries // 4
    every = planes * queries
    offset = plane * queries
    heads = w_query.shape[1] // HD
    wide = heads * HD
    scale = 1.0 / math.sqrt(HD)
    rows = w_query.shape[0]
    hidden_local = w_gate.shape[1]
    part = (hidden_local // 128 + 1) // 2 * 128
    lead = hidden_local - part
    spare = part - lead

    gain_one = norm1_gain.astype(F32)[:, None]
    gain_two = norm2_gain.astype(F32)[:, None]

    with jax.named_scope("attn_weights"):
        scaled = lambda w: (gain_one * w.astype(F32)).astype(BF16)
        own_heads = jnp.concatenate(
            [scaled(w_key), scaled(w_value), scaled(w_query), w_out.T], axis=1
        )
        half_heads = jnp.where(core == xh, own_heads, swap(own_heads))
        at_query, at_out = 2 * HD, 2 * HD + wide
        wide_weight = lax.all_gather(half_heads[:, at_query:], ("z", "y", "c"), axis=0, tiled=True)
        half_kv = from_everyone(half_heads[:, :at_query], ZY)
        pair_kv = ordered(core, half_kv[:, None], flip(half_kv, "c")[:, None], 1)
        weight_kv = pair_kv.reshape(width, at_query)

    with jax.named_scope("first_norm"):
        tokens_own = lax.dynamic_index_in_dim(tokens, core, 0, keepdims=False)
        tokens_all = ordered(xh, tokens_own, flip(tokens_own, "xh"), 0)
        unit_all = unit_scale(tokens_all.astype(F32))[0].astype(BF16)
        x_mine = lax.dynamic_slice_in_dim(tokens_own, xl * mine, mine).astype(F32)
        first_unit, first_factor = unit_scale(x_mine)

    with jax.named_scope("layout"):
        segment_own = lax.dynamic_index_in_dim(segment_ids, core, 0, keepdims=False)
        skip_own = lax.dynamic_index_in_dim(skip_mask, core, 0, keepdims=False)
        place, start, last, keep = layout(segment_own, skip_own, documents)
        here = lambda a: lax.dynamic_slice_in_dim(a, offset, queries)
        low, high = here(start), here(last)
        span = jnp.stack([low[0] // TILE, (high[-1] + TILE - 1) // TILE, chip])
        low, high = (jnp.tile(a, heads)[None] for a in (low, high))
        keep_here = here(keep).reshape(4, mine, 1)
        keep_mine = lax.dynamic_index_in_dim(keep_here, chip, 0, keepdims=False)
        cosine, sine = rope_tables(here(place))

    with jax.named_scope("project"):
        raw = dot(unit_all, weight_kv, ((1,), (0,)))
        key = rotate(raw[:, :HD].reshape(queries, 1, HD), cosine, sine)[:, 0]
        key_value = jnp.concatenate([key, raw[:, HD:]], axis=1).astype(BF16)
        everyone = from_everyone(key_value, ZY).reshape(every, 2 * HD)
        weight_query, weight_out = wide_weight[:, :wide], wide_weight[:, wide:]
        raw = dot(unit_all, weight_query, ((1,), (0,)))
        query = rotate(raw.reshape(queries, heads, HD), cosine, sine).astype(BF16)
        query = query.reshape(queries, wide)

    with jax.named_scope("ffn_weights"):
        own_hidden = [
            (gain_two * w_gate.astype(F32)).astype(BF16),
            (gain_two * w_up.astype(F32)).astype(BF16),
            w_down.T,
        ]

        def columns(which):
            blank = (which == 1) & (lax.broadcasted_iota(jnp.int32, (rows, part), 1) < spare)
            shares = []
            for w in own_hidden:
                share = jnp.where(which == 0, w[:, :part], w[:, lead:])
                shares.append(jnp.where(blank, jnp.zeros_like(share), share))
            return jnp.concatenate(shares, axis=1)

        pair_rows = ordered(xh, columns(xh), flip(after(columns(1 - xh), weight_kv), "xh"), 0)
        hidden_weight = lax.all_gather(after(pair_rows, key_value), ZY, axis=0, tiled=True)

    with jax.named_scope("cotangent"):
        grad_local = lax.dynamic_index_in_dim(cotangent, core, 0, keepdims=False)
        upstream = lax.dynamic_slice_in_dim(grad_local, xl * mine, mine).astype(F32)
        grad_all = ordered(xh, grad_local, flip(after(grad_local, key_value), "xh"), 0)
        grad_kept = (keep_here * grad_all.reshape(4, mine, width).astype(F32)).astype(BF16)
        grad_own = jnp.concatenate(behind(grad_kept, chip), axis=0)
        ffn_grads = (grad_own, flip(grad_own, "c"))

    with jax.named_scope("attend"):
        mixed, mixed_turned, log_total = attend(
            span, after(query, ffn_grads[1]), everyone, low, high, heads, scale
        )

    with jax.named_scope("branch"):
        partial = dot(mixed, weight_out, ((1,), (1,))).astype(BF16)
        branch = ring_sum(behind(partial.reshape(4, mine, width), chip))
        middle = x_mine + keep_mine * branch
        second_unit, second_factor = unit_scale(middle)
        unit_own = jnp.concatenate(ring_gather(second_unit.astype(BF16)), axis=0)
        units = (unit_own, flip(unit_own, "c"))

    def own_sum(own_part, other_part):
        both = (own_part + flip(other_part, "c").astype(F32)).astype(BF16)
        return both, ring_sum(list(both.reshape(4, mine, width)))

    with jax.named_scope("ffn"):
        hidden, gate_grad, up_grad, own_part, other_part = hidden_units(
            units, ffn_grads, hidden_weight, part
        )
        both, scaled_two = own_sum(own_part, other_part)
        hidden_weight_grad = weight_grad(
            units, ffn_grads, gate_grad, up_grad, after(hidden, both)
        )
        hidden_owned = lax.psum_scatter(hidden_weight_grad, ZY, scatter_dimension=0, tiled=True)
        middle_grad = upstream + second_factor * (
            scaled_two - second_unit * jnp.mean(scaled_two * second_unit, axis=1, keepdims=True)
        )
        pieces = ring_gather((keep_mine * middle_grad).astype(BF16))

    with jax.named_scope("attend_back"):
        query_grad, kv_grad, branch_grad = attend_back(
            span, query, everyone, weight_out, mixed_turned, log_total, low, high, pieces,
            heads, scale,
        )
        owned = exchange(kv_grad, ZY)
        query_pre = rotate(query_grad.reshape(queries, heads, HD), cosine, -sine)
        query_pre = query_pre.astype(BF16).reshape(queries, wide)
        cos_rows, sin_rows = cosine[:, 0], sine[:, 0]
        turn_back = [jnp.concatenate(t, axis=1) for t in ((cos_rows, cos_rows), (sin_rows, -sin_rows))]
        *input_parts, kv_here, kv_there = input_grad_parts(
            jnp.stack([core, chip]), owned, query_pre, wide_weight, weight_kv, unit_all, *turn_back
        )

    with jax.named_scope("ffn_grads"):
        owned_pair = hidden_owned.reshape(2, rows, 3 * part)
        kept = jnp.where(xh == 0, owned_pair[0], owned_pair[1])
        sent = flip(jnp.where(xh == 0, owned_pair[1], owned_pair[0]), "xh")

    def owned_half(grad):
        pair = grad.reshape(planes, 2, rows, grad.shape[-1])
        here_half = jnp.where(core == 0, pair[:, 0], pair[:, 1])
        there_half = jnp.where(core == 0, pair[:, 1], pair[:, 0])
        return (here_half + flip(there_half.astype(BF16), "c").astype(F32)).astype(BF16)

    def over_planes(half):
        return exchange(half, ZY).astype(F32).sum(axis=0)

    with jax.named_scope("head_grads"):
        query_half = owned_half(dot(unit_all, query_pre, ((0,), (0,))))
        out_half = owned_half(dot(branch_grad, mixed, ((0,), (0,))))
        wide_half = jnp.concatenate([query_half, out_half], axis=2)
        wide_got = exchange(after(wide_half, owned), ZY)
        wide_owned = wide_got.astype(F32).sum(axis=0)
        kv_half = (kv_here + flip(kv_there, "c").astype(F32)).astype(BF16)
        kv_got = exchange(after(kv_half, wide_got), ZY)
        kv_owned = kv_got.astype(F32).sum(axis=0)
        summed = jnp.concatenate([kv_owned, wide_owned], axis=1)
        heads_owned = jnp.where(core == xh, summed, swap(summed.astype(BF16)).astype(F32))
        query_owned = heads_owned[:, at_query:at_out]
        key_owned, value_owned = heads_owned[:, :HD], heads_owned[:, HD:at_query]
        row_sum = lambda *pairs: sum(
            jnp.sum(g * w.astype(F32), axis=1, keepdims=True) for g, w in pairs
        )
        gain_one_sum = row_sum((query_owned, w_query), (key_owned, w_key), (value_owned, w_value))

    with jax.named_scope("result"):
        down = hidden_weight[:, 2 * part :]
        partial = dot(after(hidden, kv_grad), down, ((1,), (1,)))
        feedforward = own_sum(partial[:queries], partial[queries:].astype(BF16))[1]
        result = spread((middle + keep_mine * feedforward).astype(BF16), xl, core)

    with jax.named_scope("input_grad"):
        late_parts = lax.optimization_barrier((*input_parts, wide_got))[:-1]
        late_parts = ring_parts(list(late_parts))
        late_parts = lax.optimization_barrier((*late_parts, kv_got))[:-1]
        scaled_one = sum(a.astype(F32) for a in late_parts)
        input_grad = middle_grad + first_factor * (
            scaled_one - first_unit * jnp.mean(scaled_one * first_unit, axis=1, keepdims=True)
        )
        input_grad = spread(input_grad.astype(BF16), xl, core)

    with jax.named_scope("ffn_grads"):
        low_part = pick(True, xh, kept, sent).astype(F32)
        high_part = pick(False, xh, kept, sent).astype(F32)
        gate_owned, up_owned, down_owned = (
            jnp.concatenate(
                [low_part[:, i * part : (i + 1) * part], high_part[:, i * part + spare : (i + 1) * part]],
                axis=1,
            )
            for i in range(3)
        )
        gain_two_sum = row_sum((gate_owned, w_gate), (up_owned, w_up))

    with jax.named_scope("gain_grads"):
        gain_grads = over_mp(jnp.concatenate([gain_one_sum, gain_two_sum], axis=1))

    return (
        result,
        input_grad,
        gain_grads[:, 0],
        gain_one * query_owned,
        gain_one * key_owned,
        gain_one * value_owned,
        heads_owned[:, at_out:].T,
        gain_grads[:, 1],
        gain_two * gate_owned,
        gain_two * up_owned,
        down_owned.T,
    )


def solution(mesh):
    split = Mesh(mesh.devices.reshape(4, 4, 2, 2, 2), AXES)
    token = P(None, DP, None)
    by_row = P(DP, MP)
    by_column = P(MP, DP)
    in_specs = (
        token, P(), P(), P(DP), by_row, by_row, by_row, by_column,
        P(DP), by_row, by_row, by_column, token,
    )
    out_specs = (
        token, token, P(DP), by_row, by_row, by_row, by_column,
        P(DP), by_row, by_row, by_column,
    )
    return jax.shard_map(
        on_device, mesh=split, in_specs=in_specs, out_specs=out_specs, check_vma=False
    )
```
